32 devices in a mesh: node: 2 (over core), expert: 16 (over z, y, x).
Axes of the slice: x: 2, y: 2, z: 4, core: 2. Of those that a mesh axis runs over, the one named last changes fastest.
Arguments:
- tokens: bfloat16 [16, 1024, 1024], P('expert', 'node'), may hold values from -6 to 6
- cotangent: bfloat16 [16, 1024, 1024], P('expert', 'node'), may hold values from -6 to 6
- routes: int32 [16, 1024, 1], P('expert'), may hold values from 0 to 15
- ln1_gain: float32 [1024], replicated, may hold values from 0.1 to 1.9
- w_qkv: bfloat16 [1024, 3072], replicated, may hold values from -0.1875 to 0.1875
- w_out: bfloat16 [1024, 1024], replicated, may hold values from -0.75 to 0.75
- ln2_gain: float32 [1024], replicated, may hold values from 0.1 to 1.9
- w_router: bfloat16 [1024, 16], replicated, may hold values from -0.25 to 0.25
- w_mix: bfloat16 [1024, 2], replicated, may hold values from -0.375 to 0.375
- w_up: bfloat16 [1024, 4096], P(None, 'node'), may hold values from -0.1875 to 0.1875
- w_down: bfloat16 [1024, 4096], P(None, 'node'), may hold values from -0.09375 to 0.09375
- expert_up: bfloat16 [16, 1024, 4096], P('expert', None, 'node'), may hold values from -0.1875 to 0.1875
- expert_down: bfloat16 [16, 4096, 1024], P('expert', 'node'), may hold values from -3 to 3
Outputs:
- mixed_out: bfloat16 [16, 1024, 1024], P('expert', 'node')
- input_grad: float32 [16, 1024, 1024], P('expert', 'node')
- grad_ln1: float32 [1024], P(('node', 'expert'))
- grad_w_qkv: float32 [1024, 3072], P(('node', 'expert'))
- grad_w_out: float32 [1024, 1024], P(('node', 'expert'))
- grad_ln2: float32 [1024], P(('node', 'expert'))
- grad_router: float32 [1024, 16], P(('node', 'expert'))
- grad_mix: float32 [1024, 2], P(('node', 'expert'))
- grad_w_up: float32 [1024, 4096], P('expert', 'node')
- grad_w_down: float32 [1024, 4096], P('expert', 'node')
- grad_expert_up: float32 [16, 1024, 4096], P('expert', None, 'node')
- grad_expert_down: float32 [16, 4096, 1024], P('expert', 'node')
The draws below stay inside these ranges and needn't reach their ends.
All inputs are finite; a program needn't handle non-finite values.
Results may differ from the reference program's by a relative error of at most 0.02.
Values may be sent and summed in bfloat16 or wider, within the bound.
A program may use at most 320 MiB of HBM per device.

```python
import jax
import jax.numpy as jnp
from jax import lax

D = 1024
HEADS = 16
HEAD_DIM = 64
FF = 4096
EFF = 4096
EXPERTS = 16
GROUPS = 16
GROUP_TOK = 1024
CAP = 96
N_NODE = 2


def shard_levels(own_key, dims, split, least, high):
    factor_of, own = 1.0, jax.random.fold_in(own_key, 6)
    for axis_at, shards_of in split:
        steps = jnp.exp(jax.random.uniform(jax.random.fold_in(own, axis_at), (shards_of,), jnp.float32, least / len(split), high / len(split)))
        factor_of = factor_of * jnp.repeat(steps, dims[axis_at] // shards_of).reshape([-1 if axis == axis_at else 1 for axis in range(len(dims))])
    return factor_of


def distinct(rng, rows, count, top, lift):
    ranking = jax.random.permutation(jax.random.fold_in(rng, 1), count)
    favour = ranking
    for power in range(3):
        favour = favour * favour // count
    favour = favour * lift // count
    tickets = jax.random.randint(jax.random.fold_in(rng, 2), (rows, count), 0, 4096) + favour
    fixed_rows = jax.random.permutation(jax.random.fold_in(rng, 3), rows)[jnp.arange(count) % rows]
    tickets = jnp.where(jnp.arange(rows)[:, None] == fixed_rows[None, :], 1 << 14, tickets)
    merit = tickets * count + jnp.arange(count)
    return lax.top_k(merit.astype(jnp.int32), top)[1].astype(jnp.int32)


def normal_values(rng, extent, width, bound, shards=(), held_as=jnp.bfloat16):
    result = width * jax.random.normal(rng, extent, jnp.float32)
    if shards:
        result = result * shard_levels(rng, extent, shards, -0.22, 0.18)
    return jnp.clip(result, -bound, bound).astype(held_as)


def setup_inputs(seed: int = 0) -> dict:
    key_of = jax.random.split(jax.random.key(seed), 14)
    return {
        "tokens": normal_values(key_of[0], (GROUPS, GROUP_TOK, D), 1.0, 6.0, ((0, 16), (1, 2))),
        "cotangent": normal_values(key_of[1], (GROUPS, GROUP_TOK, D), 1.0, 6.0, ((0, 16), (1, 2))),
        "routes": distinct(key_of[2], GROUPS * GROUP_TOK, EXPERTS, 1, 512).reshape((GROUPS, GROUP_TOK, 1)),
        "ln1_gain": jnp.clip(1.0 + 0.18 * jax.random.normal(key_of[3], (D,), jnp.float32), 0.1, 1.9),
        "w_qkv": normal_values(key_of[4], (D, 3 * D), D ** -0.5, 0.1875),
        "w_out": normal_values(key_of[5], (D, D), (D // 16) ** -0.5, 0.75),
        "ln2_gain": jnp.clip(1.0 + 0.18 * jax.random.normal(key_of[6], (D,), jnp.float32), 0.1, 1.9),
        "w_router": normal_values(key_of[7], (D, EXPERTS), (D // 2) ** -0.5, 0.25),
        "w_mix": normal_values(key_of[8], (D, 2), (D // 4) ** -0.5, 0.375),
        "w_up": normal_values(key_of[9], (D, FF), D ** -0.5, 0.1875, ((1, 2),)),
        "w_down": normal_values(key_of[10], (D, FF), FF ** -0.5, 0.09375, ((1, 2),)),
        "expert_up": normal_values(key_of[11], (EXPERTS, D, EFF), D ** -0.5, 0.1875, ((0, 16), (2, 2))),
        "expert_down": normal_values(key_of[12], (EXPERTS, EFF, D), (max(1, EFF // 1024)) ** -0.5, 3.0, ((0, 16), (1, 2))),
    }


@jax.custom_vjp
def low(v):
    return lax.optimization_barrier(v.astype(jnp.bfloat16)).astype(jnp.float32)

@jax.custom_vjp
def low_back(v):
    return v

def low_keep(v):
    return (low(v), None)

def low_pass(kept, grad):
    return (grad,)

def back_keep(v):
    return (v, None)

def back_low(kept, grad):
    return (low(grad),)
low.defvjp(low_keep, low_pass)
low_back.defvjp(back_keep, back_low)
EPS = 1e-05
HIGHEST_PRECISION = lax.Precision.HIGHEST

def matmul(left, right):
    return jnp.dot(left, right, precision=HIGHEST_PRECISION)

def normalize(values, gain):
    average = lax.optimization_barrier(jnp.mean(values, axis=-1, keepdims=True))
    centered = values - average
    return centered * lax.rsqrt(lax.optimization_barrier(jnp.mean(centered * centered, axis=-1, keepdims=True)) + EPS) * gain

def attend(packed):
    queries = packed[:, 0]
    key_rows = packed[:, 1]
    value_rows = packed[:, 2]
    scores = jnp.einsum('qhd,khd->hqk', queries, key_rows, precision=HIGHEST_PRECISION) * HEAD_DIM ** (-0.5)
    positions = jnp.arange(GROUP_TOK)
    allowed = positions[:, None] >= positions[None, :]
    scores = low_back(jnp.where(allowed[None], scores, -1000000000.0))
    probs = jax.nn.softmax(scores, axis=-1)
    attended = jnp.einsum('hqk,khd->qhd', low(probs), value_rows, precision=HIGHEST_PRECISION)
    return attended.reshape(GROUP_TOK, D)

def reference(tokens, cotangent, routes, ln1_gain, w_qkv, w_out, ln2_gain, w_router, w_mix, w_up, w_down, expert_up, expert_down):
    group_routes = routes.reshape(GROUPS, GROUP_TOK)
    route_onehot = (group_routes[:, :, None] == jnp.arange(EXPERTS)[None, None, :]).astype(jnp.int32)
    slot_order = lax.optimization_barrier(jnp.sum(jnp.cumsum(route_onehot, axis=1) * route_onehot, axis=2)) - 1
    within = slot_order < CAP
    slot_index = jnp.where(within, group_routes * CAP + slot_order, EXPERTS * CAP).astype(jnp.int32)
    group_index = jnp.broadcast_to(jnp.arange(GROUPS)[:, None], (GROUPS, GROUP_TOK)).astype(jnp.int32)
    route_table = route_onehot.reshape(-1, EXPERTS).astype(jnp.float32)
    half_width = EFF // N_NODE

    def forward(token_rows, gain_one, qkv_weight, out_weight, gain_two, router_weight, mix_weight, up_weight, down_weight, expert_in, expert_back):
        normed_one = low(normalize(token_rows, gain_one))
        packed = low_back(low(matmul(normed_one, qkv_weight)))
        packed = packed.reshape(GROUPS, GROUP_TOK, 3, HEADS, HEAD_DIM)
        attended = lax.map(jax.checkpoint(attend), packed)
        attended = low_back(low(attended.reshape(-1, D)))
        hidden = token_rows + low_back(matmul(attended, out_weight))
        normed_two = low(normalize(hidden, gain_two))
        dense_pre = low_back(matmul(normed_two, up_weight))
        dense_out = low_back(jnp.dot(low(jax.nn.gelu(dense_pre)), down_weight.T, precision=HIGHEST_PRECISION))
        grouped = normed_two.reshape(GROUPS, GROUP_TOK, D)
        filled = jnp.zeros((GROUPS, EXPERTS * CAP + 1, D), jnp.float32).at[group_index, slot_index].add(grouped)
        by_expert = filled[:, :-1].reshape(GROUPS, EXPERTS, CAP, D).transpose(1, 0, 2, 3).reshape(EXPERTS, GROUPS * CAP, D)
        summed = jnp.zeros_like(by_expert)
        for member in range(N_NODE):
            dispatched_copy = low_back(by_expert)
            expert_pre = low_back(jnp.einsum('erd,edf->erf', dispatched_copy, expert_in[:, :, member * half_width:(member + 1) * half_width], precision=HIGHEST_PRECISION))
            expert_act = low(jax.nn.gelu(expert_pre))
            summed = summed + low(jnp.einsum('erf,efd->erd', expert_act, expert_back[:, member * half_width:(member + 1) * half_width, :], precision=HIGHEST_PRECISION))
        returned = summed.reshape(EXPERTS, GROUPS, CAP, D).transpose(1, 0, 2, 3).reshape(GROUPS, EXPERTS * CAP, D)
        returned = jnp.concatenate([returned, jnp.zeros((GROUPS, 1, D), jnp.float32)], axis=1)
        expert_out = low_back(jnp.take_along_axis(returned, slot_index[:, :, None], axis=1).reshape(-1, D))
        router_probs = jax.nn.softmax(matmul(normed_two, router_weight), axis=-1)
        gate_value = lax.optimization_barrier(jnp.sum(router_probs * route_table, axis=-1, keepdims=True))
        mix_weights = jax.nn.softmax(matmul(normed_two, mix_weight), axis=-1)
        return hidden + mix_weights[:, 0:1] * dense_out + mix_weights[:, 1:2] * gate_value * expert_out
    primal, pullback = jax.vjp(forward, tokens.reshape(-1, D).astype(jnp.float32), ln1_gain, w_qkv.astype(jnp.float32), w_out.astype(jnp.float32), ln2_gain, w_router.astype(jnp.float32), w_mix.astype(jnp.float32), w_up.astype(jnp.float32), w_down.astype(jnp.float32), expert_up.astype(jnp.float32), expert_down.astype(jnp.float32))
    gradients = pullback(cotangent.reshape(-1, D).astype(jnp.float32))
    mixed_out = primal.astype(jnp.bfloat16).reshape(GROUPS, GROUP_TOK, D)
    input_grad = gradients[0].reshape(GROUPS, GROUP_TOK, D)
    return (mixed_out, input_grad, gradients[1], gradients[2], gradients[3], gradients[4], gradients[5], gradients[6], gradients[7], gradients[8], gradients[9], gradients[10])
```

```python
import functools

import jax
import jax.numpy as jnp
from jax import lax
from jax.experimental import pallas as pl
from jax.experimental.pallas import tpu as pltpu
from jax.sharding import PartitionSpec as P

HEAD_DIM = 64
EPS = 1e-05
LANES = 128
LOG2E = 1.4426950408889634
GELU_A = 0.7978845608028654
GELU_B = 0.044715
SWAP = [(0, 1), (1, 0)]
F32 = jnp.float32
BF16 = jnp.bfloat16


def dot(left, right):
    return jnp.dot(left, right, preferred_element_type=F32)


def dot_t(left, right):
    return lax.dot_general(left, right, (((1,), (1,)), ((), ())), preferred_element_type=F32)


def dot_n(left, right):
    return lax.dot_general(left, right, (((0,), (0,)), ((), ())), preferred_element_type=F32)


def layer_norm(values, gain):
    average = jnp.mean(values, axis=-1, keepdims=True)
    centered = values - average
    inverse = lax.rsqrt(jnp.mean(centered * centered, axis=-1, keepdims=True) + EPS)
    normed = centered * inverse
    return (normed * gain, normed, inverse)


def norm_backward(upstream, normed, inverse, gain):
    scaled = upstream * gain
    inner_term = (
        scaled
        - jnp.mean(scaled, axis=-1, keepdims=True)
        - normed * jnp.mean(scaled * normed, axis=-1, keepdims=True)
    )
    return inner_term * inverse


QB = 256


def attend_kernel(qkv_ref, out_ref, lse_ref, ot_ref):
    seq = qkv_ref.shape[0]
    factor = HEAD_DIM ** (-0.5) * LOG2E
    lane = lax.broadcasted_iota(jnp.int32, (1, LANES), 1)
    v_t = qkv_ref[:, 2 * LANES : 3 * LANES].T
    below = lax.broadcasted_iota(jnp.int32, (QB, QB), 0) <= lax.broadcasted_iota(
        jnp.int32, (QB, QB), 1
    )
    for head in range(2):
        keep = (lane // HEAD_DIM) == head
        keys = jnp.where(keep, qkv_ref[:, LANES : 2 * LANES], 0)
        v_rows = v_t[head * HEAD_DIM : (head + 1) * HEAD_DIM]
        for block in range(seq // QB):
            lo, hi = block * QB, (block + 1) * QB
            queries = qkv_ref[lo:hi, 0:LANES]
            diag = jnp.where(below, dot_t(keys[lo:hi], queries), -1e30)
            top = jnp.max(diag, axis=0, keepdims=True)
            if lo:
                past = dot_t(keys[:lo], queries)
                top = jnp.maximum(top, jnp.max(past, axis=0, keepdims=True))
            p_diag = jnp.exp2((diag - top) * factor)
            total = jnp.sum(p_diag, axis=0, keepdims=True)
            acc = dot(v_rows[:, lo:hi], p_diag.astype(BF16))
            if lo:
                p_past = jnp.exp2((past - top) * factor)
                total = total + jnp.sum(p_past, axis=0, keepdims=True)
                acc = acc + dot(v_rows[:, :lo], p_past.astype(BF16))
            ot_ref[head * HEAD_DIM : (head + 1) * HEAD_DIM, lo:hi] = acc * (1.0 / total)
            lse_ref[0, head : head + 1, lo:hi] = top * factor + jnp.log2(total)
    out_ref[...] = ot_ref[...].T.astype(BF16)


def attend(qkv, pairs):
    seq = qkv.shape[0]
    return pl.pallas_call(
        attend_kernel,
        grid=(pairs,),
        in_specs=[pl.BlockSpec((seq, 3 * LANES), lambda j: (0, j))],
        out_specs=[
            pl.BlockSpec((seq, LANES), lambda j: (0, j)),
            pl.BlockSpec((1, 8, seq), lambda j: (j, 0, 0)),
        ],
        out_shape=[
            jax.ShapeDtypeStruct((seq, pairs * LANES), BF16),
            jax.ShapeDtypeStruct((pairs, 8, seq), F32),
        ],
        scratch_shapes=[pltpu.VMEM((LANES, seq), F32)],
        cost_estimate=pl.CostEstimate(
            flops=pairs * 8 * seq * seq * LANES,
            bytes_accessed=pairs * seq * LANES * 8,
            transcendentals=pairs * seq * seq,
        ),
        compiler_params=pltpu.CompilerParams(vmem_limit_bytes=32 << 20),
        name="attend",
    )(qkv)


def attend_back_kernel(qkv_ref, out_ref, grad_ref, lse_ref, packed_ref, dqt_ref, dk_ref, dv_ref):
    seq = qkv_ref.shape[0]
    scale = HEAD_DIM ** (-0.5)
    factor = scale * LOG2E
    lane = lax.broadcasted_iota(jnp.int32, (1, LANES), 1)
    k_t = qkv_ref[:, LANES : 2 * LANES].T
    product = (grad_ref[...].astype(F32) * out_ref[...].astype(F32)).T
    below = lax.broadcasted_iota(jnp.int32, (QB, QB), 0) <= lax.broadcasted_iota(
        jnp.int32, (QB, QB), 1
    )
    dk_ref[...] = jnp.zeros_like(dk_ref)
    dv_ref[...] = jnp.zeros_like(dv_ref)
    for head in range(2):
        keep = (lane // HEAD_DIM) == head
        rows = slice(head * HEAD_DIM, (head + 1) * HEAD_DIM)
        keys = jnp.where(keep, qkv_ref[:, LANES : 2 * LANES], 0)
        values = jnp.where(keep, qkv_ref[:, 2 * LANES : 3 * LANES], 0)
        delta = jnp.sum(product[rows], axis=0, keepdims=True)
        for block in range(seq // QB):
            lo, hi = block * QB, (block + 1) * QB
            queries = jnp.where(keep, qkv_ref[lo:hi, 0:LANES], 0)
            grads = jnp.where(keep, grad_ref[lo:hi], 0)
            lse = lse_ref[0, head : head + 1, lo:hi]
            drop = delta[:, lo:hi]
            acc = None
            for start, stop in ((lo, hi), (0, lo)):
                if start == stop:
                    continue
                probs = jnp.exp2(dot_t(keys[start:stop], queries) * factor - lse)
                if start == lo:
                    probs = jnp.where(below, probs, 0.0)
                prob_grad = dot_t(values[start:stop], grads)
                score_grad = (probs * (prob_grad - drop)).astype(BF16)
                dv_ref[start:stop] += dot(probs.astype(BF16), grads)
                dk_ref[start:stop] += dot(score_grad, queries)
                part = dot(k_t[rows, start:stop], score_grad)
                acc = part if acc is None else acc + part
            dqt_ref[rows, lo:hi] = acc
    packed_ref[:, 0:LANES] = (dqt_ref[...].T * scale).astype(BF16)
    packed_ref[:, LANES : 2 * LANES] = (dk_ref[...] * scale).astype(BF16)
    packed_ref[:, 2 * LANES : 3 * LANES] = dv_ref[...].astype(BF16)


def attend_back(qkv, attended, grad, lse):
    seq = qkv.shape[0]
    pairs = lse.shape[0]
    return pl.pallas_call(
        attend_back_kernel,
        grid=(pairs,),
        in_specs=[
            pl.BlockSpec((seq, 3 * LANES), lambda j: (0, j)),
            pl.BlockSpec((seq, LANES), lambda j: (0, j)),
            pl.BlockSpec((seq, LANES), lambda j: (0, j)),
            pl.BlockSpec((1, 8, seq), lambda j: (j, 0, 0)),
        ],
        out_specs=pl.BlockSpec((seq, 3 * LANES), lambda j: (0, j)),
        out_shape=jax.ShapeDtypeStruct(qkv.shape, BF16),
        scratch_shapes=[
            pltpu.VMEM((LANES, seq), F32),
            pltpu.VMEM((seq, LANES), F32),
            pltpu.VMEM((seq, LANES), F32),
        ],
        cost_estimate=pl.CostEstimate(
            flops=pairs * 20 * seq * seq * LANES,
            bytes_accessed=pairs * seq * LANES * 16,
            transcendentals=pairs * seq * seq,
        ),
        compiler_params=pltpu.CompilerParams(vmem_limit_bytes=32 << 20),
        name="attend_back",
    )(qkv, attended, grad, lse)


def branch_kernel(dense, experts, x_ref, c_ref, sel_ref, wc_ref, wct_ref, up_ref, dn_ref, *refs):
    if dense:
        out_ref, dx_ref, gup_ref, gdn_ref, gsm_ref, probs_ref = refs[:6]
        xt_ref, g_ref, a_ref, acc_ref, dxa_ref, act_ref, dpre_ref, gt_ref = refs[6:]
    else:
        out_ref, dx_ref, gup_ref, gdn_ref, gsm_ref = refs[:5]
        xt_ref, g_ref, a_ref, acc_ref, dxa_ref, act_ref, dpre_ref = refs[5:]
    halves, rows, half = x_ref.shape
    width = halves * half
    step = pl.program_id(0)
    small = 256
    big = 512
    split = [slice(n * half, (n + 1) * half) for n in range(halves)]

    @pl.when(step == 0)
    def _():
        lane = lax.broadcasted_iota(jnp.int32, (1, LANES), 1)
        is_router = lane < experts
        is_mix = (lane >= experts) & (lane < experts + 2)
        picked = sel_ref[...]
        first = (lane == experts).astype(F32)
        second = (lane == experts + 1).astype(F32)

        def prepare(index, carry):
            at = pl.ds(pl.multiple_of(index * small, small), small)
            logits = sum(dot(x_ref[n, at, :], wc_ref[split[n], :]) for n in range(halves))

            def soft(mask):
                masked = jnp.where(mask, logits, -1e30)
                shifted = jnp.exp(masked - jnp.max(masked, axis=1, keepdims=True))
                return shifted / jnp.sum(shifted, axis=1, keepdims=True)

            mix = soft(is_mix)
            if dense:
                factor = jnp.sum(mix * first, axis=1, keepdims=True)
                probs_ref[at, :] = jnp.where(is_router, soft(is_router), mix)
                a_ref[at, :] = jnp.where(is_mix, first - mix, 0.0)
            else:
                router = soft(is_router)
                gate = jnp.sum(router * picked, axis=1, keepdims=True)
                factor = gate * jnp.sum(mix * second, axis=1, keepdims=True)
                a_ref[at, :] = jnp.where(
                    is_router, picked - router, jnp.where(is_mix, second - mix, 0.0)
                )
            for n in range(halves):
                xt_ref[split[n], at] = x_ref[n, at, :].T
                scaled = (factor * c_ref[n, at, :].astype(F32)).astype(BF16)
                g_ref[at, split[n]] = scaled
                if dense:
                    gt_ref[split[n], at] = scaled.T
            acc_ref[at, :] = jnp.zeros((small, width), F32)
            dxa_ref[at, :] = jnp.zeros((small, width), F32)
            return carry

        lax.fori_loop(0, rows // small, prepare, 0)

    def forward(index, carry):
        at = pl.ds(pl.multiple_of(index * big, big), big)
        pre = sum(dot(x_ref[n, at, :], up_ref[split[n], :]) for n in range(halves))
        square = pre * pre
        bend = jnp.tanh(pre * (GELU_A + GELU_A * GELU_B * square))
        side = 0.5 * (1.0 + bend)
        act = (pre * side).astype(BF16)
        slope = side + 0.5 * pre * (1.0 - bend * bend) * (GELU_A + 3.0 * GELU_A * GELU_B * square)
        act_ref[at, :] = act
        if dense:
            act_grad = dot(g_ref[at, :], dn_ref[...])
            acc_ref[at, :] += dot_t(act, dn_ref[...])
        else:
            act_grad = dot_t(g_ref[at, :], dn_ref[...])
            acc_ref[at, :] += dot(act, dn_ref[...])
        pre_grad = (slope * act_grad).astype(BF16)
        dpre_ref[at, :] = pre_grad
        dxa_ref[at, :] += dot_t(pre_grad, up_ref[...])
        return carry

    lax.fori_loop(0, rows // big, forward, 0)

    def weights(index, carry):
        at = pl.ds(pl.multiple_of(index * small, small), small)
        gup_ref[at, :] = dot(xt_ref[at, :], dpre_ref[...]).astype(gup_ref.dtype)
        if dense:
            gdn_ref[at, :] = dot(gt_ref[at, :], act_ref[...]).astype(gdn_ref.dtype)
        return carry

    lax.fori_loop(0, width // small, weights, 0)
    if not dense:
        gdn_ref[...] = dot_n(act_ref[...], g_ref[...]).astype(gdn_ref.dtype)

    @pl.when(step == pl.num_programs(0) - 1)
    def _():
        def finish(index, carry):
            at = pl.ds(pl.multiple_of(index * small, small), small)
            out = acc_ref[at, :]
            strength = jnp.sum(g_ref[at, :].astype(F32) * out, axis=1, keepdims=True)
            logit_grad = (strength * a_ref[at, :]).astype(BF16)
            act_ref[at, 0:LANES] = logit_grad
            grads = dxa_ref[at, :] + dot(logit_grad, wct_ref[...])
            if dense:
                mixes = probs_ref[at, :]
                lane = lax.broadcasted_iota(jnp.int32, (1, LANES), 1)
                first = jnp.sum(jnp.where(lane == experts, mixes, 0.0), axis=1, keepdims=True)
                out = out * first
            for n in range(out_ref.shape[0]):
                block = slice(n * out_ref.shape[2], (n + 1) * out_ref.shape[2])
                out_ref[n, at, :] = out[:, block].astype(BF16)
                dx_ref[n, at, :] = grads[:, block].astype(BF16)
            return carry

        lax.fori_loop(0, rows // small, finish, 0)
        gsm_ref[...] = dot(xt_ref[...], act_ref[:, 0:LANES])


def branch(x, c, picked, weights, weights_t, up, down, experts, dense):
    halves, rows, half = x.shape
    width = halves * half
    hidden = up.shape[1]
    block = 256
    up_spec = pl.BlockSpec((width, block), lambda f: (0, f))
    down_spec = up_spec if dense else pl.BlockSpec((block, width), lambda f: (f, 0))
    whole = lambda shape: pl.BlockSpec(
        shape, lambda f: (0,) * len(shape), pipeline_mode=pl.Buffered(1)
    )
    grad_type = BF16 if dense else F32
    result = (1, rows, width) if dense else (halves, rows, half)
    outs = [
        (whole(result), jax.ShapeDtypeStruct(result, BF16)),
        (whole(result), jax.ShapeDtypeStruct(result, BF16)),
        (up_spec, jax.ShapeDtypeStruct(up.shape, grad_type)),
        (down_spec, jax.ShapeDtypeStruct(down.shape, grad_type)),
        (whole((width, LANES)), jax.ShapeDtypeStruct((width, LANES), F32)),
    ]
    scratch = [
        pltpu.VMEM((width, rows), BF16),
        pltpu.VMEM((rows, width), BF16),
        pltpu.VMEM((rows, LANES), F32),
        pltpu.VMEM((rows, width), F32),
        pltpu.VMEM((rows, width), F32),
        pltpu.VMEM((rows, block), BF16),
        pltpu.VMEM((rows, block), BF16),
    ]
    if dense:
        outs.append((whole((rows, LANES)), jax.ShapeDtypeStruct((rows, LANES), F32)))
        scratch.append(pltpu.VMEM((width, rows), BF16))
    return pl.pallas_call(
        functools.partial(branch_kernel, dense, experts),
        grid=(hidden // block,),
        in_specs=[
            whole(x.shape),
            whole(c.shape),
            whole((1, LANES)),
            whole((width, LANES)),
            whole((LANES, width)),
            up_spec,
            down_spec,
        ],
        out_specs=[spec for spec, _ in outs],
        out_shape=[shape for _, shape in outs],
        scratch_shapes=scratch,
        cost_estimate=pl.CostEstimate(
            flops=12 * rows * width * hidden,
            bytes_accessed=12 * width * hidden + 8 * rows * width,
            transcendentals=rows * hidden,
        ),
        compiler_params=pltpu.CompilerParams(vmem_limit_bytes=58 << 20),
        name="dense_branch" if dense else "expert_branch",
    )(x, c, picked, weights, weights_t, up, down)


def shards(
    tokens,
    cotangent,
    routes,
    ln1_gain,
    w_qkv,
    w_out,
    ln2_gain,
    w_router,
    w_mix,
    w_up,
    w_down,
    expert_up,
    expert_down,
):
    node = lax.axis_index("node")
    member = lax.axis_index("expert")
    members = lax.axis_size("expert")
    width = tokens.shape[2]
    half = width // 2
    own_rows = tokens.shape[1]
    seq = 2 * own_rows
    experts = w_router.shape[1]
    capacity = 3 * seq // (2 * experts)
    slots = experts * capacity
    pairs = half // LANES
    own_start = node * own_rows

    seq_tokens = lax.all_gather(tokens[0], "node", axis=0, tiled=True)
    seq_cot = lax.all_gather(cotangent[0], "node", axis=0, tiled=True)

    group_routes = routes.reshape(-1)
    route_onehot = group_routes[:, None] == jnp.arange(experts)[None, :]
    ones = route_onehot.astype(BF16)
    row_at = jnp.arange(seq)
    earlier = (row_at[:, None] > row_at[None, :]).astype(BF16)
    order = jnp.sum(
        jnp.where(route_onehot, dot(earlier, ones), 0.0), axis=1
    ).astype(jnp.int32)
    place = jnp.where(order < capacity, group_routes * capacity + order, slots)
    slot_onehot = (place[:, None] == jnp.arange(slots)[None, :]).astype(BF16)

    def dispatch(rows):
        part = lax.dynamic_slice_in_dim(rows, node * half, half, 1)
        sent = dot_n(slot_onehot, part).astype(BF16).reshape(experts, capacity, half)
        got = lax.all_to_all(sent, "expert", split_axis=0, concat_axis=0, tiled=True)
        return lax.all_gather(got.reshape(slots, half), "node", axis=0)

    def give_back(parts):
        other = lax.ppermute(
            lax.dynamic_index_in_dim(parts, 1 - node, 0, False), "node", SWAP
        )
        mine = lax.dynamic_index_in_dim(parts, node, 0, False)
        total = (mine.astype(F32) + other.astype(F32)).astype(BF16)
        got = lax.all_to_all(
            total.reshape(experts, capacity, half), "expert", split_axis=0, concat_axis=0, tiled=True
        )
        return dot(slot_onehot, got.reshape(slots, half))

    expert_cot = dispatch(seq_cot)

    w_own = lax.dynamic_slice_in_dim(w_qkv.reshape(width, 3, width), node * half, half, 2)
    w_own = w_own.reshape(width, 3, pairs, LANES).transpose(0, 2, 1, 3).reshape(width, 3 * half)
    rows_f32 = seq_tokens.astype(F32)
    normed_one, _, _ = layer_norm(rows_f32, ln1_gain)
    normed_low = normed_one.astype(BF16)
    qkv = dot(normed_low, w_own).astype(BF16)
    attended_own, lse = attend(qkv, pairs)
    attended = lax.all_gather(attended_own, "node", axis=0)
    hidden = rows_f32 + dot(attended[0], w_out[:half]) + dot(attended[1], w_out[half:])
    normed_two, base_two, inverse_two = layer_norm(hidden, ln2_gain)
    inner_low = normed_two.astype(BF16)

    expert_rows = dispatch(inner_low)
    head = jnp.concatenate(
        [w_router, w_mix, jnp.zeros((width, LANES - experts - 2), BF16)], axis=1
    )
    head_t = head.T
    picked = (jnp.arange(LANES) == member).astype(F32)[None]
    dense_out, dense_dx, grad_up, grad_down, small_dense, probs = branch(
        inner_low[None], seq_cot[None], picked, head, head_t, w_up, w_down, experts, True
    )
    expert_out, expert_dx, grad_expert_up, grad_expert_down, small_expert = branch(
        expert_rows, expert_cot, picked, head, head_t, expert_up[0], expert_down[0], experts, False
    )
    grad_w_up = lax.psum_scatter(grad_up, "expert", scatter_dimension=0, tiled=True)
    grad_w_down = lax.psum_scatter(grad_down, "expert", scatter_dimension=0, tiled=True)

    dense_other = lax.ppermute(dense_dx[0], "node", SWAP)
    token_dx = give_back(expert_dx).astype(BF16)
    token_other = lax.ppermute(token_dx, "node", SWAP)

    def by_node(mine, other):
        return jnp.where(
            node == 0,
            jnp.concatenate([mine, other], axis=1),
            jnp.concatenate([other, mine], axis=1),
        )

    inner_grad = (
        dense_dx[0].astype(F32)
        + dense_other.astype(F32)
        + by_node(token_dx, token_other).astype(F32)
    )
    hidden_grad = seq_cot.astype(F32) + norm_backward(inner_grad, base_two, inverse_two, ln2_gain)
    grad_ln2 = 0.5 * jnp.sum(inner_grad * base_two, axis=0)
    attn_grad = hidden_grad.astype(BF16)
    w_out_own = lax.dynamic_slice_in_dim(w_out, node * half, half, 0)
    grad_w_out = dot_n(attended_own, attn_grad).astype(BF16)
    grad_w_out = lax.psum_scatter(grad_w_out, "expert", scatter_dimension=0, tiled=True)
    attended_grad = dot_t(attn_grad, w_out_own).astype(BF16)
    packed_grad = attend_back(qkv, attended_own, attended_grad, lse)

    token_out = give_back(expert_out)
    gate = jnp.sum(jnp.where(route_onehot, probs[:, :experts], 0.0), axis=1, keepdims=True)
    weight = gate * probs[:, experts + 1 : experts + 2]
    scaled = weight * token_out
    total_out = dense_out[0].astype(F32) + by_node(scaled, jnp.zeros_like(scaled))
    total_out = total_out.astype(BF16)

    def own_sum(partial):
        mine = lax.dynamic_slice_in_dim(partial, own_start, own_rows, 0)
        other = lax.dynamic_slice_in_dim(partial, own_rows - own_start, own_rows, 0)
        return mine.astype(F32) + lax.ppermute(other, "node", SWAP).astype(F32)

    hidden_own = lax.dynamic_slice_in_dim(hidden, own_start, own_rows, 0)
    mixed_out = (hidden_own + own_sum(total_out)).astype(BF16).reshape(tokens.shape)

    grad_qkv = dot_n(normed_low, packed_grad)
    normed_grad = own_sum(dot_t(packed_grad, w_own).astype(BF16))
    _, base_one, inverse_one = layer_norm(tokens[0].astype(F32), ln1_gain)
    input_grad = lax.dynamic_slice_in_dim(hidden_grad, own_start, own_rows, 0) + norm_backward(
        normed_grad, base_one, inverse_one, ln1_gain
    )
    grad_ln1 = jnp.sum(normed_grad * base_one, axis=0)
    small = small_dense + small_expert
    small = jnp.concatenate(
        [
            small[:, : experts + 2],
            grad_ln1[:, None],
            grad_ln2[:, None],
            jnp.zeros((width, LANES - experts - 4), F32),
        ],
        axis=1,
    )
    last = jnp.concatenate([grad_qkv.astype(BF16), small.astype(BF16)], axis=1)
    shard = width // (2 * members)
    last = last.reshape(2, members, shard, -1).transpose(1, 0, 2, 3).reshape(width, -1)
    last = lax.psum_scatter(last, "expert", scatter_dimension=0, tiled=True)
    last = last.reshape(2, shard, -1)
    kept = lax.dynamic_index_in_dim(last, node, 0, False)
    other = lax.ppermute(lax.dynamic_index_in_dim(last, 1 - node, 0, False), "node", SWAP)

    def columns(rows):
        return rows[:, : 3 * half].reshape(shard, pairs, 3, LANES).transpose(0, 2, 1, 3)

    grad_w_qkv = jnp.where(
        node == 0,
        jnp.concatenate([columns(kept), columns(other)], axis=2),
        jnp.concatenate([columns(other), columns(kept)], axis=2),
    )
    grad_w_qkv = grad_w_qkv.reshape(shard, 3 * width).astype(F32)
    small = kept[:, 3 * half :].astype(F32) + other[:, 3 * half :].astype(F32)
    return (
        mixed_out,
        input_grad.reshape(tokens.shape),
        small[:, experts + 2],
        grad_w_qkv,
        grad_w_out.astype(F32),
        small[:, experts + 3],
        small[:, :experts],
        small[:, experts : experts + 2],
        grad_w_up.astype(F32),
        grad_w_down.astype(F32),
        grad_expert_up[None],
        grad_expert_down[None],
    )


def solution(mesh):
    return jax.shard_map(
        shards,
        mesh=mesh,
        in_specs=(
            P("expert", "node", None),
            P("expert", "node", None),
            P("expert", None, None),
            P(),
            P(),
            P(),
            P(),
            P(),
            P(),
            P(None, "node"),
            P(None, "node"),
            P("expert", None, "node"),
            P("expert", "node", None),
        ),
        out_specs=(
            P("expert", "node", None),
            P("expert", "node", None),
            P(("node", "expert")),
            P(("node", "expert"), None),
            P(("node", "expert"), None),
            P(("node", "expert")),
            P(("node", "expert"), None),
            P(("node", "expert"), None),
            P("expert", "node"),
            P("expert", "node"),
            P("expert", None, "node"),
            P("expert", "node", None),
        ),
        check_vma=False,
    )
```

```python
import functools

import jax
import jax.numpy as jnp
from jax import lax
from jax.experimental import pallas as pl
from jax.experimental.pallas import tpu as pltpu
from jax.sharding import PartitionSpec as P

HEAD_DIM = 64
EPS = 1e-05
LANES = 128
LOG2E = 1.4426950408889634
GELU_A = 0.7978845608028654
GELU_B = 0.044715
SWAP = [(0, 1), (1, 0)]
F32 = jnp.float32
BF16 = jnp.bfloat16


def dot(left, right):
    return jnp.dot(left, right, preferred_element_type=F32)


def dot_t(left, right):
    return lax.dot_general(left, right, (((1,), (1,)), ((), ())), preferred_element_type=F32)


def dot_n(left, right):
    return lax.dot_general(left, right, (((0,), (0,)), ((), ())), preferred_element_type=F32)


def layer_norm(values, gain):
    average = jnp.mean(values, axis=-1, keepdims=True)
    centered = values - average
    inverse = lax.rsqrt(jnp.mean(centered * centered, axis=-1, keepdims=True) + EPS)
    normed = centered * inverse
    return (normed * gain, normed, inverse)


def norm_backward(upstream, normed, inverse, gain):
    scaled = upstream * gain
    inner_term = (
        scaled
        - jnp.mean(scaled, axis=-1, keepdims=True)
        - normed * jnp.mean(scaled * normed, axis=-1, keepdims=True)
    )
    return inner_term * inverse


def spec(shape, index):
    return pl.BlockSpec(shape, index)


def fixed(shape):
    return pl.BlockSpec(shape, lambda *_: (0,) * len(shape), pipeline_mode=pl.Buffered(1))


def struct(shape, kind):
    return jax.ShapeDtypeStruct(shape, kind)


def chunks(count, size, step):
    def run(index, carry):
        step(pl.ds(pl.multiple_of(index * size, size), size))
        return carry

    lax.fori_loop(0, count // size, run, 0)


def permutation(source, columns):
    lane = lax.broadcasted_iota(jnp.int32, (source.shape[0], columns), 1)
    return (source == lane).astype(F32).astype(BF16)


WIDE = 256


def front_kernel(node_ref, own_ref, other_ref, gain_ref, w_ref, qkv_ref, normed_ref):
    rows = own_ref.shape[0]
    node = node_ref[0]

    @pl.when(pl.program_id(0) == 0)
    def _():
        for place, part in ((node, own_ref), (1 - node, other_ref)):
            def norm(at):
                normed, _, _ = layer_norm(part[at, :].astype(F32), gain_ref[...])
                start = pl.multiple_of(place * rows + at.start, 128)
                normed_ref[pl.ds(start, 128), :] = normed.astype(BF16)

            chunks(rows, 128, norm)

    def project(at):
        qkv_ref[at, :] = dot(normed_ref[at, :], w_ref[...]).astype(BF16)

    chunks(2 * rows, 512, project)


def front(node, own, other, gain, w_qkv):
    rows, width = own.shape
    blocks = width // WIDE
    half = blocks // 2
    return pl.pallas_call(
        front_kernel,
        grid_spec=pltpu.PrefetchScalarGridSpec(
            num_scalar_prefetch=1,
            grid=(3 * half,),
            in_specs=[
                fixed(own.shape),
                fixed(own.shape),
                fixed((1, width)),
                spec((width, WIDE), lambda i, n: (0, (i % 3) * blocks + n[0] * half + i // 3)),
            ],
            out_specs=[
                spec((2 * rows, WIDE), lambda i, n: (0, i)),
                fixed((2 * rows, width)),
            ],
        ),
        out_shape=[struct((2 * rows, 3 * width // 2), BF16), struct((2 * rows, width), BF16)],
        cost_estimate=pl.CostEstimate(
            flops=6 * rows * width * width, bytes_accessed=14 * rows * width, transcendentals=0
        ),
        compiler_params=pltpu.CompilerParams(vmem_limit_bytes=32 << 20),
        name="front",
    )(node, own, other, gain[None], w_qkv)


QB = 256


def head_specs(seq):
    return [spec((seq, LANES), lambda j, at=at: (0, (j // 2) * 6 + at + j % 2)) for at in (0, 2, 4)]


def attend_kernel(q_ref, k_ref, v_ref, out_ref, lse_ref, ot_ref):
    seq = q_ref.shape[0]
    factor = HEAD_DIM ** (-0.5) * LOG2E
    lane = lax.broadcasted_iota(jnp.int32, (1, LANES), 1)
    v_t = v_ref[...].T
    below = lax.broadcasted_iota(jnp.int32, (QB, QB), 0) <= lax.broadcasted_iota(
        jnp.int32, (QB, QB), 1
    )
    for head in range(2):
        keep = (lane // HEAD_DIM) == head
        keys = jnp.where(keep, k_ref[...], 0)
        v_rows = v_t[head * HEAD_DIM : (head + 1) * HEAD_DIM]
        for block in range(seq // QB):
            lo, hi = block * QB, (block + 1) * QB
            queries = q_ref[lo:hi]
            diag = jnp.where(below, dot_t(keys[lo:hi], queries), -1e30)
            top = jnp.max(diag, axis=0, keepdims=True)
            if lo:
                past = dot_t(keys[:lo], queries)
                top = jnp.maximum(top, jnp.max(past, axis=0, keepdims=True))
            p_diag = jnp.exp2((diag - top) * factor)
            total = jnp.sum(p_diag, axis=0, keepdims=True)
            acc = dot(v_rows[:, lo:hi], p_diag.astype(BF16))
            if lo:
                p_past = jnp.exp2((past - top) * factor)
                total = total + jnp.sum(p_past, axis=0, keepdims=True)
                acc = acc + dot(v_rows[:, :lo], p_past.astype(BF16))
            ot_ref[head * HEAD_DIM : (head + 1) * HEAD_DIM, lo:hi] = acc * (1.0 / total)
            lse_ref[0, head : head + 1, lo:hi] = top * factor + jnp.log2(total)
    out_ref[...] = ot_ref[...].T.astype(BF16)


def attend(qkv, pairs):
    seq = qkv.shape[0]
    return pl.pallas_call(
        attend_kernel,
        grid=(pairs,),
        in_specs=head_specs(seq),
        out_specs=[
            spec((seq, LANES), lambda j: (0, j)),
            spec((1, 8, seq), lambda j: (j, 0, 0)),
        ],
        out_shape=[struct((seq, pairs * LANES), BF16), struct((pairs, 8, seq), F32)],
        scratch_shapes=[pltpu.VMEM((LANES, seq), F32)],
        cost_estimate=pl.CostEstimate(
            flops=pairs * 8 * seq * seq * LANES,
            bytes_accessed=pairs * seq * LANES * 8,
            transcendentals=pairs * seq * seq,
        ),
        compiler_params=pltpu.CompilerParams(vmem_limit_bytes=32 << 20),
        name="attend",
    )(qkv, qkv, qkv)


def attend_back_kernel(
    q_ref, k_ref, v_ref, out_ref, grad_ref, lse_ref, dq_ref, dk_ref, dv_ref, dqt_ref, dka_ref, dva_ref
):
    seq = q_ref.shape[0]
    scale = HEAD_DIM ** (-0.5)
    factor = scale * LOG2E
    lane = lax.broadcasted_iota(jnp.int32, (1, LANES), 1)
    k_t = k_ref[...].T
    product = (grad_ref[...].astype(F32) * out_ref[...].astype(F32)).T
    below = lax.broadcasted_iota(jnp.int32, (QB, QB), 0) <= lax.broadcasted_iota(
        jnp.int32, (QB, QB), 1
    )
    dka_ref[...] = jnp.zeros_like(dka_ref)
    dva_ref[...] = jnp.zeros_like(dva_ref)
    for head in range(2):
        keep = (lane // HEAD_DIM) == head
        rows = slice(head * HEAD_DIM, (head + 1) * HEAD_DIM)
        keys = jnp.where(keep, k_ref[...], 0)
        values = jnp.where(keep, v_ref[...], 0)
        delta = jnp.sum(product[rows], axis=0, keepdims=True)
        for block in range(seq // QB):
            lo, hi = block * QB, (block + 1) * QB
            queries = jnp.where(keep, q_ref[lo:hi], 0)
            grads = jnp.where(keep, grad_ref[lo:hi], 0)
            lse = lse_ref[0, head : head + 1, lo:hi]
            drop = delta[:, lo:hi]
            acc = None
            for start, stop in ((lo, hi), (0, lo)):
                if start == stop:
                    continue
                probs = jnp.exp2(dot_t(keys[start:stop], queries) * factor - lse)
                if start == lo:
                    probs = jnp.where(below, probs, 0.0)
                prob_grad = dot_t(values[start:stop], grads)
                score_grad = (probs * (prob_grad - drop)).astype(BF16)
                dva_ref[start:stop] += dot(probs.astype(BF16), grads)
                dka_ref[start:stop] += dot(score_grad, queries)
                part = dot(k_t[rows, start:stop], score_grad)
                acc = part if acc is None else acc + part
            dqt_ref[rows, lo:hi] = acc
    dq_ref[...] = (dqt_ref[...].T * scale).astype(BF16)
    dk_ref[...] = (dka_ref[...] * scale).astype(BF16)
    dv_ref[...] = dva_ref[...].astype(BF16)


def attend_back(qkv, attended, grad, lse):
    seq = qkv.shape[0]
    pairs = lse.shape[0]
    one = spec((seq, LANES), lambda j: (0, j))
    return pl.pallas_call(
        attend_back_kernel,
        grid=(pairs,),
        in_specs=head_specs(seq) + [one, one, spec((1, 8, seq), lambda j: (j, 0, 0))],
        out_specs=[one] * 3,
        out_shape=[struct(attended.shape, BF16)] * 3,
        scratch_shapes=[
            pltpu.VMEM((LANES, seq), F32),
            pltpu.VMEM((seq, LANES), F32),
            pltpu.VMEM((seq, LANES), F32),
        ],
        cost_estimate=pl.CostEstimate(
            flops=pairs * 20 * seq * seq * LANES,
            bytes_accessed=pairs * seq * LANES * 16,
            transcendentals=pairs * seq * seq,
        ),
        compiler_params=pltpu.CompilerParams(vmem_limit_bytes=32 << 20),
        name="attend_back",
    )(qkv, qkv, qkv, attended, grad, lse)


def middle_kernel(node_ref, tok_ref, own_ref, other_ref, w_ref, gain_ref, hidden_ref, normed_ref):
    half = own_ref.shape[1]
    node = node_ref[0]
    mine = pl.ds(pl.multiple_of(node * half, half), half)
    theirs = pl.ds(pl.multiple_of((1 - node) * half, half), half)
    hidden = tok_ref[...].astype(F32) + (
        dot(own_ref[...], w_ref[mine, :]) + dot(other_ref[...], w_ref[theirs, :])
    )
    normed, _, _ = layer_norm(hidden, gain_ref[...])
    hidden_ref[...] = hidden
    normed_ref[...] = normed.astype(BF16)


def middle(node, tokens, own, other, w_out, gain):
    seq, width = tokens.shape
    rows = 256
    row = lambda columns: spec((rows, columns), lambda i, n: (i, 0))
    return pl.pallas_call(
        middle_kernel,
        grid_spec=pltpu.PrefetchScalarGridSpec(
            num_scalar_prefetch=1,
            grid=(seq // rows,),
            in_specs=[
                row(width),
                row(width // 2),
                row(width // 2),
                fixed(w_out.shape),
                fixed((1, width)),
            ],
            out_specs=[row(width), row(width)],
        ),
        out_shape=[struct((seq, width), F32), struct((seq, width), BF16)],
        cost_estimate=pl.CostEstimate(
            flops=2 * seq * width * width, bytes_accessed=12 * seq * width, transcendentals=0
        ),
        compiler_params=pltpu.CompilerParams(vmem_limit_bytes=24 << 20),
        name="middle",
    )(node, tokens, own, other, w_out, gain[None])


def middle_back_kernel(
    parts,
    node_ref,
    source_ref,
    dense_ref,
    dense_other_ref,
    token_ref,
    token_other_ref,
    hidden_ref,
    cot_ref,
    attended_ref,
    gain_ref,
    w_ref,
    grad_ref,
    attended_grad_ref,
    ln_ref,
    *refs,
):
    weight_refs = refs[:parts]
    inner_ref, acc_ref = refs[parts:]
    half = token_ref.shape[1]
    node = node_ref[0]
    step = pl.program_id(0)

    @pl.when(step == 0)
    def _():
        ln_ref[...] = jnp.zeros_like(ln_ref)
        acc_ref[...] = jnp.zeros_like(acc_ref)

    inner_ref[...] = dense_ref[...].astype(F32) + dense_other_ref[...].astype(F32)
    inner_ref[:, pl.ds(pl.multiple_of(node * half, half), half)] += token_ref[...].astype(F32)
    inner_ref[:, pl.ds(pl.multiple_of((1 - node) * half, half), half)] += token_other_ref[
        ...
    ].astype(F32)
    inner = inner_ref[...]
    gain = gain_ref[...]
    _, base, inverse = layer_norm(hidden_ref[...], gain)
    ln_ref[0:1, :] += 0.5 * jnp.sum(inner * base, axis=0, keepdims=True)
    hidden_grad = cot_ref[...].astype(F32) + norm_backward(inner, base, inverse, gain)
    grad_ref[...] = hidden_grad
    low = hidden_grad.astype(BF16)
    attended_grad_ref[...] = dot_t(low, w_ref[...]).astype(BF16)
    turned = dot_t(permutation(source_ref[...], half), attended_ref[...]).astype(BF16)
    acc_ref[...] += dot(turned, low)

    @pl.when(step == pl.num_programs(0) - 1)
    def _():
        size = half // parts
        for part in range(parts):
            weight_refs[part][...] = acc_ref[part * size : (part + 1) * size].astype(BF16)


def middle_back(node, source, dense, dense_other, token, token_other, hidden, cot, attended, gain, w_out, parts):
    seq, width = hidden.shape
    half = width // 2
    rows = 256
    row = lambda columns: spec((rows, columns), lambda i, n: (i, 0))
    result = (half // parts, width)
    return pl.pallas_call(
        functools.partial(middle_back_kernel, parts),
        grid_spec=pltpu.PrefetchScalarGridSpec(
            num_scalar_prefetch=1,
            grid=(seq // rows,),
            in_specs=[
                fixed(source.shape),
                row(width),
                row(width),
                row(half),
                row(half),
                row(width),
                row(width),
                row(half),
                fixed((1, width)),
                spec((half, width), lambda i, n: (n[0], 0)),
            ],
            out_specs=[row(width), row(half), fixed((8, width))] + [fixed(result)] * parts,
            scratch_shapes=[pltpu.VMEM((rows, width), F32), pltpu.VMEM((half, width), F32)],
        ),
        out_shape=[
            struct((seq, width), F32),
            struct((seq, half), BF16),
            struct((8, width), F32),
        ]
        + [struct(result, BF16)] * parts,
        cost_estimate=pl.CostEstimate(
            flops=2 * seq * width * width, bytes_accessed=18 * seq * width, transcendentals=0
        ),
        compiler_params=pltpu.CompilerParams(vmem_limit_bytes=32 << 20),
        name="middle_back",
    )(node, source, dense, dense_other, token, token_other, hidden, cot, attended, gain[None], w_out)


def branch_kernel(dense, experts, parts, node_ref, *refs):
    if dense:
        x_refs, c_refs, refs = refs[:1], refs[1:2], refs[2:]
    else:
        x_refs, c_refs, refs = refs[:2], refs[2:4], refs[4:]
    side_ref, wc_ref, wct_ref, up_ref, dn_ref = refs[:5]
    refs = refs[5:]
    if dense:
        out_refs, dx_refs, gsm_ref, probs_ref = refs[:1], refs[1:2], refs[2], refs[3]
        gup_refs, gdn_refs = refs[4 : 4 + parts], refs[4 + parts : 4 + 2 * parts]
        xt_ref, g_ref, a_ref, acc_ref, dxa_ref, act_ref, dpre_ref, gt_ref = refs[4 + 2 * parts :]
    else:
        out_refs, dx_refs, gsm_ref = refs[:2], refs[2:4], refs[4]
        gup_ref, gdn_ref = refs[5:7]
        xt_ref, g_ref, a_ref, acc_ref, dxa_ref, act_ref, dpre_ref = refs[7:]
    halves = len(x_refs)
    rows, half = x_refs[0].shape
    width = halves * half
    step = pl.program_id(0)
    small = 256
    big = 512
    node = node_ref[0]
    if dense:
        split = [slice(0, width)]
    else:
        split = [
            pl.ds(pl.multiple_of(node * half, half), half),
            pl.ds(pl.multiple_of((1 - node) * half, half), half),
        ]

    @pl.when(step == 0)
    def _():
        lane = lax.broadcasted_iota(jnp.int32, (1, LANES), 1)
        is_router = lane < experts
        is_mix = (lane >= experts) & (lane < experts + 2)
        first = (lane == experts).astype(F32)
        second = (lane == experts + 1).astype(F32)
        if dense:
            turn = permutation(side_ref[...], width)
        else:
            picked = side_ref[...]

        def prepare(at):
            logits = sum(dot(x_refs[n][at, :], wc_ref[split[n], :]) for n in range(halves))

            def soft(mask):
                masked = jnp.where(mask, logits, -1e30)
                shifted = jnp.exp(masked - jnp.max(masked, axis=1, keepdims=True))
                return shifted / jnp.sum(shifted, axis=1, keepdims=True)

            mix = soft(is_mix)
            if dense:
                factor = jnp.sum(mix * first, axis=1, keepdims=True)
                probs_ref[at, :] = jnp.where(is_router, soft(is_router), mix)
                a_ref[at, :] = jnp.where(is_mix, first - mix, 0.0)
            else:
                router = soft(is_router)
                gate = jnp.sum(router * picked, axis=1, keepdims=True)
                factor = gate * jnp.sum(mix * second, axis=1, keepdims=True)
                a_ref[at, :] = jnp.where(
                    is_router, picked - router, jnp.where(is_mix, second - mix, 0.0)
                )
            for n in range(halves):
                scaled = (factor * c_refs[n][at, :].astype(F32)).astype(BF16)
                g_ref[at, split[n]] = scaled
                if dense:
                    xt_ref[:, at] = dot_t(turn, x_refs[n][at, :]).astype(BF16)
                    gt_ref[:, at] = dot_t(turn, scaled).astype(BF16)
                else:
                    xt_ref[split[n], at] = x_refs[n][at, :].T
            acc_ref[at, :] = jnp.zeros((small, width), F32)
            dxa_ref[at, :] = jnp.zeros((small, width), F32)

        chunks(rows, small, prepare)

    def forward(at):
        pre = sum(dot(x_refs[n][at, :], up_ref[split[n], :]) for n in range(halves))
        square = pre * pre
        bend = jnp.tanh(pre * (GELU_A + GELU_A * GELU_B * square))
        side = 0.5 * (1.0 + bend)
        act = (pre * side).astype(BF16)
        slope = side + 0.5 * pre * (1.0 - bend * bend) * (GELU_A + 3.0 * GELU_A * GELU_B * square)
        act_ref[at, :] = act
        if dense:
            act_grad = dot(g_ref[at, :], dn_ref[...])
            acc_ref[at, :] += dot_t(act, dn_ref[...])
        else:
            act_grad = dot_t(g_ref[at, :], dn_ref[...])
            acc_ref[at, :] += dot(act, dn_ref[...])
        pre_grad = (slope * act_grad).astype(BF16)
        dpre_ref[at, :] = pre_grad
        dxa_ref[at, :] += dot_t(pre_grad, up_ref[...])

    chunks(rows, big, forward)
    if dense:
        size = width // parts
        for part in range(parts):

            def weights(at):
                start = pl.multiple_of(part * size + at.start, small)
                rows_at = pl.ds(start, small)
                gup_refs[part][at, :] = dot(xt_ref[rows_at, :], dpre_ref[...]).astype(BF16)
                gdn_refs[part][at, :] = dot(gt_ref[rows_at, :], act_ref[...]).astype(BF16)

            chunks(size, small, weights)
    else:

        def weights(at):
            gup_ref[at, :] = dot(xt_ref[at, :], dpre_ref[...])

        chunks(width, small, weights)
        gdn_ref[...] = dot_n(act_ref[...], g_ref[...])

    @pl.when(step == pl.num_programs(0) - 1)
    def _():
        gsm_ref[...] = jnp.zeros_like(gsm_ref)

        def finish(at):
            out = acc_ref[at, :]
            strength = jnp.sum(g_ref[at, :].astype(F32) * out, axis=1, keepdims=True)
            logit_grad = strength * a_ref[at, :]
            low = logit_grad.astype(BF16)
            turned = logit_grad.T.astype(BF16)
            for n in range(halves):
                gsm_ref[:, split[n]] += dot(turned, x_refs[n][at, :])
                part = acc_ref[at, split[n]]
                if dense:
                    mixes = probs_ref[at, :]
                    lane = lax.broadcasted_iota(jnp.int32, (1, LANES), 1)
                    part = part * jnp.sum(
                        jnp.where(lane == experts, mixes, 0.0), axis=1, keepdims=True
                    )
                out_refs[n][at, :] = part.astype(BF16)
                dx_refs[n][at, :] = (dxa_ref[at, split[n]] + dot(low, wct_ref[:, split[n]])).astype(
                    BF16
                )

        chunks(rows, small, finish)


def branch(node, xs, cs, side, head, head_t, up, down, experts, parts):
    dense = len(xs) == 1
    rows, half = xs[0].shape
    width = len(xs) * half
    hidden = up.shape[1]
    block = 256
    column = lambda size: spec((size, block), lambda f, n: (0, f))
    up_spec = column(width)
    down_spec = up_spec if dense else spec((block, width), lambda f, n: (f, 0))
    outs = [(fixed((rows, half)), struct((rows, half), BF16))] * (2 * len(xs))
    outs = outs + [(fixed((LANES, width)), struct((LANES, width), F32))]
    scratch = [
        pltpu.VMEM((width, rows), BF16),
        pltpu.VMEM((rows, width), BF16),
        pltpu.VMEM((rows, LANES), F32),
        pltpu.VMEM((rows, width), F32),
        pltpu.VMEM((rows, width), F32),
        pltpu.VMEM((rows, block), BF16),
        pltpu.VMEM((rows, block), BF16),
    ]
    if dense:
        outs = outs + [(fixed((rows, LANES)), struct((rows, LANES), F32))]
        size = width // parts
        outs = outs + [(column(size), struct((size, hidden), BF16))] * (2 * parts)
        scratch = scratch + [pltpu.VMEM((width, rows), BF16)]
    else:
        outs = outs + [
            (up_spec, struct(up.shape, F32)),
            (down_spec, struct(down.shape, F32)),
        ]
    return pl.pallas_call(
        functools.partial(branch_kernel, dense, experts, parts),
        grid_spec=pltpu.PrefetchScalarGridSpec(
            num_scalar_prefetch=1,
            grid=(hidden // block,),
            in_specs=[fixed((rows, half))] * (2 * len(xs))
            + [
                fixed(side.shape),
                fixed((width, LANES)),
                fixed((LANES, width)),
                up_spec,
                down_spec,
            ],
            out_specs=[one for one, _ in outs],
            scratch_shapes=scratch,
        ),
        out_shape=[shape for _, shape in outs],
        cost_estimate=pl.CostEstimate(
            flops=12 * rows * width * hidden,
            bytes_accessed=12 * width * hidden + 8 * rows * width,
            transcendentals=rows * hidden,
        ),
        compiler_params=pltpu.CompilerParams(vmem_limit_bytes=58 << 20),
        name="dense_branch" if dense else "expert_branch",
    )(node, *xs, *cs, side, head, head_t, up, down)


def tail_kernel(
    parts,
    ln_lane,
    node_ref,
    source_ref,
    x_ref,
    gain_ref,
    small_ref,
    dq_ref,
    dk_ref,
    dv_ref,
    w_ref,
    keep_ref,
    send_ref,
    *refs,
):
    part_refs = refs[:parts]
    xt_ref, acc_ref = refs[parts:]
    seq, width = x_ref.shape
    size = width // parts
    own = keep_ref.shape[0]
    step = pl.program_id(0)
    last = pl.num_programs(0) - 1

    @pl.when(step == 0)
    def _():
        turn = permutation(source_ref[...], width)

        def prepare(at):
            xt_ref[:, at] = dot_t(turn, x_ref[at, :]).astype(BF16)
            acc_ref[at, :] = jnp.zeros((256, width), F32)

        chunks(seq, 256, prepare)

    for which, ref in enumerate((dq_ref, dk_ref, dv_ref)):

        @pl.when((step < last) & (step % 3 == which))
        def _():
            for part in range(parts):

                def weights(at):
                    rows_at = pl.ds(pl.multiple_of(part * size + at.start, 256), 256)
                    part_refs[part][at, :] = dot(xt_ref[rows_at, :], ref[...]).astype(BF16)

                chunks(size, 256, weights)

            def back(at):
                acc_ref[at, :] += dot_t(ref[at, :], w_ref[...])

            chunks(seq, 256, back)

    @pl.when(step == last)
    def _():
        gain = gain_ref[...]
        node = node_ref[0]
        total = jnp.zeros((1, width), F32)
        for piece in range(seq // 256):
            rows = slice(piece * 256, (piece + 1) * 256)
            total = total + jnp.sum(
                acc_ref[rows] * (x_ref[rows, :].astype(F32) / gain), axis=0, keepdims=True
            )
        row = lax.broadcasted_iota(jnp.int32, (LANES, 1), 0)
        small = (small_ref[...] + jnp.where(row == ln_lane, total, 0.0)).astype(BF16)
        turned = dot_t(permutation(source_ref[...], width), small).astype(BF16)
        for part in range(parts):
            part_refs[part][:, 0:LANES] = turned[part * size : (part + 1) * size]
            part_refs[part][:, LANES:WIDE] = jnp.zeros((size, WIDE - LANES), BF16)
        keep_ref[...] = acc_ref[pl.ds(pl.multiple_of(node * own, own), own), :]
        send_ref[...] = acc_ref[pl.ds(pl.multiple_of((1 - node) * own, own), own), :].astype(BF16)


def tail(node, source, normed, gain, small, dq, dk, dv, w_qkv, parts, ln_lane):
    seq, width = normed.shape
    blocks = width // WIDE
    half = blocks // 2
    steps = 3 * half
    grad_spec = spec((seq, WIDE), lambda i, n: (0, jnp.minimum(i // 3, half - 1)))

    def column(i, n):
        i = jnp.minimum(i, steps - 1)
        return (0, (i % 3) * blocks + n[0] * half + i // 3)

    part = (width // parts, WIDE)
    return pl.pallas_call(
        functools.partial(tail_kernel, parts, ln_lane),
        grid_spec=pltpu.PrefetchScalarGridSpec(
            num_scalar_prefetch=1,
            grid=(steps + 1,),
            in_specs=[
                fixed(source.shape),
                fixed(normed.shape),
                fixed((1, width)),
                fixed((LANES, width)),
                grad_spec,
                grad_spec,
                grad_spec,
                spec((width, WIDE), column),
            ],
            out_specs=[fixed((seq // 2, width)), fixed((seq // 2, width))]
            + [spec(part, lambda i, n: (0, i))] * parts,
            scratch_shapes=[pltpu.VMEM((width, seq), BF16), pltpu.VMEM((seq, width), F32)],
        ),
        out_shape=[struct((seq // 2, width), F32), struct((seq // 2, width), BF16)]
        + [struct((width // parts, (steps + 1) * WIDE), BF16)] * parts,
        cost_estimate=pl.CostEstimate(
            flops=6 * seq * width * width, bytes_accessed=16 * seq * width, transcendentals=0
        ),
        compiler_params=pltpu.CompilerParams(vmem_limit_bytes=32 << 20),
        name="tail",
    )(node, source, normed, gain[None], small, dq, dk, dv, w_qkv)


class Grid:

    def __init__(self, members):
        self.third = 4 if members % 4 == 0 else 1
        self.first = round((members // self.third) ** 0.5)
        assert self.third * self.first * self.first == members
        self.members = members
        self.sizes = (self.first, self.first, self.third)

    def digits(self, node, member):
        low, high = member % self.first, (member // self.first) % self.first
        top = member // (self.first * self.first)
        return (low, high, top) if node == 0 else (high, low, top)

    def index(self, node, digits):
        low, high = (digits[0], digits[1]) if node == 0 else (digits[1], digits[0])
        return (digits[2] * self.first + high) * self.first + low

    def shift(self, stage, by):
        pairs = []
        for node in range(2):
            for member in range(self.members):
                digits = list(self.digits(node, member))
                digits[stage] = (digits[stage] + by) % self.sizes[stage]
                target = self.index(node, digits)
                pairs.append((node * self.members + member, node * self.members + target))
        return pairs

    def order(self, node, member):
        tables = []
        for one in range(2):
            table = []
            for own in range(self.members):
                base = self.digits(one, own)
                row = []
                for place in range(self.members):
                    steps = (
                        place // (self.first * self.third),
                        (place // self.third) % self.first,
                        place % self.third,
                    )
                    row.append(
                        self.index(one, [(b + s) % k for b, s, k in zip(base, steps, self.sizes)])
                    )
                table.append(row)
            tables.append(table)
        return jnp.array(tables, jnp.int32)[node, member]

    def reduce(self, parts):
        for stage, size in enumerate(self.sizes):
            came = [
                lax.ppermute(parts[by], ("node", "expert"), self.shift(stage, by))
                for by in range(1, size)
            ]
            pieces = self.sizes[stage + 1] if stage < 2 else 1
            rows = parts[0].shape[0] // pieces
            sums = []
            for piece in range(pieces):
                at = slice(piece * rows, (piece + 1) * rows)
                total = parts[0][at].astype(F32)
                for other in came:
                    total = total + other[at].astype(F32)
                sums.append(total.astype(BF16) if stage < 2 else total)
            parts = sums
        return parts[0]


def shards(
    tokens,
    cotangent,
    routes,
    ln1_gain,
    w_qkv,
    w_out,
    ln2_gain,
    w_router,
    w_mix,
    w_up,
    w_down,
    expert_up,
    expert_down,
):
    node = lax.axis_index("node")
    member = lax.axis_index("expert")
    members = lax.axis_size("expert")
    width = tokens.shape[2]
    half = width // 2
    own_rows = tokens.shape[1]
    seq = 2 * own_rows
    experts = w_router.shape[1]
    capacity = 3 * seq // (2 * experts)
    slots = experts * capacity
    pairs = half // LANES
    own_start = node * own_rows
    scalar = node.astype(jnp.int32).reshape(1)
    grid = Grid(members)
    parts = grid.sizes[0]
    order_of = grid.order(node, member)

    def swap(value):
        return lax.ppermute(value, "node", SWAP)

    def in_order(mine, other, axis):
        return jnp.where(
            node == 0,
            jnp.concatenate([mine, other], axis=axis),
            jnp.concatenate([other, mine], axis=axis),
        )

    own_tokens, own_cot = tokens[0], cotangent[0]
    other_tokens, other_cot = swap(own_tokens), swap(own_cot)
    seq_cot = in_order(own_cot, other_cot, 0)
    seq_tokens = in_order(own_tokens, other_tokens, 0)

    group_routes = routes.reshape(-1)
    route_onehot = group_routes[:, None] == jnp.arange(experts)[None, :]
    ones = route_onehot.astype(BF16)
    row_at = jnp.arange(seq)
    earlier = (row_at[:, None] > row_at[None, :]).astype(BF16)
    order = jnp.sum(jnp.where(route_onehot, dot(earlier, ones), 0.0), axis=1).astype(jnp.int32)
    place = jnp.where(order < capacity, group_routes * capacity + order, slots)
    slot_onehot = (place[:, None] == jnp.arange(slots)[None, :]).astype(BF16)

    def dispatch(rows):
        part = lax.dynamic_slice_in_dim(rows, node * half, half, 1)
        sent = dot_n(slot_onehot, part).astype(BF16).reshape(experts, capacity, half)
        got = lax.all_to_all(sent, "expert", split_axis=0, concat_axis=0, tiled=True)
        got = got.reshape(slots, half)
        return [got, swap(got)]

    def give_back(mine, other):
        total = (mine.astype(F32) + swap(other).astype(F32)).astype(BF16)
        got = lax.all_to_all(
            total.reshape(experts, capacity, half), "expert", split_axis=0, concat_axis=0, tiled=True
        )
        return dot(slot_onehot, got.reshape(slots, half))

    expert_cot = dispatch(seq_cot)

    qkv, normed_low = front(scalar, own_tokens, other_tokens, ln1_gain, w_qkv)
    attended_own, lse = attend(qkv, pairs)
    hidden, inner_low = middle(
        scalar, seq_tokens, attended_own, swap(attended_own), w_out, ln2_gain
    )

    expert_rows = dispatch(inner_low)
    head = jnp.concatenate(
        [w_router, w_mix, jnp.zeros((width, LANES - experts - 2), BF16)], axis=1
    )
    head_t = head.T
    picked = (jnp.arange(LANES) == member).astype(F32)[None]

    def sources(block):
        return (order_of[:, None] * block + jnp.arange(block)[None, :]).reshape(-1, 1)

    results = branch(
        scalar, [inner_low], [seq_cot], sources(width // members), head, head_t, w_up, w_down,
        experts, parts,
    )
    dense_out, dense_dx, small_dense, probs = results[:4]
    grad_up, grad_down = results[4 : 4 + parts], results[4 + parts :]
    out_keep, out_send, dx_keep, dx_send, small_expert, grad_expert_up, grad_expert_down = branch(
        scalar, expert_rows, expert_cot, picked, head, head_t, expert_up[0], expert_down[0],
        experts, parts,
    )
    grad_w_up = grid.reduce(grad_up)
    grad_w_down = grid.reduce(grad_down)

    token_dx = give_back(dx_keep, dx_send).astype(BF16)
    results = middle_back(
        scalar, sources(half // members), dense_dx, swap(dense_dx), token_dx, swap(token_dx),
        hidden, seq_cot, attended_own, ln2_gain, w_out, parts,
    )
    hidden_grad, attended_grad, ln2_row = results[:3]
    grad_w_out = grid.reduce(results[3:])
    dq, dk, dv = attend_back(qkv, attended_own, attended_grad, lse)

    token_out = give_back(out_keep, out_send)
    gate = jnp.sum(jnp.where(route_onehot, probs[:, :experts], 0.0), axis=1, keepdims=True)
    scaled = gate * probs[:, experts + 1 : experts + 2] * token_out
    total_out = dense_out.astype(F32) + in_order(scaled, jnp.zeros_like(scaled), 1)
    total_out = total_out.astype(BF16)
    out_mine = lax.dynamic_slice_in_dim(total_out, own_start, own_rows, 0)
    out_other = swap(lax.dynamic_slice_in_dim(total_out, own_rows - own_start, own_rows, 0))
    hidden_own = lax.dynamic_slice_in_dim(hidden, own_start, own_rows, 0)
    mixed_out = (hidden_own + out_mine.astype(F32) + out_other.astype(F32)).astype(BF16)

    small = small_dense + small_expert
    small = small + jnp.where(jnp.arange(LANES)[:, None] == experts + 3, ln2_row[0:1], 0.0)
    block = width // (2 * members)
    source = (
        order_of[:, None, None] * block
        + jnp.arange(2)[None, :, None] * half
        + jnp.arange(block)[None, None, :]
    ).reshape(-1, 1)
    results = tail(
        scalar, source, normed_low, ln1_gain, small, dq, dk, dv, w_qkv, parts, experts + 2
    )
    normed_grad = results[0] + swap(results[1]).astype(F32)
    _, base_one, inverse_one = layer_norm(own_tokens.astype(F32), ln1_gain)
    input_grad = lax.dynamic_slice_in_dim(hidden_grad, own_start, own_rows, 0) + norm_backward(
        normed_grad, base_one, inverse_one, ln1_gain
    )
    last = grid.reduce(results[2:]).reshape(2, block, -1)
    kept = lax.dynamic_index_in_dim(last, node, 0, False)
    other = swap(lax.dynamic_index_in_dim(last, 1 - node, 0, False).astype(BF16)).astype(F32)

    def columns(rows):
        rows = rows[:, : 3 * half].reshape(block, half // WIDE, 3, WIDE)
        return rows.transpose(0, 2, 1, 3).reshape(block, 3, half)

    grad_w_qkv = in_order(columns(kept), columns(other), 2).reshape(block, 3 * width)
    small = kept[:, 3 * half :] + other[:, 3 * half :]
    return (
        mixed_out.reshape(tokens.shape),
        input_grad.reshape(tokens.shape),
        small[:, experts + 2],
        grad_w_qkv,
        grad_w_out,
        small[:, experts + 3],
        small[:, :experts],
        small[:, experts : experts + 2],
        grad_w_up,
        grad_w_down,
        grad_expert_up[None],
        grad_expert_down[None],
    )


def solution(mesh):
    return jax.shard_map(
        shards,
        mesh=mesh,
        in_specs=(
            P("expert", "node", None),
            P("expert", "node", None),
            P("expert", None, None),
            P(),
            P(),
            P(),
            P(),
            P(),
            P(),
            P(None, "node"),
            P(None, "node"),
            P("expert", None, "node"),
            P("expert", "node", None),
        ),
        out_specs=(
            P("expert", "node", None),
            P("expert", "node", None),
            P(("node", "expert")),
            P(("node", "expert"), None),
            P(("node", "expert"), None),
            P(("node", "expert")),
            P(("node", "expert"), None),
            P(("node", "expert"), None),
            P("expert", "node"),
            P("expert", "node"),
            P("expert", None, "node"),
            P("expert", "node", None),
        ),
        check_vma=False,
    )
```

```python
import functools

import jax
import jax.numpy as jnp
from jax import lax
from jax.experimental import pallas as pl
from jax.experimental.pallas import tpu as pltpu
from jax.sharding import PartitionSpec as P


HEAD_DIM = 64
EPS = 1e-05
LANES = 128
LOG2E = 1.4426950408889634
GELU_A = 0.7978845608028654
GELU_B = 0.044715
SWAP = [(0, 1), (1, 0)]
F32 = jnp.float32
BF16 = jnp.bfloat16


def dot(left, right):
    return jnp.dot(left, right, preferred_element_type=F32)


def dot_t(left, right):
    return lax.dot_general(left, right, (((1,), (1,)), ((), ())), preferred_element_type=F32)


def dot_n(left, right):
    return lax.dot_general(left, right, (((0,), (0,)), ((), ())), preferred_element_type=F32)


def layer_norm(values, gain):
    average = jnp.mean(values, axis=-1, keepdims=True)
    centered = values - average
    inverse = lax.rsqrt(jnp.mean(centered * centered, axis=-1, keepdims=True) + EPS)
    normed = centered * inverse
    return (normed * gain, normed, inverse)


def norm_backward(upstream, normed, inverse, gain):
    scaled = upstream * gain
    inner_term = (
        scaled
        - jnp.mean(scaled, axis=-1, keepdims=True)
        - normed * jnp.mean(scaled * normed, axis=-1, keepdims=True)
    )
    return inner_term * inverse


def spec(shape, index):
    return pl.BlockSpec(shape, index)


def fixed(shape):
    return pl.BlockSpec(shape, lambda *_: (0,) * len(shape), pipeline_mode=pl.Buffered(1))


def struct(shape, kind):
    return jax.ShapeDtypeStruct(shape, kind)


def chunks(count, size, step):
    def run(index, carry):
        step(pl.ds(pl.multiple_of(index * size, size), size))
        return carry

    lax.fori_loop(0, count // size, run, 0)


def after(value, *others):
    return lax.optimization_barrier((value, others))[0]


def row_pick(node, index, own, other):
    return jnp.where(index == node, own, other)


def permutation(source, columns):
    lane = lax.broadcasted_iota(jnp.int32, (source.shape[0], columns), 1)
    return (source == lane).astype(F32).astype(BF16)


WIDE = 256


def front_kernel(node_ref, own_ref, other_ref, gain_ref, w_ref, qkv_ref, normed_ref):
    rows = own_ref.shape[0]
    node = node_ref[0]

    @pl.when(pl.program_id(0) == 0)
    def _():
        for place, part in ((node, own_ref), (1 - node, other_ref)):
            def norm(at):
                normed, _, _ = layer_norm(part[at, :].astype(F32), gain_ref[...])
                start = pl.multiple_of(place * rows + at.start, 128)
                normed_ref[pl.ds(start, 128), :] = normed.astype(BF16)

            chunks(rows, 128, norm)

    def project(at):
        qkv_ref[at, :] = dot(normed_ref[at, :], w_ref[...]).astype(BF16)

    chunks(2 * rows, 512, project)


def front(node, own, other, gain, w_qkv):
    rows, width = own.shape
    blocks = width // WIDE
    half = blocks // 2
    return pl.pallas_call(
        front_kernel,
        grid_spec=pltpu.PrefetchScalarGridSpec(
            num_scalar_prefetch=1,
            grid=(3 * half,),
            in_specs=[
                fixed(own.shape),
                fixed(own.shape),
                fixed((1, width)),
                spec((width, WIDE), lambda i, n: (0, (i % 3) * blocks + n[0] * half + i // 3)),
            ],
            out_specs=[
                spec((2 * rows, WIDE), lambda i, n: (0, i)),
                fixed((2 * rows, width)),
            ],
        ),
        out_shape=[struct((2 * rows, 3 * width // 2), BF16), struct((2 * rows, width), BF16)],
        cost_estimate=pl.CostEstimate(
            flops=6 * rows * width * width, bytes_accessed=14 * rows * width, transcendentals=0
        ),
        compiler_params=pltpu.CompilerParams(vmem_limit_bytes=32 << 20),
        name="front",
    )(node, own, other, gain[None], w_qkv)


QB = 256


def head_specs(seq):
    return [spec((seq, LANES), lambda j, at=at: (0, (j // 2) * 6 + at + j % 2)) for at in (0, 2, 4)]


def attend_kernel(q_ref, k_ref, v_ref, out_ref, lse_ref, ot_ref):
    seq = q_ref.shape[0]
    factor = HEAD_DIM ** (-0.5) * LOG2E
    lane = lax.broadcasted_iota(jnp.int32, (1, LANES), 1)
    v_t = v_ref[...].T
    below = lax.broadcasted_iota(jnp.int32, (QB, QB), 0) <= lax.broadcasted_iota(
        jnp.int32, (QB, QB), 1
    )
    for head in range(2):
        keep = (lane // HEAD_DIM) == head
        keys = jnp.where(keep, k_ref[...], 0)
        v_rows = v_t[head * HEAD_DIM : (head + 1) * HEAD_DIM]
        for block in range(seq // QB):
            lo, hi = block * QB, (block + 1) * QB
            queries = q_ref[lo:hi]
            diag = jnp.where(below, dot_t(keys[lo:hi], queries), -1e30)
            top = jnp.max(diag, axis=0, keepdims=True)
            if lo:
                past = dot_t(keys[:lo], queries)
                top = jnp.maximum(top, jnp.max(past, axis=0, keepdims=True))
            p_diag = jnp.exp2((diag - top) * factor)
            total = jnp.sum(p_diag, axis=0, keepdims=True)
            acc = dot(v_rows[:, lo:hi], p_diag.astype(BF16))
            if lo:
                p_past = jnp.exp2((past - top) * factor)
                total = total + jnp.sum(p_past, axis=0, keepdims=True)
                acc = acc + dot(v_rows[:, :lo], p_past.astype(BF16))
            ot_ref[head * HEAD_DIM : (head + 1) * HEAD_DIM, lo:hi] = acc * (1.0 / total)
            lse_ref[0, head : head + 1, lo:hi] = top * factor + jnp.log2(total)
    out_ref[...] = ot_ref[...].T.astype(BF16)


def attend(qkv, pairs):
    seq = qkv.shape[0]
    return pl.pallas_call(
        attend_kernel,
        grid=(pairs,),
        in_specs=head_specs(seq),
        out_specs=[
            spec((seq, LANES), lambda j: (0, j)),
            spec((1, 8, seq), lambda j: (j, 0, 0)),
        ],
        out_shape=[struct((seq, pairs * LANES), BF16), struct((pairs, 8, seq), F32)],
        scratch_shapes=[pltpu.VMEM((LANES, seq), F32)],
        cost_estimate=pl.CostEstimate(
            flops=pairs * 8 * seq * seq * LANES,
            bytes_accessed=pairs * seq * LANES * 8,
            transcendentals=pairs * seq * seq,
        ),
        compiler_params=pltpu.CompilerParams(vmem_limit_bytes=32 << 20),
        name="attend",
    )(qkv, qkv, qkv)


def attend_back_kernel(
    q_ref, k_ref, v_ref, out_ref, grad_ref, lse_ref, dq_ref, dk_ref, dv_ref, dqt_ref, dka_ref, dva_ref
):
    seq = q_ref.shape[0]
    scale = HEAD_DIM ** (-0.5)
    factor = scale * LOG2E
    lane = lax.broadcasted_iota(jnp.int32, (1, LANES), 1)
    k_t = k_ref[...].T
    product = (grad_ref[...].astype(F32) * out_ref[...].astype(F32)).T
    below = lax.broadcasted_iota(jnp.int32, (QB, QB), 0) <= lax.broadcasted_iota(
        jnp.int32, (QB, QB), 1
    )
    dka_ref[...] = jnp.zeros_like(dka_ref)
    dva_ref[...] = jnp.zeros_like(dva_ref)
    for head in range(2):
        keep = (lane // HEAD_DIM) == head
        rows = slice(head * HEAD_DIM, (head + 1) * HEAD_DIM)
        keys = jnp.where(keep, k_ref[...], 0)
        values = jnp.where(keep, v_ref[...], 0)
        delta = jnp.sum(product[rows], axis=0, keepdims=True)
        for block in range(seq // QB):
            lo, hi = block * QB, (block + 1) * QB
            queries = jnp.where(keep, q_ref[lo:hi], 0)
            grads = jnp.where(keep, grad_ref[lo:hi], 0)
            lse = lse_ref[0, head : head + 1, lo:hi]
            drop = delta[:, lo:hi]
            acc = None
            for start, stop in ((lo, hi), (0, lo)):
                if start == stop:
                    continue
                probs = jnp.exp2(dot_t(keys[start:stop], queries) * factor - lse)
                if start == lo:
                    probs = jnp.where(below, probs, 0.0)
                prob_grad = dot_t(values[start:stop], grads)
                score_grad = (probs * (prob_grad - drop)).astype(BF16)
                dva_ref[start:stop] += dot(probs.astype(BF16), grads)
                dka_ref[start:stop] += dot(score_grad, queries)
                part = dot(k_t[rows, start:stop], score_grad)
                acc = part if acc is None else acc + part
            dqt_ref[rows, lo:hi] = acc
    dq_ref[...] = (dqt_ref[...].T * scale).astype(BF16)
    dk_ref[...] = (dka_ref[...] * scale).astype(BF16)
    dv_ref[...] = dva_ref[...].astype(BF16)


def attend_back(qkv, attended, grad, lse):
    seq = qkv.shape[0]
    pairs = lse.shape[0]
    one = spec((seq, LANES), lambda j: (0, j))
    return pl.pallas_call(
        attend_back_kernel,
        grid=(pairs,),
        in_specs=head_specs(seq) + [one, one, spec((1, 8, seq), lambda j: (j, 0, 0))],
        out_specs=[one] * 3,
        out_shape=[struct(attended.shape, BF16)] * 3,
        scratch_shapes=[
            pltpu.VMEM((LANES, seq), F32),
            pltpu.VMEM((seq, LANES), F32),
            pltpu.VMEM((seq, LANES), F32),
        ],
        cost_estimate=pl.CostEstimate(
            flops=pairs * 20 * seq * seq * LANES,
            bytes_accessed=pairs * seq * LANES * 16,
            transcendentals=pairs * seq * seq,
        ),
        compiler_params=pltpu.CompilerParams(vmem_limit_bytes=32 << 20),
        name="attend_back",
    )(qkv, qkv, qkv, attended, grad, lse)


def middle_kernel(
    node_ref, tok_ref, tok_other_ref, own_ref, other_ref, w_ref, gain_ref, hidden_ref, normed_ref
):
    half = own_ref.shape[1]
    node = node_ref[0]
    index = pl.program_id(0) // (pl.num_programs(0) // 2)
    tok = row_pick(node, index, tok_ref[...], tok_other_ref[...])
    mine = pl.ds(pl.multiple_of(node * half, half), half)
    theirs = pl.ds(pl.multiple_of((1 - node) * half, half), half)
    hidden = tok.astype(F32) + (
        dot(own_ref[...], w_ref[mine, :]) + dot(other_ref[...], w_ref[theirs, :])
    )
    normed, _, _ = layer_norm(hidden, gain_ref[...])
    hidden_ref[...] = hidden
    normed_ref[...] = normed.astype(BF16)


def middle(node, tokens, tokens_other, own, other, w_out, gain):
    width = tokens.shape[1]
    seq = 2 * tokens.shape[0]
    rows = 256
    steps = seq // rows
    half_row = spec((rows, width), lambda i, n: (i % (steps // 2), 0))
    row = lambda columns: spec((rows, columns), lambda i, n: (i, 0))
    return pl.pallas_call(
        middle_kernel,
        grid_spec=pltpu.PrefetchScalarGridSpec(
            num_scalar_prefetch=1,
            grid=(seq // rows,),
            in_specs=[
                half_row,
                half_row,
                row(width // 2),
                row(width // 2),
                fixed(w_out.shape),
                fixed((1, width)),
            ],
            out_specs=[row(width), row(width)],
        ),
        out_shape=[struct((seq, width), F32), struct((seq, width), BF16)],
        cost_estimate=pl.CostEstimate(
            flops=2 * seq * width * width, bytes_accessed=12 * seq * width, transcendentals=0
        ),
        compiler_params=pltpu.CompilerParams(vmem_limit_bytes=24 << 20),
        name="middle",
    )(node, tokens, tokens_other, own, other, w_out, gain[None])


def middle_back_kernel(
    parts,
    node_ref,
    source_ref,
    dense_ref,
    dense_other_ref,
    token_ref,
    token_other_ref,
    hidden_ref,
    cot_ref,
    cot_other_ref,
    attended_ref,
    gain_ref,
    w_ref,
    grad_ref,
    attended_grad_ref,
    ln_ref,
    *refs,
):
    weight_refs = refs[:parts]
    inner_ref, acc_ref = refs[parts:]
    half = token_ref.shape[1]
    node = node_ref[0]
    step = pl.program_id(0)

    @pl.when(step == 0)
    def _():
        ln_ref[...] = jnp.zeros_like(ln_ref)
        acc_ref[...] = jnp.zeros_like(acc_ref)

    inner_ref[...] = dense_ref[...].astype(F32) + dense_other_ref[...].astype(F32)
    inner_ref[:, pl.ds(pl.multiple_of(node * half, half), half)] += token_ref[...].astype(F32)
    inner_ref[:, pl.ds(pl.multiple_of((1 - node) * half, half), half)] += token_other_ref[
        ...
    ].astype(F32)
    inner = inner_ref[...]
    gain = gain_ref[...]
    _, base, inverse = layer_norm(hidden_ref[...], gain)
    ln_ref[0:1, :] += 0.5 * jnp.sum(inner * base, axis=0, keepdims=True)
    index = step // (pl.num_programs(0) // 2)
    cot = row_pick(node, index, cot_ref[...], cot_other_ref[...])
    hidden_grad = cot.astype(F32) + norm_backward(inner, base, inverse, gain)
    grad_ref[...] = hidden_grad
    low = hidden_grad.astype(BF16)
    attended_grad_ref[...] = dot_t(low, w_ref[...]).astype(BF16)
    turned = dot_t(permutation(source_ref[...], half), attended_ref[...]).astype(BF16)
    acc_ref[...] += dot(turned, low)

    @pl.when(step == pl.num_programs(0) - 1)
    def _():
        size = half // parts
        for part in range(parts):
            weight_refs[part][...] = acc_ref[part * size : (part + 1) * size].astype(BF16)


def middle_back(
    node, source, dense, dense_other, token, token_other, hidden, cot, cot_other, attended, gain, w_out, parts
):
    seq, width = hidden.shape
    half = width // 2
    rows = 256
    steps = seq // rows
    half_row = spec((rows, width), lambda i, n: (i % (steps // 2), 0))
    row = lambda columns: spec((rows, columns), lambda i, n: (i, 0))
    result = (half // parts, width)
    return pl.pallas_call(
        functools.partial(middle_back_kernel, parts),
        grid_spec=pltpu.PrefetchScalarGridSpec(
            num_scalar_prefetch=1,
            grid=(seq // rows,),
            in_specs=[
                fixed(source.shape),
                row(width),
                row(width),
                row(half),
                row(half),
                row(width),
                half_row,
                half_row,
                row(half),
                fixed((1, width)),
                spec((half, width), lambda i, n: (n[0], 0)),
            ],
            out_specs=[row(width), row(half), fixed((8, width))] + [fixed(result)] * parts,
            scratch_shapes=[pltpu.VMEM((rows, width), F32), pltpu.VMEM((half, width), F32)],
        ),
        out_shape=[
            struct((seq, width), F32),
            struct((seq, half), BF16),
            struct((8, width), F32),
        ]
        + [struct(result, BF16)] * parts,
        cost_estimate=pl.CostEstimate(
            flops=2 * seq * width * width, bytes_accessed=18 * seq * width, transcendentals=0
        ),
        compiler_params=pltpu.CompilerParams(vmem_limit_bytes=32 << 20),
        name="middle_back",
    )(
        node, source, dense, dense_other, token, token_other, hidden, cot, cot_other, attended,
        gain[None], w_out,
    )


def dispatch_kernel(node_ref, place_ref, own_ref, other_ref, sent_ref):
    size = sent_ref.shape[0]
    node = node_ref[0]
    slot = pl.program_id(0) * size + lax.broadcasted_iota(jnp.int32, (size, 1), 0)
    total = None
    for at, ref in ((node, own_ref), (1 - node, other_ref)):
        place = place_ref[pl.ds(at, 1), :]
        part = dot((place == slot).astype(F32).astype(BF16), ref[...])
        total = part if total is None else total + part
    sent_ref[...] = total.astype(BF16)


def dispatch_rows(node, place, own, other, slots):
    rows = place.shape[1]
    half = own.shape[1] // 2
    size = 256
    if own.shape[0] == rows:
        first = spec((rows, half), lambda i, n: (0, n[0]))
        second = first
    else:
        first = spec((rows, half), lambda i, n: (n[0], n[0]))
        second = spec((rows, half), lambda i, n: (1 - n[0], n[0]))
    return pl.pallas_call(
        dispatch_kernel,
        grid_spec=pltpu.PrefetchScalarGridSpec(
            num_scalar_prefetch=1,
            grid=(slots // size,),
            in_specs=[fixed(place.shape), first, second],
            out_specs=spec((size, half), lambda i, n: (i, 0)),
        ),
        out_shape=struct((slots, half), BF16),
        cost_estimate=pl.CostEstimate(
            flops=4 * slots * rows * half, bytes_accessed=4 * slots * half, transcendentals=0
        ),
        compiler_params=pltpu.CompilerParams(vmem_limit_bytes=16 << 20),
        name="dispatch",
    )(node, place, own, other)


def combine_kernel(place_ref, got_ref, out_ref):
    size = place_ref.shape[0]
    slot = lax.broadcasted_iota(jnp.int32, (size, got_ref.shape[0]), 1)
    onehot = (place_ref[...] == slot).astype(F32).astype(BF16)
    out_ref[...] = dot(onehot, got_ref[...]).astype(BF16)


def combine_rows(place, got):
    rows = place.shape[0]
    size = 256
    return pl.pallas_call(
        combine_kernel,
        grid=(rows // size,),
        in_specs=[spec((size, 1), lambda i: (i, 0)), fixed(got.shape)],
        out_specs=spec((size, got.shape[1]), lambda i: (i, 0)),
        out_shape=struct((rows, got.shape[1]), BF16),
        cost_estimate=pl.CostEstimate(
            flops=2 * rows * got.shape[0] * got.shape[1],
            bytes_accessed=4 * rows * got.shape[1],
            transcendentals=0,
        ),
        compiler_params=pltpu.CompilerParams(vmem_limit_bytes=16 << 20),
        name="combine",
    )(place, got)


def branch_kernel(dense, experts, parts, node_ref, *refs):
    if dense:
        x_refs, c_refs, refs = refs[:1], refs[1:3], refs[3:]
    else:
        x_refs, c_refs, refs = refs[:2], refs[2:4], refs[4:]
    side_ref, wc_ref, wct_ref, up_ref, dn_ref = refs[:5]
    refs = refs[5:]
    if dense:
        out_refs, dx_refs, gsm_ref, probs_ref = refs[:1], refs[1:2], refs[2], refs[3]
        gup_refs, gdn_refs = refs[4 : 4 + parts], refs[4 + parts : 4 + 2 * parts]
        xt_ref, g_ref, a_ref, acc_ref, dxa_ref, act_ref, dpre_ref, gt_ref = refs[4 + 2 * parts :]
    else:
        out_refs, dx_refs, gsm_ref = refs[:2], refs[2:4], refs[4]
        g_ref, act_ref, dpre_ref, a_ref, acc_ref, dxa_ref = refs[5:]
    halves = len(x_refs)
    rows, half = x_refs[0].shape
    width = halves * half
    step = pl.program_id(0)
    small = 256
    big = 512
    node = node_ref[0]
    if dense:
        split = [slice(0, width)]
    else:
        split = [
            pl.ds(pl.multiple_of(node * half, half), half),
            pl.ds(pl.multiple_of((1 - node) * half, half), half),
        ]

    @pl.when(step == 0)
    def _():
        lane = lax.broadcasted_iota(jnp.int32, (1, LANES), 1)
        is_router = lane < experts
        is_mix = (lane >= experts) & (lane < experts + 2)
        first = (lane == experts).astype(F32)
        second = (lane == experts + 1).astype(F32)
        if dense:
            turn = permutation(side_ref[...], width)
        else:
            picked = side_ref[...]

        def prepare(at):
            logits = sum(dot(x_refs[n][at, :], wc_ref[split[n], :]) for n in range(halves))

            def soft(mask):
                masked = jnp.where(mask, logits, -1e30)
                shifted = jnp.exp(masked - jnp.max(masked, axis=1, keepdims=True))
                return shifted / jnp.sum(shifted, axis=1, keepdims=True)

            mix = soft(is_mix)
            if dense:
                factor = jnp.sum(mix * first, axis=1, keepdims=True)
                probs_ref[at, :] = jnp.where(is_router, soft(is_router), mix)
                a_ref[at, :] = jnp.where(is_mix, first - mix, 0.0)
            else:
                router = soft(is_router)
                gate = jnp.sum(router * picked, axis=1, keepdims=True)
                factor = gate * jnp.sum(mix * second, axis=1, keepdims=True)
                a_ref[at, :] = jnp.where(
                    is_router, picked - router, jnp.where(is_mix, second - mix, 0.0)
                )
            if dense:
                own = c_refs[0].shape[0]
                place = at.start // own
                inside = pl.ds(pl.multiple_of(at.start - place * own, small), small)
                cot = row_pick(node, place, c_refs[0][inside, :], c_refs[1][inside, :])
                scaled = (factor * cot.astype(F32)).astype(BF16)
                g_ref[at, :] = scaled
                xt_ref[:, at] = dot_t(turn, x_refs[0][at, :]).astype(BF16)
                gt_ref[:, at] = dot_t(turn, scaled).astype(BF16)
            else:
                for n in range(halves):
                    g_ref[at, split[n]] = (factor * c_refs[n][at, :].astype(F32)).astype(BF16)
            acc_ref[at, :] = jnp.zeros((small, width), F32)
            dxa_ref[at, :] = jnp.zeros((small, width), F32)

        chunks(rows, small, prepare)

    def forward(at):
        pre = sum(dot(x_refs[n][at, :], up_ref[split[n], :]) for n in range(halves))
        square = pre * pre
        bend = jnp.tanh(pre * (GELU_A + GELU_A * GELU_B * square))
        side = 0.5 * (1.0 + bend)
        act = (pre * side).astype(BF16)
        slope = side + 0.5 * pre * (1.0 - bend * bend) * (GELU_A + 3.0 * GELU_A * GELU_B * square)
        act_ref[at, :] = act
        if dense:
            act_grad = dot(g_ref[at, :], dn_ref[...])
            acc_ref[at, :] += dot_t(act, dn_ref[...])
        else:
            act_grad = dot_t(g_ref[at, :], dn_ref[...])
            acc_ref[at, :] += dot(act, dn_ref[...])
        pre_grad = (slope * act_grad).astype(BF16)
        dpre_ref[at, :] = pre_grad
        dxa_ref[at, :] += dot_t(pre_grad, up_ref[...])

    chunks(rows, big, forward)
    if dense:
        size = width // parts
        for part in range(parts):

            def weights(at):
                start = pl.multiple_of(part * size + at.start, small)
                rows_at = pl.ds(start, small)
                gup_refs[part][at, :] = dot(xt_ref[rows_at, :], dpre_ref[...]).astype(BF16)
                gdn_refs[part][at, :] = dot(gt_ref[rows_at, :], act_ref[...]).astype(BF16)

            chunks(size, small, weights)

    @pl.when(step == pl.num_programs(0) - 1)
    def _():
        gsm_ref[...] = jnp.zeros_like(gsm_ref)

        def finish(at):
            out = acc_ref[at, :]
            strength = jnp.sum(g_ref[at, :].astype(F32) * out, axis=1, keepdims=True)
            logit_grad = strength * a_ref[at, :]
            low = logit_grad.astype(BF16)
            turned = logit_grad.T.astype(BF16)
            for n in range(halves):
                gsm_ref[:, split[n]] += dot(turned, x_refs[n][at, :])
                part = acc_ref[at, split[n]]
                if dense:
                    mixes = probs_ref[at, :]
                    lane = lax.broadcasted_iota(jnp.int32, (1, LANES), 1)
                    part = part * jnp.sum(
                        jnp.where(lane == experts, mixes, 0.0), axis=1, keepdims=True
                    )
                out_refs[n][at, :] = part.astype(BF16)
                dx_refs[n][at, :] = (dxa_ref[at, split[n]] + dot(low, wct_ref[:, split[n]])).astype(
                    BF16
                )

        chunks(rows, small, finish)


def branch(node, xs, cs, side, head, head_t, up, down, experts, parts):
    dense = len(xs) == 1
    rows, half = xs[0].shape
    width = len(xs) * half
    hidden = up.shape[1]
    block = 512
    column = lambda size: spec((size, block), lambda f, n: (0, f))
    up_spec = column(width)
    down_spec = up_spec if dense else spec((block, width), lambda f, n: (f, 0))
    outs = [(fixed((rows, half)), struct((rows, half), BF16))] * (2 * len(xs))
    outs = outs + [(fixed((LANES, width)), struct((LANES, width), F32))]
    sums = [
        pltpu.VMEM((rows, LANES), F32),
        pltpu.VMEM((rows, width), F32),
        pltpu.VMEM((rows, width), F32),
    ]
    if dense:
        outs = outs + [(fixed((rows, LANES)), struct((rows, LANES), F32))]
        size = width // parts
        outs = outs + [(column(size), struct((size, hidden), BF16))] * (2 * parts)
        scratch = [
            pltpu.VMEM((width, rows), BF16),
            pltpu.VMEM((rows, width), BF16),
            *sums,
            pltpu.VMEM((rows, block), BF16),
            pltpu.VMEM((rows, block), BF16),
            pltpu.VMEM((width, rows), BF16),
        ]
    else:
        outs = outs + [(fixed((rows, width)), struct((rows, width), BF16))]
        outs = outs + [(column(rows), struct((rows, hidden), BF16))] * 2
        scratch = sums
    return pl.pallas_call(
        functools.partial(branch_kernel, dense, experts, parts),
        grid_spec=pltpu.PrefetchScalarGridSpec(
            num_scalar_prefetch=1,
            grid=(hidden // block,),
            in_specs=[fixed(one.shape) for one in [*xs, *cs]]
            + [
                fixed(side.shape),
                fixed((width, LANES)),
                fixed((LANES, width)),
                up_spec,
                down_spec,
            ],
            out_specs=[one for one, _ in outs],
            scratch_shapes=scratch,
        ),
        out_shape=[shape for _, shape in outs],
        cost_estimate=pl.CostEstimate(
            flops=(12 if dense else 8) * rows * width * hidden,
            bytes_accessed=12 * width * hidden + 8 * rows * width,
            transcendentals=rows * hidden,
        ),
        compiler_params=pltpu.CompilerParams(vmem_limit_bytes=58 << 20),
        name="dense_branch" if dense else "expert_branch",
    )(node, *xs, *cs, side, head, head_t, up, down)


def expert_weights_kernel(node_ref, own_ref, other_ref, g_ref, act_ref, dpre_ref, gup_ref, gdn_ref, xt_ref):
    rows, half = own_ref.shape
    node = node_ref[0]

    @pl.when(pl.program_id(0) == 0)
    def _():
        for at, ref in ((node, own_ref), (1 - node, other_ref)):
            place = pl.ds(pl.multiple_of(at * half, half), half)

            def turn(rows_at):
                xt_ref[place, rows_at] = ref[rows_at, :].T

            chunks(rows, 256, turn)

    def weights(at):
        gup_ref[at, :] = dot(xt_ref[at, :], dpre_ref[...])

    chunks(2 * half, 256, weights)
    gdn_ref[...] = dot_n(act_ref[...], g_ref[...])


def expert_weights(node, own, other, g, act, dpre):
    rows, half = own.shape
    width = 2 * half
    hidden = act.shape[1]
    block = 512
    column = spec((rows, block), lambda f, n: (0, f))
    return pl.pallas_call(
        expert_weights_kernel,
        grid_spec=pltpu.PrefetchScalarGridSpec(
            num_scalar_prefetch=1,
            grid=(hidden // block,),
            in_specs=[fixed(own.shape), fixed(own.shape), fixed(g.shape), column, column],
            out_specs=[
                spec((width, block), lambda f, n: (0, f)),
                spec((block, width), lambda f, n: (f, 0)),
            ],
            scratch_shapes=[pltpu.VMEM((width, rows), BF16)],
        ),
        out_shape=[struct((width, hidden), F32), struct((hidden, width), F32)],
        cost_estimate=pl.CostEstimate(
            flops=4 * rows * width * hidden,
            bytes_accessed=8 * width * hidden + 4 * rows * hidden,
            transcendentals=0,
        ),
        compiler_params=pltpu.CompilerParams(vmem_limit_bytes=48 << 20),
        name="expert_weights",
    )(node, own, other, g, act, dpre)


def tail_kernel(
    parts,
    ln_lane,
    node_ref,
    source_ref,
    x_ref,
    gain_ref,
    small_ref,
    dq_ref,
    dk_ref,
    dv_ref,
    w_ref,
    keep_ref,
    send_ref,
    *refs,
):
    part_refs = refs[:parts]
    xt_ref, acc_ref = refs[parts:]
    seq, width = x_ref.shape
    size = width // parts
    own = keep_ref.shape[0]
    step = pl.program_id(0)
    last = pl.num_programs(0) - 1

    @pl.when(step == 0)
    def _():
        turn = permutation(source_ref[...], width)

        def prepare(at):
            xt_ref[:, at] = dot_t(turn, x_ref[at, :]).astype(BF16)
            acc_ref[at, :] = jnp.zeros((256, width), F32)

        chunks(seq, 256, prepare)

    for which, ref in enumerate((dq_ref, dk_ref, dv_ref)):

        @pl.when((step < last) & (step % 3 == which))
        def _():
            for part in range(parts):

                def weights(at):
                    rows_at = pl.ds(pl.multiple_of(part * size + at.start, 256), 256)
                    part_refs[part][at, :] = dot(xt_ref[rows_at, :], ref[...]).astype(BF16)

                chunks(size, 256, weights)

            def back(at):
                acc_ref[at, :] += dot_t(ref[at, :], w_ref[...])

            chunks(seq, 256, back)

    @pl.when(step == last)
    def _():
        gain = gain_ref[...]
        node = node_ref[0]
        total = jnp.zeros((1, width), F32)
        for piece in range(seq // 256):
            rows = slice(piece * 256, (piece + 1) * 256)
            total = total + jnp.sum(
                acc_ref[rows] * (x_ref[rows, :].astype(F32) / gain), axis=0, keepdims=True
            )
        row = lax.broadcasted_iota(jnp.int32, (LANES, 1), 0)
        small = (small_ref[...] + jnp.where(row == ln_lane, total, 0.0)).astype(BF16)
        turned = dot_t(permutation(source_ref[...], width), small).astype(BF16)
        for part in range(parts):
            part_refs[part][:, 0:LANES] = turned[part * size : (part + 1) * size]
            part_refs[part][:, LANES:WIDE] = jnp.zeros((size, WIDE - LANES), BF16)
        keep_ref[...] = acc_ref[pl.ds(pl.multiple_of(node * own, own), own), :]
        send_ref[...] = acc_ref[pl.ds(pl.multiple_of((1 - node) * own, own), own), :].astype(BF16)


def tail(node, source, normed, gain, small, dq, dk, dv, w_qkv, parts, ln_lane):
    seq, width = normed.shape
    blocks = width // WIDE
    half = blocks // 2
    steps = 3 * half
    grad_spec = spec((seq, WIDE), lambda i, n: (0, jnp.minimum(i // 3, half - 1)))

    def column(i, n):
        i = jnp.minimum(i, steps - 1)
        return (0, (i % 3) * blocks + n[0] * half + i // 3)

    part = (width // parts, WIDE)
    return pl.pallas_call(
        functools.partial(tail_kernel, parts, ln_lane),
        grid_spec=pltpu.PrefetchScalarGridSpec(
            num_scalar_prefetch=1,
            grid=(steps + 1,),
            in_specs=[
                fixed(source.shape),
                fixed(normed.shape),
                fixed((1, width)),
                fixed((LANES, width)),
                grad_spec,
                grad_spec,
                grad_spec,
                spec((width, WIDE), column),
            ],
            out_specs=[fixed((seq // 2, width)), fixed((seq // 2, width))]
            + [spec(part, lambda i, n: (0, i))] * parts,
            scratch_shapes=[pltpu.VMEM((width, seq), BF16), pltpu.VMEM((seq, width), F32)],
        ),
        out_shape=[struct((seq // 2, width), F32), struct((seq // 2, width), BF16)]
        + [struct((width // parts, (steps + 1) * WIDE), BF16)] * parts,
        cost_estimate=pl.CostEstimate(
            flops=6 * seq * width * width, bytes_accessed=16 * seq * width, transcendentals=0
        ),
        compiler_params=pltpu.CompilerParams(vmem_limit_bytes=32 << 20),
        name="tail",
    )(node, source, normed, gain[None], small, dq, dk, dv, w_qkv)


class Grid:

    def __init__(self, members):
        self.third = 4 if members % 4 == 0 else 1
        self.first = round((members // self.third) ** 0.5)
        assert self.third * self.first * self.first == members
        self.members = members
        self.sizes = (self.first, self.first, self.third)

    def digits(self, node, member):
        low, high = member % self.first, (member // self.first) % self.first
        top = member // (self.first * self.first)
        return (low, high, top) if node == 0 else (high, low, top)

    def index(self, node, digits):
        low, high = (digits[0], digits[1]) if node == 0 else (digits[1], digits[0])
        return (digits[2] * self.first + high) * self.first + low

    def shift(self, stage, by):
        pairs = []
        for node in range(2):
            for member in range(self.members):
                digits = list(self.digits(node, member))
                digits[stage] = (digits[stage] + by) % self.sizes[stage]
                target = self.index(node, digits)
                pairs.append((node * self.members + member, node * self.members + target))
        return pairs

    def order(self, node, member):
        tables = []
        for one in range(2):
            table = []
            for own in range(self.members):
                base = self.digits(one, own)
                row = []
                for place in range(self.members):
                    steps = (
                        place // (self.first * self.third),
                        (place // self.third) % self.first,
                        place % self.third,
                    )
                    row.append(
                        self.index(one, [(b + s) % k for b, s, k in zip(base, steps, self.sizes)])
                    )
                table.append(row)
            tables.append(table)
        return jnp.array(tables, jnp.int32)[node, member]

    def reduce(self, parts, gates=(None, None, None)):
        for stage, size in enumerate(self.sizes):
            came = [
                lax.ppermute(parts[by], ("node", "expert"), self.shift(stage, by))
                for by in range(1, size)
            ]
            if gates[stage] is not None:
                came = [after(other, gates[stage]) for other in came]
            pieces = self.sizes[stage + 1] if stage < 2 else 1
            rows = parts[0].shape[0] // pieces
            sums = []
            for piece in range(pieces):
                at = slice(piece * rows, (piece + 1) * rows)
                total = parts[0][at].astype(F32)
                for other in came:
                    total = total + other[at].astype(F32)
                sums.append(total.astype(BF16) if stage < 2 else total)
            parts = sums
        return parts[0]


def shards(
    tokens,
    cotangent,
    routes,
    ln1_gain,
    w_qkv,
    w_out,
    ln2_gain,
    w_router,
    w_mix,
    w_up,
    w_down,
    expert_up,
    expert_down,
):
    node = lax.axis_index("node")
    member = lax.axis_index("expert")
    members = lax.axis_size("expert")
    width = tokens.shape[2]
    half = width // 2
    own_rows = tokens.shape[1]
    seq = 2 * own_rows
    experts = w_router.shape[1]
    capacity = 3 * seq // (2 * experts)
    slots = experts * capacity
    pairs = half // LANES
    own_start = node * own_rows
    scalar = node.astype(jnp.int32).reshape(1)
    grid = Grid(members)
    parts = grid.sizes[0]
    order_of = grid.order(node, member)

    def swap(value):
        return lax.ppermute(value, "node", SWAP)

    def in_order(mine, other, axis):
        return jnp.where(
            node == 0,
            jnp.concatenate([mine, other], axis=axis),
            jnp.concatenate([other, mine], axis=axis),
        )

    own_tokens, own_cot = tokens[0], cotangent[0]
    other_tokens, other_cot = swap(own_tokens), swap(own_cot)

    group_routes = routes.reshape(-1)
    route_onehot = group_routes[:, None] == jnp.arange(experts)[None, :]
    ones = route_onehot.astype(BF16)
    row_at = jnp.arange(seq)
    earlier = (row_at[:, None] > row_at[None, :]).astype(BF16)
    order = jnp.sum(jnp.where(route_onehot, dot(earlier, ones), 0.0), axis=1).astype(jnp.int32)
    place = jnp.where(order < capacity, group_routes * capacity + order, slots)
    place_rows = place.reshape(2, own_rows)
    place_column = place.reshape(seq, 1)

    def exchange(value):
        value = value.reshape(experts, capacity, half)
        got = lax.all_to_all(value, "expert", split_axis=0, concat_axis=0, tiled=True)
        return got.reshape(slots, half)

    def give_back(mine, other):
        total = (mine.astype(F32) + swap(other).astype(F32)).astype(BF16)
        return total, exchange(total)

    got_cot = exchange(dispatch_rows(scalar, place_rows, own_cot, other_cot, slots))

    qkv, normed_low = front(scalar, own_tokens, other_tokens, ln1_gain, w_qkv)
    attended_own, lse = attend(qkv, pairs)
    hidden, inner_low = middle(
        scalar, own_tokens, other_tokens, attended_own, swap(attended_own), w_out, ln2_gain
    )

    got_rows = exchange(dispatch_rows(scalar, place_rows, inner_low, inner_low, slots))
    head = jnp.concatenate(
        [w_router, w_mix, jnp.zeros((width, LANES - experts - 2), BF16)], axis=1
    )
    head_t = head.T
    picked = (jnp.arange(LANES) == member).astype(F32)[None]

    def sources(block):
        return (order_of[:, None] * block + jnp.arange(block)[None, :]).reshape(-1, 1)

    results = branch(
        scalar, [inner_low], [own_cot, other_cot], sources(width // members), head, head_t, w_up,
        w_down, experts, parts,
    )
    dense_out, dense_dx, small_dense, probs = results[:4]
    grad_up, grad_down = results[4 : 4 + parts], results[4 + parts :]
    got_rows = after(got_rows, small_dense)
    expert_rows = [got_rows, swap(got_rows)]
    out_keep, out_send, dx_keep, dx_send, small_expert, expert_g, expert_act, expert_dpre = branch(
        scalar, expert_rows, [got_cot, swap(got_cot)], picked, head, head_t, expert_up[0],
        expert_down[0], experts, parts,
    )

    sent_dx, got_dx = give_back(dx_keep, dx_send)
    _, got_out = give_back(out_keep, after(out_send, sent_dx))
    token_dx = combine_rows(place_column, got_dx)
    results = middle_back(
        scalar, sources(half // members), dense_dx, swap(dense_dx), token_dx, swap(token_dx),
        hidden, own_cot, other_cot, attended_own, ln2_gain, w_out, parts,
    )
    hidden_grad, attended_grad, ln2_row = results[:3]
    grad_w_out = results[3:]
    dq, dk, dv = attend_back(qkv, attended_own, attended_grad, lse)

    small = small_dense + small_expert
    small = small + jnp.where(jnp.arange(LANES)[:, None] == experts + 3, ln2_row[0:1], 0.0)
    block = width // (2 * members)
    source = (
        order_of[:, None, None] * block
        + jnp.arange(2)[None, :, None] * half
        + jnp.arange(block)[None, None, :]
    ).reshape(-1, 1)
    results = tail(
        scalar, source, normed_low, ln1_gain, small, dq, dk, dv, w_qkv, parts, experts + 2
    )
    normed_grad = results[0] + swap(results[1]).astype(F32)
    _, base_one, inverse_one = layer_norm(own_tokens.astype(F32), ln1_gain)
    input_grad = lax.dynamic_slice_in_dim(hidden_grad, own_start, own_rows, 0) + norm_backward(
        normed_grad, base_one, inverse_one, ln1_gain
    )
    gate = results[0]
    grad_expert_up, grad_expert_down = expert_weights(
        scalar, *expert_rows, after(expert_g, gate), expert_act, expert_dpre
    )
    late = grad_expert_up
    grad_w_up = grid.reduce(grad_up, (sent_dx, ln2_row, late))
    grad_w_down = grid.reduce(grad_down, (sent_dx, ln2_row, late))
    grad_w_out = grid.reduce(grad_w_out, (gate, late, None))

    token_out = combine_rows(place_column, after(got_out, late)).astype(F32)
    chance = jnp.sum(jnp.where(route_onehot, probs[:, :experts], 0.0), axis=1, keepdims=True)
    scaled = chance * probs[:, experts + 1 : experts + 2] * token_out
    total_out = dense_out.astype(F32) + in_order(scaled, jnp.zeros_like(scaled), 1)
    total_out = total_out.astype(BF16)
    out_mine = lax.dynamic_slice_in_dim(total_out, own_start, own_rows, 0)
    out_other = swap(lax.dynamic_slice_in_dim(total_out, own_rows - own_start, own_rows, 0))
    hidden_own = lax.dynamic_slice_in_dim(hidden, own_start, own_rows, 0)
    mixed_out = (hidden_own + out_mine.astype(F32) + out_other.astype(F32)).astype(BF16)

    last = grid.reduce(results[2:]).reshape(2, block, -1)
    kept = lax.dynamic_index_in_dim(last, node, 0, False)
    other = swap(lax.dynamic_index_in_dim(last, 1 - node, 0, False).astype(BF16)).astype(F32)

    def columns(rows):
        rows = rows[:, : 3 * half].reshape(block, half // WIDE, 3, WIDE)
        return rows.transpose(0, 2, 1, 3).reshape(block, 3, half)

    grad_w_qkv = in_order(columns(kept), columns(other), 2).reshape(block, 3 * width)
    small = kept[:, 3 * half :] + other[:, 3 * half :]
    return (
        mixed_out.reshape(tokens.shape),
        input_grad.reshape(tokens.shape),
        small[:, experts + 2],
        grad_w_qkv,
        grad_w_out,
        small[:, experts + 3],
        small[:, :experts],
        small[:, experts : experts + 2],
        grad_w_up,
        grad_w_down,
        grad_expert_up[None],
        grad_expert_down[None],
    )


def solution(mesh):
    return jax.shard_map(
        shards,
        mesh=mesh,
        in_specs=(
            P("expert", "node", None),
            P("expert", "node", None),
            P("expert", None, None),
            P(),
            P(),
            P(),
            P(),
            P(),
            P(),
            P(None, "node"),
            P(None, "node"),
            P("expert", None, "node"),
            P("expert", "node", None),
        ),
        out_specs=(
            P("expert", "node", None),
            P("expert", "node", None),
            P(("node", "expert")),
            P(("node", "expert"), None),
            P(("node", "expert"), None),
            P(("node", "expert")),
            P(("node", "expert"), None),
            P(("node", "expert"), None),
            P("expert", "node"),
            P("expert", "node"),
            P("expert", None, "node"),
            P("expert", "node", None),
        ),
        check_vma=False,
    )
```

```python
import functools

import jax
import jax.numpy as jnp
from jax import lax
from jax.experimental import pallas as pl
from jax.experimental.pallas import tpu as pltpu
from jax.sharding import PartitionSpec as P


HEAD_DIM = 64
LIMIT = 60 << 20
EPS = 1e-05
LANES = 128
LOG2E = 1.4426950408889634
GELU_A = 0.7978845608028654
GELU_B = 0.044715
SWAP = [(0, 1), (1, 0)]
F32 = jnp.float32
BF16 = jnp.bfloat16


def dot(left, right):
    return jnp.dot(left, right, preferred_element_type=F32)


def dot_t(left, right):
    return lax.dot_general(left, right, (((1,), (1,)), ((), ())), preferred_element_type=F32)


def dot_n(left, right):
    return lax.dot_general(left, right, (((0,), (0,)), ((), ())), preferred_element_type=F32)


def layer_norm(values, gain):
    average = jnp.mean(values, axis=-1, keepdims=True)
    centered = values - average
    inverse = lax.rsqrt(jnp.mean(centered * centered, axis=-1, keepdims=True) + EPS)
    normed = centered * inverse
    return (normed * gain, normed, inverse)


def norm_backward(upstream, normed, inverse, gain):
    scaled = upstream * gain
    inner_term = (
        scaled
        - jnp.mean(scaled, axis=-1, keepdims=True)
        - normed * jnp.mean(scaled * normed, axis=-1, keepdims=True)
    )
    return inner_term * inverse


def spec(shape, index):
    return pl.BlockSpec(shape, index)


def fixed(shape):
    return pl.BlockSpec(shape, lambda *_: (0,) * len(shape), pipeline_mode=pl.Buffered(1))


def struct(shape, kind):
    return jax.ShapeDtypeStruct(shape, kind)


def chunks(count, size, step):
    def run(index, carry):
        step(pl.ds(pl.multiple_of(index * size, size), size))
        return carry

    lax.fori_loop(0, count // size, run, 0)


def after(value, *others):
    return lax.optimization_barrier((value, others))[0]


def row_pick(node, index, own, other):
    return jnp.where(index == node, own, other)


def permutation(order_ref, start, count, block, columns, copies=1):
    lane = lax.broadcasted_iota(jnp.int32, (block, columns), 1)
    row = lax.broadcasted_iota(jnp.int32, (block, columns), 0)
    pieces = []
    for index in range(count // block):
        place = start // block + index
        first = order_ref[place // copies] * block + (place % copies) * (columns // copies)
        pieces.append((row + first == lane).astype(F32))
    return jnp.concatenate(pieces, axis=0).astype(BF16)


def front_kernel(node_ref, own_ref, other_ref, gain_ref, w_ref, qkv_ref, normed_ref):
    rows = own_ref.shape[0]
    node = node_ref[0]

    @pl.when(pl.program_id(0) == 0)
    def _():
        for place, part in ((node, own_ref), (1 - node, other_ref)):
            def norm(at):
                normed, _, _ = layer_norm(part[at, :].astype(F32), gain_ref[...])
                start = pl.multiple_of(place * rows + at.start, 128)
                normed_ref[pl.ds(start, 128), :] = normed.astype(BF16)

            chunks(rows, 128, norm)

    def project(at):
        qkv_ref[at, :] = dot(normed_ref[at, :], w_ref[...]).astype(BF16)

    chunks(2 * rows, 512, project)


def front(node, own, other, gain, w_qkv):
    rows, width = own.shape
    half = width // 2
    return pl.pallas_call(
        front_kernel,
        grid_spec=pltpu.PrefetchScalarGridSpec(
            num_scalar_prefetch=1,
            grid=(3,),
            in_specs=[
                fixed(own.shape),
                fixed(own.shape),
                fixed((1, width)),
                spec((width, half), lambda i, n: (0, 2 * i + n[0])),
            ],
            out_specs=[
                spec((2 * rows, half), lambda i, n: (0, i)),
                fixed((2 * rows, width)),
            ],
        ),
        out_shape=[struct((2 * rows, 3 * half), BF16), struct((2 * rows, width), BF16)],
        cost_estimate=pl.CostEstimate(
            flops=6 * rows * width * width, bytes_accessed=14 * rows * width, transcendentals=0
        ),
        compiler_params=pltpu.CompilerParams(vmem_limit_bytes=28 << 20),
        name="front",
    )(node, own, other, gain[None], w_qkv)


QB = 256


def head_specs(seq, pairs):
    return [spec((seq, LANES), lambda j, at=at: (0, at * pairs + j)) for at in range(3)]


def attend_kernel(q_ref, k_ref, v_ref, out_ref, lse_ref, ot_ref):
    seq = q_ref.shape[0]
    factor = HEAD_DIM ** (-0.5) * LOG2E
    lane = lax.broadcasted_iota(jnp.int32, (1, LANES), 1)
    v_t = v_ref[...].T
    below = lax.broadcasted_iota(jnp.int32, (QB, QB), 0) <= lax.broadcasted_iota(
        jnp.int32, (QB, QB), 1
    )
    for head in range(2):
        keep = (lane // HEAD_DIM) == head
        keys = jnp.where(keep, k_ref[...], 0)
        v_rows = v_t[head * HEAD_DIM : (head + 1) * HEAD_DIM]
        for block in range(seq // QB):
            lo, hi = block * QB, (block + 1) * QB
            queries = q_ref[lo:hi]
            diag = jnp.where(below, dot_t(keys[lo:hi], queries), -1e30)
            top = jnp.max(diag, axis=0, keepdims=True)
            if lo:
                past = dot_t(keys[:lo], queries)
                top = jnp.maximum(top, jnp.max(past, axis=0, keepdims=True))
            p_diag = jnp.exp2((diag - top) * factor)
            total = jnp.sum(p_diag, axis=0, keepdims=True)
            acc = dot(v_rows[:, lo:hi], p_diag.astype(BF16))
            if lo:
                p_past = jnp.exp2((past - top) * factor)
                total = total + jnp.sum(p_past, axis=0, keepdims=True)
                acc = acc + dot(v_rows[:, :lo], p_past.astype(BF16))
            ot_ref[head * HEAD_DIM : (head + 1) * HEAD_DIM, lo:hi] = acc * (1.0 / total)
            lse_ref[0, head : head + 1, lo:hi] = top * factor + jnp.log2(total)
    out_ref[...] = ot_ref[...].T.astype(BF16)


def attend(qkv, pairs):
    seq = qkv.shape[0]
    return pl.pallas_call(
        attend_kernel,
        grid=(pairs,),
        in_specs=head_specs(seq, pairs),
        out_specs=[
            spec((seq, LANES), lambda j: (0, j)),
            spec((1, 8, seq), lambda j: (j, 0, 0)),
        ],
        out_shape=[struct((seq, pairs * LANES), BF16), struct((pairs, 8, seq), F32)],
        scratch_shapes=[
            pltpu.VMEM((LANES, seq), F32),
        ],
        cost_estimate=pl.CostEstimate(
            flops=pairs * 8 * seq * seq * LANES,
            bytes_accessed=pairs * seq * LANES * 8,
            transcendentals=pairs * seq * seq,
        ),
        compiler_params=pltpu.CompilerParams(vmem_limit_bytes=14 << 20),
        name="attend",
    )(qkv, qkv, qkv)


def attend_back_kernel(
    q_ref, k_ref, v_ref, out_ref, grad_ref, lse_ref, dq_ref, dk_ref, dv_ref, dqt_ref, dka_ref, dva_ref
):
    seq = q_ref.shape[0]
    scale = HEAD_DIM ** (-0.5)
    factor = scale * LOG2E
    lane = lax.broadcasted_iota(jnp.int32, (1, LANES), 1)
    k_t = k_ref[...].T
    product = (grad_ref[...].astype(F32) * out_ref[...].astype(F32)).T
    below = lax.broadcasted_iota(jnp.int32, (QB, QB), 0) <= lax.broadcasted_iota(
        jnp.int32, (QB, QB), 1
    )
    dka_ref[...] = jnp.zeros_like(dka_ref)
    dva_ref[...] = jnp.zeros_like(dva_ref)
    for head in range(2):
        keep = (lane // HEAD_DIM) == head
        rows = slice(head * HEAD_DIM, (head + 1) * HEAD_DIM)
        keys = jnp.where(keep, k_ref[...], 0)
        values = jnp.where(keep, v_ref[...], 0)
        delta = jnp.sum(product[rows], axis=0, keepdims=True)
        for block in range(seq // QB):
            lo, hi = block * QB, (block + 1) * QB
            queries = jnp.where(keep, q_ref[lo:hi], 0)
            grads = jnp.where(keep, grad_ref[lo:hi], 0)
            lse = lse_ref[0, head : head + 1, lo:hi]
            drop = delta[:, lo:hi]
            acc = None
            for start, stop in ((lo, hi), (0, lo)):
                if start == stop:
                    continue
                probs = jnp.exp2(dot_t(keys[start:stop], queries) * factor - lse)
                if start == lo:
                    probs = jnp.where(below, probs, 0.0)
                prob_grad = dot_t(values[start:stop], grads)
                score_grad = (probs * (prob_grad - drop)).astype(BF16)
                dva_ref[start:stop] += dot(probs.astype(BF16), grads)
                dka_ref[start:stop] += dot(score_grad, queries)
                part = dot(k_t[rows, start:stop], score_grad)
                acc = part if acc is None else acc + part
            dqt_ref[rows, lo:hi] = acc
    dq_ref[...] = (dqt_ref[...].T * scale).astype(BF16)
    dk_ref[...] = (dka_ref[...] * scale).astype(BF16)
    dv_ref[...] = dva_ref[...].astype(BF16)


def attend_back(qkv, attended, grad, lse):
    seq = qkv.shape[0]
    pairs = lse.shape[0]
    one = spec((seq, LANES), lambda j: (0, j))
    return pl.pallas_call(
        attend_back_kernel,
        grid=(pairs,),
        in_specs=head_specs(seq, pairs) + [one, one, spec((1, 8, seq), lambda j: (j, 0, 0))],
        out_specs=[one] * 3,
        out_shape=[struct(attended.shape, BF16)] * 3,
        scratch_shapes=[
            pltpu.VMEM((LANES, seq), F32),
            pltpu.VMEM((seq, LANES), F32),
            pltpu.VMEM((seq, LANES), F32),
        ],
        cost_estimate=pl.CostEstimate(
            flops=pairs * 20 * seq * seq * LANES,
            bytes_accessed=pairs * seq * LANES * 16,
            transcendentals=pairs * seq * seq,
        ),
        compiler_params=pltpu.CompilerParams(vmem_limit_bytes=20 << 20),
        name="attend_back",
    )(qkv, qkv, qkv, attended, grad, lse)


def middle_kernel(
    node_ref, tok_ref, tok_other_ref, own_ref, other_ref, w_ref, gain_ref, hidden_ref, normed_ref
):
    half = own_ref.shape[1]
    node = node_ref[0]
    index = pl.program_id(0) // (pl.num_programs(0) // 2)
    tok = row_pick(node, index, tok_ref[...], tok_other_ref[...])
    mine = pl.ds(pl.multiple_of(node * half, half), half)
    theirs = pl.ds(pl.multiple_of((1 - node) * half, half), half)
    hidden = tok.astype(F32) + (
        dot(own_ref[...], w_ref[mine, :]) + dot(other_ref[...], w_ref[theirs, :])
    )
    normed, _, _ = layer_norm(hidden, gain_ref[...])
    hidden_ref[...] = hidden
    normed_ref[...] = normed.astype(BF16)


def middle(node, tokens, tokens_other, own, other, w_out, gain):
    width = tokens.shape[1]
    seq = 2 * tokens.shape[0]
    rows = 256
    steps = seq // rows
    half_row = spec((rows, width), lambda i, n: (i % (steps // 2), 0))
    row = lambda columns: spec((rows, columns), lambda i, n: (i, 0))
    return pl.pallas_call(
        middle_kernel,
        grid_spec=pltpu.PrefetchScalarGridSpec(
            num_scalar_prefetch=1,
            grid=(seq // rows,),
            in_specs=[
                half_row,
                half_row,
                row(width // 2),
                row(width // 2),
                fixed(w_out.shape),
                fixed((1, width)),
            ],
            out_specs=[row(width), row(width)],
        ),
        out_shape=[struct((seq, width), F32), struct((seq, width), BF16)],
        cost_estimate=pl.CostEstimate(
            flops=2 * seq * width * width, bytes_accessed=12 * seq * width, transcendentals=0
        ),
        compiler_params=pltpu.CompilerParams(vmem_limit_bytes=20 << 20),
        name="middle",
    )(node, tokens, tokens_other, own, other, w_out, gain[None])


def middle_back_kernel(
    parts,
    block,
    node_ref,
    order_ref,
    dense_ref,
    dense_other_ref,
    token_ref,
    token_other_ref,
    hidden_ref,
    cot_ref,
    cot_other_ref,
    attended_ref,
    gain_ref,
    w_ref,
    grad_ref,
    attended_grad_ref,
    ln_ref,
    *refs,
):
    weight_refs = refs[:parts]
    inner_ref, acc_ref = refs[parts:]
    half = token_ref.shape[1]
    node = node_ref[0]
    step = pl.program_id(0)

    @pl.when(step == 0)
    def _():
        ln_ref[...] = jnp.zeros_like(ln_ref)
        acc_ref[...] = jnp.zeros_like(acc_ref)

    inner_ref[...] = dense_ref[...].astype(F32) + dense_other_ref[...].astype(F32)
    inner_ref[:, pl.ds(pl.multiple_of(node * half, half), half)] += token_ref[...].astype(F32)
    inner_ref[:, pl.ds(pl.multiple_of((1 - node) * half, half), half)] += token_other_ref[
        ...
    ].astype(F32)
    inner = inner_ref[...]
    gain = gain_ref[...]
    _, base, inverse = layer_norm(hidden_ref[...], gain)
    ln_ref[0:1, :] += 0.5 * jnp.sum(inner * base, axis=0, keepdims=True)
    index = step // (pl.num_programs(0) // 2)
    cot = row_pick(node, index, cot_ref[...], cot_other_ref[...])
    hidden_grad = cot.astype(F32) + norm_backward(inner, base, inverse, gain)
    grad_ref[...] = hidden_grad
    low = hidden_grad.astype(BF16)
    attended_grad_ref[...] = dot_t(low, w_ref[...]).astype(BF16)
    turn = permutation(order_ref, 0, half, block, half)
    turned = dot_t(turn, attended_ref[...]).astype(BF16)
    acc_ref[...] += dot(turned, low)

    @pl.when(step == pl.num_programs(0) - 1)
    def _():
        size = half // parts
        for part in range(parts):
            weight_refs[part][...] = acc_ref[part * size : (part + 1) * size].astype(BF16)


def middle_back(
    node, order, dense, dense_other, token, token_other, hidden, cot, cot_other, attended, gain, w_out, parts
):
    seq, width = hidden.shape
    half = width // 2
    rows = 256
    steps = seq // rows
    half_row = spec((rows, width), lambda i, n, o: (i % (steps // 2), 0))
    row = lambda columns: spec((rows, columns), lambda i, n, o: (i, 0))
    result = (half // parts, width)
    return pl.pallas_call(
        functools.partial(middle_back_kernel, parts, half // order.shape[0]),
        grid_spec=pltpu.PrefetchScalarGridSpec(
            num_scalar_prefetch=2,
            grid=(seq // rows,),
            in_specs=[
                row(width),
                row(width),
                row(half),
                row(half),
                row(width),
                half_row,
                half_row,
                row(half),
                fixed((1, width)),
                spec((half, width), lambda i, n, o: (n[0], 0)),
            ],
            out_specs=[row(width), row(half), fixed((8, width))] + [fixed(result)] * parts,
            scratch_shapes=[pltpu.VMEM((rows, width), F32), pltpu.VMEM((half, width), F32)],
        ),
        out_shape=[
            struct((seq, width), F32),
            struct((seq, half), BF16),
            struct((8, width), F32),
        ]
        + [struct(result, BF16)] * parts,
        cost_estimate=pl.CostEstimate(
            flops=2 * seq * width * width, bytes_accessed=18 * seq * width, transcendentals=0
        ),
        compiler_params=pltpu.CompilerParams(vmem_limit_bytes=28 << 20),
        name="middle_back",
    )(
        node, order, dense, dense_other, token, token_other, hidden, cot, cot_other, attended,
        gain[None], w_out,
    )


def dispatch_kernel(node_ref, place_ref, own_ref, other_ref, sent_ref):
    size = sent_ref.shape[0]
    node = node_ref[0]
    slot = pl.program_id(0) * size + lax.broadcasted_iota(jnp.int32, (size, 1), 0)
    total = None
    for at, ref in ((node, own_ref), (1 - node, other_ref)):
        place = place_ref[pl.ds(at, 1), :]
        part = dot((place == slot).astype(F32).astype(BF16), ref[...])
        total = part if total is None else total + part
    sent_ref[...] = total.astype(BF16)


def dispatch_rows(node, place, own, other, slots):
    rows = place.shape[1]
    half = own.shape[1] // 2
    size = 256
    if own.shape[0] == rows:
        first = spec((rows, half), lambda i, n: (0, n[0]))
        second = first
    else:
        first = spec((rows, half), lambda i, n: (n[0], n[0]))
        second = spec((rows, half), lambda i, n: (1 - n[0], n[0]))
    return pl.pallas_call(
        dispatch_kernel,
        grid_spec=pltpu.PrefetchScalarGridSpec(
            num_scalar_prefetch=1,
            grid=(slots // size,),
            in_specs=[fixed(place.shape), first, second],
            out_specs=spec((size, half), lambda i, n: (i, 0)),
        ),
        out_shape=struct((slots, half), BF16),
        cost_estimate=pl.CostEstimate(
            flops=4 * slots * rows * half, bytes_accessed=4 * slots * half, transcendentals=0
        ),
        compiler_params=pltpu.CompilerParams(vmem_limit_bytes=14 << 20),
        name="dispatch",
    )(node, place, own, other)


def combine_kernel(place_ref, got_ref, out_ref):
    size = place_ref.shape[0]
    slot = lax.broadcasted_iota(jnp.int32, (size, got_ref.shape[0]), 1)
    onehot = (place_ref[...] == slot).astype(F32).astype(BF16)
    out_ref[...] = dot(onehot, got_ref[...]).astype(BF16)


def combine_rows(place, got):
    rows = place.shape[0]
    size = 256
    return pl.pallas_call(
        combine_kernel,
        grid=(rows // size,),
        in_specs=[spec((size, 1), lambda i: (i, 0)), fixed(got.shape)],
        out_specs=spec((size, got.shape[1]), lambda i: (i, 0)),
        out_shape=struct((rows, got.shape[1]), BF16),
        cost_estimate=pl.CostEstimate(
            flops=2 * rows * got.shape[0] * got.shape[1],
            bytes_accessed=4 * rows * got.shape[1],
            transcendentals=0,
        ),
        compiler_params=pltpu.CompilerParams(vmem_limit_bytes=12 << 20),
        name="combine",
    )(place, got)


def branch_kernel(dense, experts, parts, unit, node_ref, order_ref, *refs):
    if dense:
        x_refs, c_refs, refs = refs[:1], refs[1:3], refs[3:]
    else:
        x_refs, c_refs, refs = refs[:2], refs[2:4], refs[4:]
    side_ref, wct_ref, up_ref, dn_ref = refs[:4]
    refs = refs[4:]
    if dense:
        out_refs, dx_refs, gsm_ref, probs_ref = refs[:1], refs[1:2], refs[2], refs[3]
        grad_refs = refs[4 : 4 + parts]
        xt_ref, g_ref, a_ref, acc_ref, dxa_ref, act_ref, dpre_ref, gt_ref = refs[4 + parts :]
    else:
        out_refs, dx_refs, gsm_ref = refs[:2], refs[2:4], refs[4]
        g_ref, act_ref, dpre_ref, a_ref, acc_ref, dxa_ref = refs[5:]
    halves = len(x_refs)
    rows, half = x_refs[0].shape
    width = halves * half
    step = pl.program_id(0)
    small = 256
    big = 512
    node = node_ref[0]
    if dense:
        split = [slice(0, width)]
    else:
        split = [
            pl.ds(pl.multiple_of(node * half, half), half),
            pl.ds(pl.multiple_of((1 - node) * half, half), half),
        ]

    @pl.when(step == 0)
    def _():
        lane = lax.broadcasted_iota(jnp.int32, (1, LANES), 1)
        is_router = lane < experts
        is_mix = (lane >= experts) & (lane < experts + 2)
        first = (lane == experts).astype(F32)
        second = (lane == experts + 1).astype(F32)
        picked = side_ref[...]

        def prepare(at):
            logits = sum(dot_t(x_refs[n][at, :], wct_ref[:, split[n]]) for n in range(halves))

            def soft(mask):
                masked = jnp.where(mask, logits, -1e30)
                shifted = jnp.exp(masked - jnp.max(masked, axis=1, keepdims=True))
                return shifted / jnp.sum(shifted, axis=1, keepdims=True)

            mix = soft(is_mix)
            if dense:
                factor = jnp.sum(mix * first, axis=1, keepdims=True)
                probs_ref[at, :] = jnp.where(is_router, soft(is_router), mix)
                a_ref[at, :] = jnp.where(is_mix, first - mix, 0.0)
            else:
                router = soft(is_router)
                gate = jnp.sum(router * picked, axis=1, keepdims=True)
                factor = gate * jnp.sum(mix * second, axis=1, keepdims=True)
                a_ref[at, :] = jnp.where(
                    is_router, picked - router, jnp.where(is_mix, second - mix, 0.0)
                )
            if dense:
                own = c_refs[0].shape[0]
                place = at.start // own
                inside = pl.ds(pl.multiple_of(at.start - place * own, small), small)
                cot = row_pick(node, place, c_refs[0][inside, :], c_refs[1][inside, :])
                scaled = (factor * cot.astype(F32)).astype(BF16)
                g_ref[at, :] = scaled
            else:
                for n in range(halves):
                    g_ref[at, split[n]] = (factor * c_refs[n][at, :].astype(F32)).astype(BF16)
            acc_ref[at, :] = jnp.zeros((small, width), F32)
            dxa_ref[at, :] = jnp.zeros((small, width), F32)

        chunks(rows, small, prepare)
        if dense:

            def transpose(at):
                turn = permutation(order_ref, at.start, small, unit, width)
                for index in range(rows // big):
                    some = slice(index * big, (index + 1) * big)
                    xt_ref[at, some] = dot_t(turn, x_refs[0][some, :]).astype(BF16)
                    gt_ref[at, some] = dot_t(turn, g_ref[some, :]).astype(BF16)

            chunks(width, small, transpose)

    def forward(at):
        pre = sum(dot(x_refs[n][at, :], up_ref[split[n], :]) for n in range(halves))
        square = pre * pre
        bend = jnp.tanh(pre * (GELU_A + GELU_A * GELU_B * square))
        side = 0.5 * (1.0 + bend)
        act = (pre * side).astype(BF16)
        slope = side + 0.5 * pre * (1.0 - bend * bend) * (GELU_A + 3.0 * GELU_A * GELU_B * square)
        act_ref[at, :] = act
        if dense:
            act_grad = dot(g_ref[at, :], dn_ref[...])
            acc_ref[at, :] += dot_t(act, dn_ref[...])
        else:
            act_grad = dot_t(g_ref[at, :], dn_ref[...])
            acc_ref[at, :] += dot(act, dn_ref[...])
        pre_grad = (slope * act_grad).astype(BF16)
        dpre_ref[at, :] = pre_grad
        dxa_ref[at, :] += dot_t(pre_grad, up_ref[...])

    chunks(rows, big, forward)
    if dense:
        size = width // parts
        for part in range(parts):

            def weights(at):
                rows_at = pl.ds(pl.multiple_of(part * size + at.start, small), small)
                pair = (
                    dot(xt_ref[rows_at, :], dpre_ref[...]).astype(BF16),
                    dot(gt_ref[rows_at, :], act_ref[...]).astype(BF16),
                )
                for index in range(2 * small // unit):
                    to = pl.multiple_of(2 * at.start + index * unit, unit)
                    place = index // 2 * unit
                    grad_refs[part][pl.ds(to, unit), :] = pair[index % 2][place : place + unit]

            chunks(size, small, weights)

    @pl.when(step == pl.num_programs(0) - 1)
    def _():
        gsm_ref[...] = jnp.zeros_like(gsm_ref)

        def finish(at):
            out = acc_ref[at, :]
            strength = jnp.sum(g_ref[at, :].astype(F32) * out, axis=1, keepdims=True)
            logit_grad = strength * a_ref[at, :]
            low = logit_grad.astype(BF16)
            turned = logit_grad.T.astype(BF16)
            for n in range(halves):
                gsm_ref[:, split[n]] += dot(turned, x_refs[n][at, :])
                part = acc_ref[at, split[n]]
                if dense:
                    mixes = probs_ref[at, :]
                    lane = lax.broadcasted_iota(jnp.int32, (1, LANES), 1)
                    part = part * jnp.sum(
                        jnp.where(lane == experts, mixes, 0.0), axis=1, keepdims=True
                    )
                out_refs[n][at, :] = part.astype(BF16)
                dx_refs[n][at, :] = (dxa_ref[at, split[n]] + dot(low, wct_ref[:, split[n]])).astype(
                    BF16
                )

        chunks(rows, small, finish)


def branch(node, order, xs, cs, side, head_t, up, down, experts, parts):
    dense = len(xs) == 1
    rows, half = xs[0].shape
    width = len(xs) * half
    hidden = up.shape[1]
    block = 512
    column = lambda size: spec((size, block), lambda f, n, o: (0, f))
    up_spec = column(width)
    down_spec = up_spec if dense else spec((block, width), lambda f, n, o: (f, 0))
    outs = [(fixed((rows, half)), struct((rows, half), BF16))] * (2 * len(xs))
    outs = outs + [(fixed((LANES, width)), struct((LANES, width), F32))]
    sums = [
        pltpu.VMEM((rows, LANES), F32),
        pltpu.VMEM((rows, width), F32),
        pltpu.VMEM((rows, width), F32),
    ]
    if dense:
        outs = outs + [(fixed((rows, LANES)), struct((rows, LANES), F32))]
        size = 2 * width // parts
        outs = outs + [(column(size), struct((size, hidden), BF16))] * parts
        scratch = [
            pltpu.VMEM((width, rows), BF16),
            pltpu.VMEM((rows, width), BF16),
            *sums,
            pltpu.VMEM((rows, block), BF16),
            pltpu.VMEM((rows, block), BF16),
            pltpu.VMEM((width, rows), BF16),
        ]
    else:
        outs = outs + [(fixed((rows, width)), struct((rows, width), BF16))]
        outs = outs + [(column(rows), struct((rows, hidden), BF16))] * 2
        scratch = sums
    return pl.pallas_call(
        functools.partial(branch_kernel, dense, experts, parts, width // order.shape[0]),
        grid_spec=pltpu.PrefetchScalarGridSpec(
            num_scalar_prefetch=2,
            grid=(hidden // block,),
            in_specs=[fixed(one.shape) for one in [*xs, *cs]]
            + [
                fixed(side.shape),
                fixed((LANES, width)),
                up_spec,
                down_spec,
            ],
            out_specs=[one for one, _ in outs],
            scratch_shapes=scratch,
        ),
        out_shape=[shape for _, shape in outs],
        cost_estimate=pl.CostEstimate(
            flops=(12 if dense else 8) * rows * width * hidden,
            bytes_accessed=12 * width * hidden + 8 * rows * width,
            transcendentals=rows * hidden,
        ),
        compiler_params=pltpu.CompilerParams(vmem_limit_bytes=LIMIT),
        name="dense_branch" if dense else "expert_branch",
    )(node, order, *xs, *cs, side, head_t, up, down)


def expert_up_kernel(node_ref, own_ref, other_ref, dpre_ref, grad_ref, xt_ref):
    rows, half = own_ref.shape
    node = node_ref[0]

    @pl.when(pl.program_id(0) == 0)
    def _():
        for at, ref in ((node, own_ref), (1 - node, other_ref)):
            place = pl.ds(pl.multiple_of(at * half, half), half)

            def turn(rows_at):
                xt_ref[place, rows_at] = ref[rows_at, :].T

            chunks(rows, 256, turn)

    def weights(at):
        grad_ref[at, :] = dot(xt_ref[at, :], dpre_ref[...])

    chunks(2 * half, 256, weights)


def expert_down_kernel(act_ref, g_ref, grad_ref):
    grad_ref[...] = dot_n(act_ref[...], g_ref[...])


def expert_up_grad(node, own, other, dpre):
    rows, half = own.shape
    hidden = dpre.shape[1]
    block = 512
    return pl.pallas_call(
        expert_up_kernel,
        grid_spec=pltpu.PrefetchScalarGridSpec(
            num_scalar_prefetch=1,
            grid=(hidden // block,),
            in_specs=[
                fixed(own.shape),
                fixed(own.shape),
                spec((rows, block), lambda f, n: (0, f)),
            ],
            out_specs=spec((2 * half, block), lambda f, n: (0, f)),
            scratch_shapes=[pltpu.VMEM((2 * half, rows), BF16)],
        ),
        out_shape=struct((2 * half, hidden), F32),
        cost_estimate=pl.CostEstimate(
            flops=4 * rows * half * hidden,
            bytes_accessed=8 * half * hidden + 2 * rows * hidden,
            transcendentals=0,
        ),
        compiler_params=pltpu.CompilerParams(vmem_limit_bytes=36 << 20),
        name="expert_up_grad",
    )(node, own, other, dpre)


def expert_down_grad(act, g):
    rows, hidden = act.shape
    width = g.shape[1]
    block = 256
    return pl.pallas_call(
        expert_down_kernel,
        grid=(hidden // block,),
        in_specs=[spec((rows, block), lambda f: (0, f)), fixed(g.shape)],
        out_specs=spec((block, width), lambda f: (f, 0)),
        out_shape=struct((hidden, width), F32),
        cost_estimate=pl.CostEstimate(
            flops=2 * rows * width * hidden,
            bytes_accessed=4 * width * hidden + 2 * rows * hidden,
            transcendentals=0,
        ),
        compiler_params=pltpu.CompilerParams(vmem_limit_bytes=28 << 20),
        name="expert_down_grad",
    )(act, g)


def tail_kernel(
    parts,
    ln_lane,
    block,
    node_ref,
    order_ref,
    x_ref,
    gain_ref,
    small_ref,
    dq_ref,
    dk_ref,
    dv_ref,
    w_ref,
    keep_ref,
    send_ref,
    *refs,
):
    part_refs = refs[:parts]
    xt_ref, acc_ref = refs[parts:]
    seq, width = x_ref.shape
    size = width // parts
    own = keep_ref.shape[0]
    step = pl.program_id(0)
    last = pl.num_programs(0) - 1

    @pl.when(step == 0)
    def _():
        def prepare(at):
            turn = permutation(order_ref, at.start, 256, block, width, 2)
            for index in range(seq // 512):
                some = slice(index * 512, (index + 1) * 512)
                xt_ref[at, some] = dot_t(turn, x_ref[some, :]).astype(BF16)

        chunks(width, 256, prepare)

    for which, ref in enumerate((dq_ref, dk_ref, dv_ref)):

        @pl.when(step == which)
        def _():
            for part in range(parts):

                def weights(at):
                    rows_at = pl.ds(pl.multiple_of(part * size + at.start, 256), 256)
                    part_refs[part][at, :] = dot(xt_ref[rows_at, :], ref[...]).astype(BF16)

                chunks(size, 256, weights)

            def back(at):
                piece = dot_t(ref[at, :], w_ref[...])
                acc_ref[at, :] = acc_ref[at, :] + piece if which else piece

            chunks(seq, 256, back)

    @pl.when(step == last)
    def _():
        gain = gain_ref[...]
        node = node_ref[0]

        def column_sum(index, total):
            rows = pl.ds(pl.multiple_of(index * 256, 256), 256)
            return total + jnp.sum(
                acc_ref[rows, :] * x_ref[rows, :].astype(F32), axis=0, keepdims=True
            )

        total = lax.fori_loop(0, seq // 256, column_sum, jnp.zeros((1, width), F32)) / gain
        row = lax.broadcasted_iota(jnp.int32, (LANES, 1), 0)
        small = (small_ref[...] + jnp.where(row == ln_lane, total, 0.0)).astype(BF16)
        for part in range(parts):

            def turn(at):
                rows = permutation(order_ref, part * size + at.start, 256, block, width, 2)
                part_refs[part][at, 0:LANES] = dot_t(rows, small).astype(BF16)

            chunks(size, 256, turn)
        keep_ref[...] = acc_ref[pl.ds(pl.multiple_of(node * own, own), own), :]
        send_ref[...] = acc_ref[pl.ds(pl.multiple_of((1 - node) * own, own), own), :].astype(BF16)


def tail(node, order, normed, gain, small, dq, dk, dv, w_qkv, parts, ln_lane):
    seq, width = normed.shape
    half = width // 2
    steps = 3
    part = (width // parts, half)
    return pl.pallas_call(
        functools.partial(tail_kernel, parts, ln_lane, half // order.shape[0]),
        grid_spec=pltpu.PrefetchScalarGridSpec(
            num_scalar_prefetch=2,
            grid=(steps + 1,),
            in_specs=[
                fixed(normed.shape),
                fixed((1, width)),
                fixed((LANES, width)),
                fixed((seq, half)),
                fixed((seq, half)),
                fixed((seq, half)),
                spec((width, half), lambda i, n, o: (0, 2 * jnp.minimum(i, steps - 1) + n[0])),
            ],
            out_specs=[fixed((seq // 2, width)), fixed((seq // 2, width))]
            + [spec(part, lambda i, n, o: (0, i))] * parts,
            scratch_shapes=[pltpu.VMEM((width, seq), BF16), pltpu.VMEM((seq, width), F32)],
        ),
        out_shape=[struct((seq // 2, width), F32), struct((seq // 2, width), BF16)]
        + [struct((width // parts, steps * half + LANES), BF16)] * parts,
        cost_estimate=pl.CostEstimate(
            flops=6 * seq * width * width, bytes_accessed=16 * seq * width, transcendentals=0
        ),
        compiler_params=pltpu.CompilerParams(vmem_limit_bytes=32 << 20),
        name="tail",
    )(node, order, normed, gain[None], small, dq, dk, dv, w_qkv)


class Grid:

    def __init__(self, members):
        self.third = 4 if members % 4 == 0 else 1
        self.first = round((members // self.third) ** 0.5)
        assert self.third * self.first * self.first == members
        self.members = members
        self.sizes = (self.first, self.first, self.third)

    def digits(self, node, member):
        low, high = member % self.first, (member // self.first) % self.first
        top = member // (self.first * self.first)
        return (low, high, top) if node == 0 else (high, low, top)

    def index(self, node, digits):
        low, high = (digits[0], digits[1]) if node == 0 else (digits[1], digits[0])
        return (digits[2] * self.first + high) * self.first + low

    def shift(self, stage, by):
        pairs = []
        for node in range(2):
            for member in range(self.members):
                digits = list(self.digits(node, member))
                digits[stage] = (digits[stage] + by) % self.sizes[stage]
                target = self.index(node, digits)
                pairs.append((node * self.members + member, node * self.members + target))
        return pairs

    def order(self, node, member):
        tables = []
        for one in range(2):
            table = []
            for own in range(self.members):
                base = self.digits(one, own)
                row = []
                for place in range(self.members):
                    steps = (
                        place // (self.first * self.third),
                        (place // self.third) % self.first,
                        place % self.third,
                    )
                    row.append(
                        self.index(one, [(b + s) % k for b, s, k in zip(base, steps, self.sizes)])
                    )
                table.append(row)
            tables.append(table)
        return jnp.array(tables, jnp.int32)[node, member]

    def send(self, parts, stage):
        return [
            lax.ppermute(parts[by], ("node", "expert"), self.shift(stage, by))
            for by in range(1, self.sizes[stage])
        ]

    def add(self, parts, came, stage, *gates):
        if gates:
            came = [after(other, *gates) for other in came]
        pieces = self.sizes[stage + 1] if stage < 2 else 1
        rows = parts[0].shape[0] // pieces
        sums = []
        for piece in range(pieces):
            at = slice(piece * rows, (piece + 1) * rows)
            total = parts[0][at].astype(F32)
            for other in came:
                total = total + other[at].astype(F32)
            sums.append(total.astype(BF16) if stage < 2 else total)
        return sums


def shards(
    tokens,
    cotangent,
    routes,
    ln1_gain,
    w_qkv,
    w_out,
    ln2_gain,
    w_router,
    w_mix,
    w_up,
    w_down,
    expert_up,
    expert_down,
):
    node = lax.axis_index("node")
    member = lax.axis_index("expert")
    members = lax.axis_size("expert")
    width = tokens.shape[2]
    half = width // 2
    own_rows = tokens.shape[1]
    seq = 2 * own_rows
    experts = w_router.shape[1]
    capacity = 3 * seq // (2 * experts)
    slots = experts * capacity
    pairs = half // LANES
    own_start = node * own_rows
    scalar = node.astype(jnp.int32).reshape(1)
    grid = Grid(members)
    parts = grid.sizes[0]
    order_of = grid.order(node, member)

    def swap(value):
        return lax.ppermute(value, "node", SWAP)

    def in_order(mine, other, axis):
        return jnp.where(
            node == 0,
            jnp.concatenate([mine, other], axis=axis),
            jnp.concatenate([other, mine], axis=axis),
        )

    own_tokens, own_cot = tokens[0], cotangent[0]
    other_tokens, other_cot = swap(own_tokens), swap(own_cot)

    group_routes = routes.reshape(-1)
    route_onehot = group_routes[:, None] == jnp.arange(experts)[None, :]
    ones = route_onehot.astype(BF16)
    row_at = jnp.arange(seq)
    earlier = (row_at[:, None] > row_at[None, :]).astype(BF16)
    order = jnp.sum(jnp.where(route_onehot, dot(earlier, ones), 0.0), axis=1).astype(jnp.int32)
    place = jnp.where(order < capacity, group_routes * capacity + order, slots)
    place_rows = place.reshape(2, own_rows)
    place_column = place.reshape(seq, 1)

    def exchange(value):
        value = value.reshape(experts, capacity, half)
        got = lax.all_to_all(value, "expert", split_axis=0, concat_axis=0, tiled=True)
        return got.reshape(slots, half)

    def give_back(mine, other):
        total = (mine.astype(F32) + swap(other).astype(F32)).astype(BF16)
        return total, exchange(total)

    got_cot = exchange(dispatch_rows(scalar, place_rows, own_cot, other_cot, slots))

    qkv, normed_low = front(scalar, own_tokens, other_tokens, ln1_gain, w_qkv)
    attended_own, lse = attend(qkv, pairs)
    hidden, inner_low = middle(
        scalar, own_tokens, other_tokens, attended_own, swap(attended_own), w_out, ln2_gain
    )

    got_rows = exchange(dispatch_rows(scalar, place_rows, inner_low, inner_low, slots))
    head_t = jnp.concatenate(
        [w_router, w_mix, jnp.zeros((width, LANES - experts - 2), BF16)], axis=1
    ).T
    picked = (jnp.arange(LANES) == member).astype(F32)[None]
    results = branch(
        scalar, order_of, [inner_low], [own_cot, other_cot], picked, head_t, w_up, w_down,
        experts, parts,
    )
    dense_out, dense_dx, small_dense, probs = results[:4]
    pair0 = results[4:]
    came = grid.send(pair0, 0)
    got_rows = after(got_rows, small_dense)
    expert_rows = [got_rows, swap(got_rows)]
    out_keep, out_send, dx_keep, dx_send, small_expert, expert_g, expert_act, expert_dpre = branch(
        scalar, order_of, expert_rows, [got_cot, swap(got_cot)], picked, head_t, expert_up[0],
        expert_down[0], experts, parts,
    )

    sent_dx, got_dx = give_back(dx_keep, dx_send)
    pair1 = grid.add(pair0, came, 0, sent_dx)
    came = grid.send(pair1, 1)
    _, got_out = give_back(out_keep, after(out_send, sent_dx))
    grad_expert_down = expert_down_grad(expert_act, after(expert_g, sent_dx))
    token_dx = combine_rows(place_column, after(got_dx, pair1, grad_expert_down))
    results = middle_back(
        scalar, order_of, dense_dx, swap(dense_dx), token_dx, swap(token_dx), hidden, own_cot,
        other_cot, attended_own, ln2_gain, w_out, parts,
    )
    hidden_grad, attended_grad, ln2_row = results[:3]
    out0 = results[3:]
    out_came = grid.send(out0, 0)
    pair2 = grid.add(pair1, came, 1, ln2_row)
    came = grid.send(pair2, 2)
    dq, dk, dv = attend_back(qkv, attended_own, attended_grad, lse)

    small = small_dense + small_expert
    small = small + jnp.where(jnp.arange(LANES)[:, None] == experts + 3, ln2_row[0:1], 0.0)
    results = tail(
        scalar, order_of, normed_low, ln1_gain, small, dq, dk, dv, w_qkv, parts, experts + 2
    )
    grad_keep, grad_send, last0 = results[0], results[1], results[2:]
    last_came = grid.send(last0, 0)
    out1 = grid.add(out0, out_came, 0, grad_keep)
    out_came = grid.send(out1, 1)
    grad_expert_up = expert_up_grad(scalar, *expert_rows, after(expert_dpre, grad_keep))

    token_out = combine_rows(place_column, after(got_out, grad_expert_up)).astype(F32)
    chance = jnp.sum(jnp.where(route_onehot, probs[:, :experts], 0.0), axis=1, keepdims=True)
    scaled = chance * probs[:, experts + 1 : experts + 2] * token_out
    total_out = dense_out.astype(F32) + in_order(scaled, jnp.zeros_like(scaled), 1)
    total_out = total_out.astype(BF16)
    out_mine = lax.dynamic_slice_in_dim(total_out, own_start, own_rows, 0)
    out_other = swap(lax.dynamic_slice_in_dim(total_out, own_rows - own_start, own_rows, 0))
    out2 = grid.add(out1, out_came, 1, grad_expert_up)
    out_came = grid.send(out2, 2)

    last1 = grid.add(last0, last_came, 0, grad_expert_up, total_out)
    last_came = grid.send(last1, 1)

    unit = width // members
    both = grid.add(pair2, came, 2, last1)[0]
    grad_w_up, grad_w_down = both[:unit], both[unit:]
    hidden_own = lax.dynamic_slice_in_dim(hidden, own_start, own_rows, 0)
    out_other = after(out_other, last1)
    mixed_out = (hidden_own + out_mine.astype(F32) + out_other.astype(F32)).astype(BF16)
    last2 = grid.add(last1, last_came, 1, mixed_out, both)
    last_came = grid.send(last2, 2)
    grad_w_out = grid.add(out2, out_came, 2, last2)[0]
    normed_grad = grad_keep + after(swap(grad_send), last2).astype(F32)
    _, base_one, inverse_one = layer_norm(own_tokens.astype(F32), ln1_gain)
    input_grad = lax.dynamic_slice_in_dim(hidden_grad, own_start, own_rows, 0) + norm_backward(
        normed_grad, base_one, inverse_one, ln1_gain
    )
    block = width // (2 * members)
    last = grid.add(last2, last_came, 2, input_grad, grad_w_out)[0].reshape(2, block, -1)
    kept = lax.dynamic_index_in_dim(last, node, 0, False)
    other = swap(lax.dynamic_index_in_dim(last, 1 - node, 0, False).astype(BF16)).astype(F32)

    def columns(rows):
        return rows[:, : 3 * half].reshape(block, 3, half)

    grad_w_qkv = in_order(columns(kept), columns(other), 2).reshape(block, 3 * width)
    small = kept[:, 3 * half :] + other[:, 3 * half :]
    return (
        mixed_out.reshape(tokens.shape),
        input_grad.reshape(tokens.shape),
        small[:, experts + 2],
        grad_w_qkv,
        grad_w_out,
        small[:, experts + 3],
        small[:, :experts],
        small[:, experts : experts + 2],
        grad_w_up,
        grad_w_down,
        grad_expert_up[None],
        grad_expert_down[None],
    )


def solution(mesh):
    return jax.shard_map(
        shards,
        mesh=mesh,
        in_specs=(
            P("expert", "node", None),
            P("expert", "node", None),
            P("expert", None, None),
            P(),
            P(),
            P(),
            P(),
            P(),
            P(),
            P(None, "node"),
            P(None, "node"),
            P("expert", None, "node"),
            P("expert", "node", None),
        ),
        out_specs=(
            P("expert", "node", None),
            P("expert", "node", None),
            P(("node", "expert")),
            P(("node", "expert"), None),
            P(("node", "expert"), None),
            P(("node", "expert")),
            P(("node", "expert"), None),
            P(("node", "expert"), None),
            P("expert", "node"),
            P("expert", "node"),
            P("expert", None, "node"),
            P("expert", "node", None),
        ),
        check_vma=False,
    )
```

```python
import functools

import jax
import jax.numpy as jnp
from jax import lax
from jax.experimental import pallas as pl
from jax.experimental.pallas import tpu as pltpu
from jax.sharding import PartitionSpec as P


HEAD_DIM = 64
LIMIT = 60 << 20
EPS = 1e-05
LANES = 128
LOG2E = 1.4426950408889634
GELU_A = 0.7978845608028654
GELU_B = 0.044715
SWAP = [(0, 1), (1, 0)]
F32 = jnp.float32
BF16 = jnp.bfloat16


def dot(left, right):
    return jnp.dot(left, right, preferred_element_type=F32)


def dot_t(left, right):
    return lax.dot_general(left, right, (((1,), (1,)), ((), ())), preferred_element_type=F32)


def dot_n(left, right):
    return lax.dot_general(left, right, (((0,), (0,)), ((), ())), preferred_element_type=F32)


def layer_norm(values, gain):
    average = jnp.mean(values, axis=-1, keepdims=True)
    centered = values - average
    inverse = lax.rsqrt(jnp.mean(centered * centered, axis=-1, keepdims=True) + EPS)
    normed = centered * inverse
    return (normed * gain, normed, inverse)


def norm_backward(upstream, normed, inverse, gain):
    scaled = upstream * gain
    inner_term = (
        scaled
        - jnp.mean(scaled, axis=-1, keepdims=True)
        - normed * jnp.mean(scaled * normed, axis=-1, keepdims=True)
    )
    return inner_term * inverse


def spec(shape, index):
    return pl.BlockSpec(shape, index)


def fixed(shape):
    return pl.BlockSpec(shape, lambda *_: (0,) * len(shape), pipeline_mode=pl.Buffered(1))


def struct(shape, kind):
    return jax.ShapeDtypeStruct(shape, kind)


def chunks(count, size, step):
    def run(index, carry):
        step(pl.ds(pl.multiple_of(index * size, size), size))
        return carry

    lax.fori_loop(0, count // size, run, 0)


def after(value, *others):
    return lax.optimization_barrier((value, others))[0]


def row_pick(node, index, own, other):
    return jnp.where(index == node, own, other)


def permutation(order, start, count, block, columns, copies=1):
    lane = lax.broadcasted_iota(jnp.int32, (block, columns), 1)
    row = lax.broadcasted_iota(jnp.int32, (block, columns), 0)
    pieces = []
    for index in range(count // block):
        place = start // block + index
        first = order(place // copies) * block + (place % copies) * (columns // copies)
        pieces.append((row + first == lane).astype(F32))
    return jnp.concatenate(pieces, axis=0).astype(BF16)


def half_rows(shape, steps):
    return [
        spec(shape, lambda i, n, at=at: (jnp.clip(i - abs(at - n[0]) * steps, 0, steps - 1), 0))
        for at in range(2)
    ]


def front_kernel(node_ref, own_ref, other_ref, gain_ref, w_ref, qkv_ref, normed_ref):
    rows = own_ref.shape[0]
    node = node_ref[0]

    @pl.when(pl.program_id(0) == 0)
    def _():
        for place, part in ((node, own_ref), (1 - node, other_ref)):
            def norm(at):
                normed, _, _ = layer_norm(part[at, :].astype(F32), gain_ref[...])
                start = pl.multiple_of(place * rows + at.start, 128)
                normed_ref[pl.ds(start, 128), :] = normed.astype(BF16)

            chunks(rows, 128, norm)

    def project(at):
        qkv_ref[at, :] = dot(normed_ref[at, :], w_ref[...]).astype(BF16)

    chunks(2 * rows, 512, project)


def front(node, own, other, gain, w_qkv):
    rows, width = own.shape
    half = width // 2
    return pl.pallas_call(
        front_kernel,
        grid_spec=pltpu.PrefetchScalarGridSpec(
            num_scalar_prefetch=1,
            grid=(3,),
            in_specs=[
                fixed(own.shape),
                fixed(own.shape),
                fixed((1, width)),
                spec((width, half), lambda i, n: (0, 2 * i + n[0])),
            ],
            out_specs=[
                spec((2 * rows, half), lambda i, n: (0, i)),
                fixed((2 * rows, width)),
            ],
        ),
        out_shape=[struct((2 * rows, 3 * half), BF16), struct((2 * rows, width), BF16)],
        cost_estimate=pl.CostEstimate(
            flops=6 * rows * width * width, bytes_accessed=14 * rows * width, transcendentals=0
        ),
        compiler_params=pltpu.CompilerParams(vmem_limit_bytes=28 << 20),
        name="front",
    )(node, own, other, gain[None], w_qkv)


QB = 256


def head_specs(seq, pairs):
    return [spec((seq, LANES), lambda j, at=at: (0, at * pairs + j)) for at in range(3)]


def attend_kernel(q_ref, k_ref, v_ref, out_ref, lse_ref, ot_ref):
    seq = q_ref.shape[0]
    factor = HEAD_DIM ** (-0.5) * LOG2E
    lane = lax.broadcasted_iota(jnp.int32, (1, LANES), 1)
    v_t = v_ref[...].T
    below = lax.broadcasted_iota(jnp.int32, (QB, QB), 0) <= lax.broadcasted_iota(
        jnp.int32, (QB, QB), 1
    )
    for head in range(2):
        keep = (lane // HEAD_DIM) == head
        keys = jnp.where(keep, k_ref[...], 0)
        v_rows = v_t[head * HEAD_DIM : (head + 1) * HEAD_DIM]
        for block in range(seq // QB):
            lo, hi = block * QB, (block + 1) * QB
            queries = q_ref[lo:hi]
            diag = jnp.where(below, dot_t(keys[lo:hi], queries), -1e30)
            top = jnp.max(diag, axis=0, keepdims=True)
            if lo:
                past = dot_t(keys[:lo], queries)
                top = jnp.maximum(top, jnp.max(past, axis=0, keepdims=True))
            p_diag = jnp.exp2((diag - top) * factor)
            total = jnp.sum(p_diag, axis=0, keepdims=True)
            acc = dot(v_rows[:, lo:hi], p_diag.astype(BF16))
            if lo:
                p_past = jnp.exp2((past - top) * factor)
                total = total + jnp.sum(p_past, axis=0, keepdims=True)
                acc = acc + dot(v_rows[:, :lo], p_past.astype(BF16))
            ot_ref[head * HEAD_DIM : (head + 1) * HEAD_DIM, lo:hi] = acc * (1.0 / total)
            lse_ref[0, head : head + 1, lo:hi] = top * factor + jnp.log2(total)
    out_ref[...] = ot_ref[...].T.astype(BF16)


def attend(qkv, pairs):
    seq = qkv.shape[0]
    return pl.pallas_call(
        attend_kernel,
        grid=(pairs,),
        in_specs=head_specs(seq, pairs),
        out_specs=[
            spec((seq, LANES), lambda j: (0, j)),
            spec((1, 8, seq), lambda j: (j, 0, 0)),
        ],
        out_shape=[struct((seq, pairs * LANES), BF16), struct((pairs, 8, seq), F32)],
        scratch_shapes=[
            pltpu.VMEM((LANES, seq), F32),
        ],
        cost_estimate=pl.CostEstimate(
            flops=pairs * 8 * seq * seq * LANES,
            bytes_accessed=pairs * seq * LANES * 8,
            transcendentals=pairs * seq * seq,
        ),
        compiler_params=pltpu.CompilerParams(vmem_limit_bytes=14 << 20),
        name="attend",
    )(qkv, qkv, qkv)


def attend_back_kernel(
    q_ref, k_ref, v_ref, out_ref, grad_ref, lse_ref, packed_ref, dqt_ref, dka_ref, dva_ref
):
    seq = q_ref.shape[0]
    scale = HEAD_DIM ** (-0.5)
    factor = scale * LOG2E
    lane = lax.broadcasted_iota(jnp.int32, (1, LANES), 1)
    k_t = k_ref[...].T
    product = (grad_ref[...].astype(F32) * out_ref[...].astype(F32)).T
    below = lax.broadcasted_iota(jnp.int32, (QB, QB), 0) <= lax.broadcasted_iota(
        jnp.int32, (QB, QB), 1
    )
    dka_ref[...] = jnp.zeros_like(dka_ref)
    dva_ref[...] = jnp.zeros_like(dva_ref)
    for head in range(2):
        keep = (lane // HEAD_DIM) == head
        rows = slice(head * HEAD_DIM, (head + 1) * HEAD_DIM)
        keys = jnp.where(keep, k_ref[...], 0)
        values = jnp.where(keep, v_ref[...], 0)
        delta = jnp.sum(product[rows], axis=0, keepdims=True)
        for block in range(seq // QB):
            lo, hi = block * QB, (block + 1) * QB
            queries = jnp.where(keep, q_ref[lo:hi], 0)
            grads = jnp.where(keep, grad_ref[lo:hi], 0)
            lse = lse_ref[0, head : head + 1, lo:hi]
            drop = delta[:, lo:hi]
            acc = None
            for start, stop in ((lo, hi), (0, lo)):
                if start == stop:
                    continue
                probs = jnp.exp2(dot_t(keys[start:stop], queries) * factor - lse)
                if start == lo:
                    probs = jnp.where(below, probs, 0.0)
                prob_grad = dot_t(values[start:stop], grads)
                score_grad = (probs * (prob_grad - drop)).astype(BF16)
                dva_ref[start:stop] += dot(probs.astype(BF16), grads)
                dka_ref[start:stop] += dot(score_grad, queries)
                part = dot(k_t[rows, start:stop], score_grad)
                acc = part if acc is None else acc + part
            dqt_ref[rows, lo:hi] = acc
    packed_ref[0] = (dqt_ref[...].T * scale).astype(BF16)
    packed_ref[1] = (dka_ref[...] * scale).astype(BF16)
    packed_ref[2] = dva_ref[...].astype(BF16)


def attend_back(qkv, attended, grad, lse):
    seq = qkv.shape[0]
    pairs = lse.shape[0]
    one = spec((seq, LANES), lambda j: (0, j))
    return pl.pallas_call(
        attend_back_kernel,
        grid=(pairs,),
        in_specs=head_specs(seq, pairs) + [one, one, spec((1, 8, seq), lambda j: (j, 0, 0))],
        out_specs=spec((3, seq, LANES), lambda j: (0, 0, j)),
        out_shape=struct((3, *attended.shape), BF16),
        scratch_shapes=[
            pltpu.VMEM((LANES, seq), F32),
            pltpu.VMEM((seq, LANES), F32),
            pltpu.VMEM((seq, LANES), F32),
        ],
        cost_estimate=pl.CostEstimate(
            flops=pairs * 20 * seq * seq * LANES,
            bytes_accessed=pairs * seq * LANES * 16,
            transcendentals=pairs * seq * seq,
        ),
        compiler_params=pltpu.CompilerParams(vmem_limit_bytes=20 << 20),
        name="attend_back",
    )(qkv, qkv, qkv, attended, grad, lse)


def middle_kernel(
    row_steps,
    node_ref,
    tok_ref,
    tok_other_ref,
    own_ref,
    other_ref,
    w_ref,
    gain_ref,
    place_ref,
    hidden_ref,
    normed_ref,
    sent_ref,
    half_ref,
):
    rows, half = own_ref.shape
    node = node_ref[0]
    step = pl.program_id(0)
    mine = pl.ds(pl.multiple_of(node * half, half), half)
    theirs = pl.ds(pl.multiple_of((1 - node) * half, half), half)

    @pl.when(step < row_steps)
    def _():
        tok = row_pick(node, step // (row_steps // 2), tok_ref[...], tok_other_ref[...])
        hidden = tok.astype(F32) + (
            dot(own_ref[...], w_ref[mine, :]) + dot(other_ref[...], w_ref[theirs, :])
        )
        normed, _, _ = layer_norm(hidden, gain_ref[...])
        hidden_ref[...] = hidden
        normed_ref[...] = normed.astype(BF16)
        half_ref[pl.ds(pl.multiple_of(step * rows, rows), rows), :] = normed_ref[:, mine]

    @pl.when(step >= row_steps)
    def _():
        size = sent_ref.shape[0]
        first = (step - row_steps) * size
        slot = first + lax.broadcasted_iota(jnp.int32, (size, 1), 0)
        onehot = (place_ref[...] == slot).astype(F32).astype(BF16)
        sent_ref[...] = dot(onehot, half_ref[...]).astype(BF16)


def middle(node, tokens, tokens_other, own, other, w_out, gain, place, slots):
    width = tokens.shape[1]
    seq = 2 * tokens.shape[0]
    rows = 256
    size = 512
    steps = seq // rows
    mine, theirs = half_rows((rows, width), steps // 2)
    row = lambda columns: spec((rows, columns), lambda i, n: (jnp.minimum(i, steps - 1), 0))
    return pl.pallas_call(
        functools.partial(middle_kernel, steps),
        grid_spec=pltpu.PrefetchScalarGridSpec(
            num_scalar_prefetch=1,
            grid=(steps + slots // size,),
            in_specs=[
                mine,
                theirs,
                row(width // 2),
                row(width // 2),
                fixed(w_out.shape),
                fixed((1, width)),
                fixed(place.shape),
            ],
            out_specs=[
                row(width),
                row(width),
                spec((size, width // 2), lambda i, n: (jnp.maximum(i - steps, 0), 0)),
            ],
            scratch_shapes=[pltpu.VMEM((seq, width // 2), BF16)],
        ),
        out_shape=[
            struct((seq, width), F32),
            struct((seq, width), BF16),
            struct((slots, width // 2), BF16),
        ],
        cost_estimate=pl.CostEstimate(
            flops=2 * seq * width * width + seq * slots * width,
            bytes_accessed=12 * seq * width,
            transcendentals=0,
        ),
        compiler_params=pltpu.CompilerParams(vmem_limit_bytes=24 << 20),
        name="middle",
    )(node, tokens, tokens_other, own, other, w_out, gain[None], place)


def middle_back_kernel(
    parts,
    grid,
    node_ref,
    dense_ref,
    dense_other_ref,
    token_ref,
    token_other_ref,
    hidden_ref,
    cot_ref,
    cot_other_ref,
    attended_ref,
    gain_ref,
    w_ref,
    grad_ref,
    attended_grad_ref,
    ln_ref,
    *refs,
):
    weight_refs = refs[:parts]
    inner_ref, acc_ref, turn_ref = refs[parts:]
    half = token_ref.shape[1]
    node = node_ref[0]
    step = pl.program_id(0)

    @pl.when(step == 0)
    def _():
        ln_ref[...] = jnp.zeros_like(ln_ref)
        acc_ref[...] = jnp.zeros_like(acc_ref)
        order = functools.partial(grid.place, node_ref[0], node_ref[1])
        turn_ref[...] = permutation(order, 0, half, half // grid.members, half)

    inner_ref[...] = dense_ref[...].astype(F32) + dense_other_ref[...].astype(F32)
    inner_ref[:, pl.ds(pl.multiple_of(node * half, half), half)] += token_ref[...].astype(F32)
    inner_ref[:, pl.ds(pl.multiple_of((1 - node) * half, half), half)] += token_other_ref[
        ...
    ].astype(F32)
    inner = inner_ref[...]
    gain = gain_ref[...]
    _, base, inverse = layer_norm(hidden_ref[...], gain)
    ln_ref[0:1, :] += 0.5 * jnp.sum(inner * base, axis=0, keepdims=True)
    index = step // (pl.num_programs(0) // 2)
    cot = row_pick(node, index, cot_ref[...], cot_other_ref[...])
    hidden_grad = cot.astype(F32) + norm_backward(inner, base, inverse, gain)

    @pl.when(index == node)
    def _():
        grad_ref[...] = hidden_grad

    low = hidden_grad.astype(BF16)
    attended_grad_ref[...] = dot_t(low, w_ref[...]).astype(BF16)
    turned = dot_t(turn_ref[...], attended_ref[...]).astype(BF16)
    acc_ref[...] += dot(turned, low)

    @pl.when(step == pl.num_programs(0) - 1)
    def _():
        size = half // parts
        for part in range(parts):
            weight_refs[part][...] = acc_ref[part * size : (part + 1) * size].astype(BF16)


def middle_back(
    node, grid, dense, dense_other, token, token_other, hidden, cot, cot_other, attended, gain, w_out, parts
):
    seq, width = hidden.shape
    half = width // 2
    rows = 256
    steps = seq // rows
    mine, theirs = half_rows((rows, width), steps // 2)
    row = lambda columns: spec((rows, columns), lambda i, n: (i, 0))
    result = (half // parts, width)
    return pl.pallas_call(
        functools.partial(middle_back_kernel, parts, grid),
        grid_spec=pltpu.PrefetchScalarGridSpec(
            num_scalar_prefetch=1,
            grid=(seq // rows,),
            in_specs=[
                row(width),
                row(width),
                row(half),
                row(half),
                row(width),
                mine,
                theirs,
                row(half),
                fixed((1, width)),
                spec((half, width), lambda i, n: (n[0], 0)),
            ],
            out_specs=[mine, row(half), fixed((8, width))] + [fixed(result)] * parts,
            scratch_shapes=[
                pltpu.VMEM((rows, width), F32),
                pltpu.VMEM((half, width), F32),
                pltpu.VMEM((half, half), BF16),
            ],
        ),
        out_shape=[
            struct((seq // 2, width), F32),
            struct((seq, half), BF16),
            struct((8, width), F32),
        ]
        + [struct(result, BF16)] * parts,
        cost_estimate=pl.CostEstimate(
            flops=2 * seq * width * width, bytes_accessed=18 * seq * width, transcendentals=0
        ),
        compiler_params=pltpu.CompilerParams(vmem_limit_bytes=LIMIT),
        name="middle_back",
    )(
        node, dense, dense_other, token, token_other, hidden, cot, cot_other, attended,
        gain[None], w_out,
    )


def dispatch_kernel(node_ref, place_ref, own_ref, other_ref, sent_ref):
    size = sent_ref.shape[0]
    node = node_ref[0]
    slot = pl.program_id(0) * size + lax.broadcasted_iota(jnp.int32, (size, 1), 0)
    total = None
    for at, ref in ((node, own_ref), (1 - node, other_ref)):
        place = place_ref[pl.ds(at, 1), :]
        part = dot((place == slot).astype(F32).astype(BF16), ref[...])
        total = part if total is None else total + part
    sent_ref[...] = total.astype(BF16)


def dispatch_rows(node, place, own, other, slots):
    rows = place.shape[1]
    half = own.shape[1] // 2
    size = 256
    column = spec((rows, half), lambda i, n: (0, n[0]))
    return pl.pallas_call(
        dispatch_kernel,
        grid_spec=pltpu.PrefetchScalarGridSpec(
            num_scalar_prefetch=1,
            grid=(slots // size,),
            in_specs=[fixed(place.shape), column, column],
            out_specs=spec((size, half), lambda i, n: (i, 0)),
        ),
        out_shape=struct((slots, half), BF16),
        cost_estimate=pl.CostEstimate(
            flops=4 * slots * rows * half, bytes_accessed=4 * slots * half, transcendentals=0
        ),
        compiler_params=pltpu.CompilerParams(vmem_limit_bytes=14 << 20),
        name="dispatch",
    )(node, place, own, other)


def combine_kernel(place_ref, got_ref, out_ref):
    size = place_ref.shape[0]
    slot = lax.broadcasted_iota(jnp.int32, (size, got_ref.shape[0]), 1)
    onehot = (place_ref[...] == slot).astype(F32).astype(BF16)
    out_ref[...] = dot(onehot, got_ref[...]).astype(BF16)


def combine_rows(place, got):
    rows = place.shape[0]
    size = 256
    return pl.pallas_call(
        combine_kernel,
        grid=(rows // size,),
        in_specs=[spec((size, 1), lambda i: (i, 0)), fixed(got.shape)],
        out_specs=spec((size, got.shape[1]), lambda i: (i, 0)),
        out_shape=struct((rows, got.shape[1]), BF16),
        cost_estimate=pl.CostEstimate(
            flops=2 * rows * got.shape[0] * got.shape[1],
            bytes_accessed=4 * rows * got.shape[1],
            transcendentals=0,
        ),
        compiler_params=pltpu.CompilerParams(vmem_limit_bytes=12 << 20),
        name="combine",
    )(place, got)


def combine_out_kernel(node_ref, place_ref, got_ref, dense_ref, share_ref, out_ref, sum_ref):
    size = place_ref.shape[0]
    half = got_ref.shape[1]
    node = node_ref[0]
    slot = lax.broadcasted_iota(jnp.int32, (size, got_ref.shape[0]), 1)
    onehot = (place_ref[...] == slot).astype(F32).astype(BF16)
    sum_ref[...] = dense_ref[...].astype(F32)
    sum_ref[:, pl.ds(pl.multiple_of(node * half, half), half)] += share_ref[:, 0:1] * dot(
        onehot, got_ref[...]
    )
    out_ref[...] = sum_ref[...].astype(BF16)


def combine_out(node, place, got, dense, share):
    rows, width = dense.shape
    size = 256
    steps = rows // size

    def chunk(i, n):
        mine = i // (steps // 2) == 0
        return (jnp.where(mine, n[0], 1 - n[0]) * (steps // 2) + i % (steps // 2), 0)

    return pl.pallas_call(
        combine_out_kernel,
        grid_spec=pltpu.PrefetchScalarGridSpec(
            num_scalar_prefetch=1,
            grid=(steps,),
            in_specs=[
                spec((size, 1), chunk),
                fixed(got.shape),
                spec((size, width), chunk),
                spec((size, LANES), chunk),
            ],
            out_specs=spec((size, width), lambda i, n: (i, 0)),
            scratch_shapes=[pltpu.VMEM((size, width), F32)],
        ),
        out_shape=struct((rows, width), BF16),
        cost_estimate=pl.CostEstimate(
            flops=2 * rows * got.shape[0] * got.shape[1],
            bytes_accessed=4 * rows * width,
            transcendentals=0,
        ),
        compiler_params=pltpu.CompilerParams(vmem_limit_bytes=20 << 20),
        name="combine_out",
    )(node, place, got, dense, share)


def branch_kernel(dense, experts, parts, layout, node_ref, *refs):
    if dense:
        x_refs, c_refs, route_ref, refs = refs[:1], refs[1:3], refs[3], refs[4:]
    else:
        x_refs, c_refs, refs = refs[:2], refs[2:4], refs[4:]
    side_ref, wct_ref, up_ref, dn_ref = refs[:4]
    refs = refs[4:]
    if dense:
        out_refs, dx_refs, gsm_ref, probs_ref = refs[:1], refs[1:2], refs[2], refs[3]
        grad_refs = refs[4 : 4 + parts]
        xt_ref, g_ref, a_ref, acc_ref, dxa_ref, act_ref, dpre_ref, gt_ref = refs[4 + parts :]
    else:
        out_refs, dx_refs, gsm_ref = refs[:2], refs[2:4], refs[4]
        g_ref, act_ref, dpre_ref, a_ref, acc_ref, dxa_ref = refs[5:]
    halves = len(x_refs)
    rows, half = x_refs[0].shape
    width = halves * half
    step = pl.program_id(0)
    small = 256
    big = 512
    unit = width // layout.members
    node = node_ref[0]
    if dense:
        order = functools.partial(layout.place, node, node_ref[1])
        split = [slice(0, width)]
    else:
        split = [
            pl.ds(pl.multiple_of(node * half, half), half),
            pl.ds(pl.multiple_of((1 - node) * half, half), half),
        ]

    @pl.when(step == 0)
    def _():
        lane = lax.broadcasted_iota(jnp.int32, (1, LANES), 1)
        is_router = lane < experts
        is_mix = (lane >= experts) & (lane < experts + 2)
        first = (lane == experts).astype(F32)
        second = (lane == experts + 1).astype(F32)
        picked = side_ref[...]

        def prepare(at):
            logits = sum(dot_t(x_refs[n][at, :], wct_ref[:, split[n]]) for n in range(halves))

            def soft(mask):
                masked = jnp.where(mask, logits, -1e30)
                shifted = jnp.exp(masked - jnp.max(masked, axis=1, keepdims=True))
                return shifted / jnp.sum(shifted, axis=1, keepdims=True)

            mix = soft(is_mix)
            if dense:
                factor = jnp.sum(mix * first, axis=1, keepdims=True)
                chosen = lane == route_ref[at, :]
                gate = jnp.sum(jnp.where(chosen, soft(is_router), 0.0), axis=1, keepdims=True)
                share = gate * jnp.sum(mix * second, axis=1, keepdims=True)
                probs_ref[at, :] = jnp.where(lane == 0, share, factor)
                a_ref[at, :] = jnp.where(is_mix, first - mix, 0.0)
            else:
                router = soft(is_router)
                gate = jnp.sum(router * picked, axis=1, keepdims=True)
                factor = gate * jnp.sum(mix * second, axis=1, keepdims=True)
                a_ref[at, :] = jnp.where(
                    is_router, picked - router, jnp.where(is_mix, second - mix, 0.0)
                )
            if dense:
                own = c_refs[0].shape[0]
                place = at.start // own
                inside = pl.ds(pl.multiple_of(at.start - place * own, small), small)
                cot = row_pick(node, place, c_refs[0][inside, :], c_refs[1][inside, :])
                scaled = (factor * cot.astype(F32)).astype(BF16)
                g_ref[at, :] = scaled
            else:
                for n in range(halves):
                    g_ref[at, split[n]] = (factor * c_refs[n][at, :].astype(F32)).astype(BF16)
            acc_ref[at, :] = jnp.zeros((small, width), F32)
            dxa_ref[at, :] = jnp.zeros((small, width), F32)

        chunks(rows, small, prepare)
        if dense:

            def transpose(at):
                turn = permutation(order, at.start, small, unit, width)
                for index in range(rows // big):
                    some = slice(index * big, (index + 1) * big)
                    xt_ref[at, some] = dot_t(turn, x_refs[0][some, :]).astype(BF16)
                    gt_ref[at, some] = dot_t(turn, g_ref[some, :]).astype(BF16)

            chunks(width, small, transpose)

    def forward(at):
        pre = sum(dot(x_refs[n][at, :], up_ref[split[n], :]) for n in range(halves))
        square = pre * pre
        bend = jnp.tanh(pre * (GELU_A + GELU_A * GELU_B * square))
        side = 0.5 * (1.0 + bend)
        act = (pre * side).astype(BF16)
        slope = side + 0.5 * pre * (1.0 - bend * bend) * (GELU_A + 3.0 * GELU_A * GELU_B * square)
        act_ref[at, :] = act
        if dense:
            act_grad = dot(g_ref[at, :], dn_ref[...])
            acc_ref[at, :] += dot_t(act, dn_ref[...])
        else:
            act_grad = dot_t(g_ref[at, :], dn_ref[...])
            acc_ref[at, :] += dot(act, dn_ref[...])
        pre_grad = (slope * act_grad).astype(BF16)
        dpre_ref[at, :] = pre_grad
        dxa_ref[at, :] += dot_t(pre_grad, up_ref[...])

    chunks(rows, big, forward)
    if dense:
        size = width // parts
        for part in range(parts):

            def weights(at):
                rows_at = pl.ds(pl.multiple_of(part * size + at.start, small), small)
                pair = (
                    dot(xt_ref[rows_at, :], dpre_ref[...]).astype(BF16),
                    dot(gt_ref[rows_at, :], act_ref[...]).astype(BF16),
                )
                for index in range(2 * small // unit):
                    to = pl.multiple_of(2 * at.start + index * unit, unit)
                    place = index // 2 * unit
                    grad_refs[part][pl.ds(to, unit), :] = pair[index % 2][place : place + unit]

            chunks(size, small, weights)

    @pl.when(step == pl.num_programs(0) - 1)
    def _():
        gsm_ref[...] = jnp.zeros_like(gsm_ref)

        def finish(at):
            out = acc_ref[at, :]
            strength = jnp.sum(g_ref[at, :].astype(F32) * out, axis=1, keepdims=True)
            logit_grad = strength * a_ref[at, :]
            low = logit_grad.astype(BF16)
            turned = logit_grad.T.astype(BF16)
            for n in range(halves):
                gsm_ref[:, split[n]] += dot(turned, x_refs[n][at, :])
                part = acc_ref[at, split[n]]
                if dense:
                    part = part * probs_ref[at, 1:2]
                out_refs[n][at, :] = part.astype(BF16)
                dx_refs[n][at, :] = (dxa_ref[at, split[n]] + dot(low, wct_ref[:, split[n]])).astype(
                    BF16
                )

        chunks(rows, small, finish)


def branch(node, layout, xs, cs, side, head_t, up, down, experts, parts):
    dense = len(xs) == 1
    rows, half = xs[0].shape
    width = len(xs) * half
    hidden = up.shape[1]
    block = 512
    column = lambda size: spec((size, block), lambda f, n: (0, f))
    up_spec = column(width)
    down_spec = up_spec if dense else spec((block, width), lambda f, n: (f, 0))
    outs = [(fixed((rows, half)), struct((rows, half), BF16))] * (2 * len(xs))
    outs = outs + [(fixed((LANES, width)), struct((LANES, width), F32))]
    sums = [
        pltpu.VMEM((rows, LANES), F32),
        pltpu.VMEM((rows, width), F32),
        pltpu.VMEM((rows, width), F32),
    ]
    if dense:
        outs = outs + [(fixed((rows, LANES)), struct((rows, LANES), F32))]
        size = 2 * width // parts
        outs = outs + [(column(size), struct((size, hidden), BF16))] * parts
        scratch = [
            pltpu.VMEM((width, rows), BF16),
            pltpu.VMEM((rows, width), BF16),
            *sums,
            pltpu.VMEM((rows, block), BF16),
            pltpu.VMEM((rows, block), BF16),
            pltpu.VMEM((width, rows), BF16),
        ]
    else:
        outs = outs + [(fixed((rows, width)), struct((rows, width), BF16))]
        outs = outs + [(column(rows), struct((rows, hidden), BF16))] * 2
        scratch = sums
    return pl.pallas_call(
        functools.partial(branch_kernel, dense, experts, parts, layout),
        grid_spec=pltpu.PrefetchScalarGridSpec(
            num_scalar_prefetch=1,
            grid=(hidden // block,),
            in_specs=[fixed(one.shape) for one in [*xs, *cs]]
            + [
                fixed(side.shape),
                fixed((LANES, width)),
                up_spec,
                down_spec,
            ],
            out_specs=[one for one, _ in outs],
            scratch_shapes=scratch,
        ),
        out_shape=[shape for _, shape in outs],
        cost_estimate=pl.CostEstimate(
            flops=(12 if dense else 8) * rows * width * hidden,
            bytes_accessed=12 * width * hidden + 8 * rows * width,
            transcendentals=rows * hidden,
        ),
        compiler_params=pltpu.CompilerParams(vmem_limit_bytes=LIMIT),
        name="dense_branch" if dense else "expert_branch",
    )(node, *xs, *cs, side, head_t, up, down)


def expert_up_kernel(node_ref, own_ref, other_ref, dpre_ref, grad_ref, xt_ref):
    rows, half = own_ref.shape
    node = node_ref[0]

    @pl.when(pl.program_id(0) == 0)
    def _():
        for at, ref in ((node, own_ref), (1 - node, other_ref)):
            place = pl.ds(pl.multiple_of(at * half, half), half)

            def turn(rows_at):
                xt_ref[place, rows_at] = ref[rows_at, :].T

            chunks(rows, 256, turn)

    def weights(at):
        grad_ref[at, :] = dot(xt_ref[at, :], dpre_ref[...])

    chunks(2 * half, 256, weights)


def expert_down_kernel(act_ref, g_ref, grad_ref):
    grad_ref[...] = dot_n(act_ref[...], g_ref[...])


def expert_up_grad(node, own, other, dpre):
    rows, half = own.shape
    hidden = dpre.shape[1]
    block = 512
    return pl.pallas_call(
        expert_up_kernel,
        grid_spec=pltpu.PrefetchScalarGridSpec(
            num_scalar_prefetch=1,
            grid=(hidden // block,),
            in_specs=[
                fixed(own.shape),
                fixed(own.shape),
                spec((rows, block), lambda f, n: (0, f)),
            ],
            out_specs=spec((2 * half, block), lambda f, n: (0, f)),
            scratch_shapes=[pltpu.VMEM((2 * half, rows), BF16)],
        ),
        out_shape=struct((2 * half, hidden), F32),
        cost_estimate=pl.CostEstimate(
            flops=4 * rows * half * hidden,
            bytes_accessed=8 * half * hidden + 2 * rows * hidden,
            transcendentals=0,
        ),
        compiler_params=pltpu.CompilerParams(vmem_limit_bytes=LIMIT),
        name="expert_up_grad",
    )(node, own, other, dpre)


def expert_down_grad(act, g):
    rows, hidden = act.shape
    width = g.shape[1]
    block = 256
    return pl.pallas_call(
        expert_down_kernel,
        grid=(hidden // block,),
        in_specs=[spec((rows, block), lambda f: (0, f)), fixed(g.shape)],
        out_specs=spec((block, width), lambda f: (f, 0)),
        out_shape=struct((hidden, width), F32),
        cost_estimate=pl.CostEstimate(
            flops=2 * rows * width * hidden,
            bytes_accessed=4 * width * hidden + 2 * rows * hidden,
            transcendentals=0,
        ),
        compiler_params=pltpu.CompilerParams(vmem_limit_bytes=28 << 20),
        name="expert_down_grad",
    )(act, g)


def turn_kernel(grid, node_ref, x_ref, out_ref):
    rows, width = out_ref.shape[0], x_ref.shape[1]
    order = functools.partial(grid.place, node_ref[0], node_ref[1])
    start = pl.program_id(0) * rows
    rows_of = permutation(order, start, rows, width // (2 * grid.members), width, 2)
    out_ref[...] = dot_t(rows_of, x_ref[...]).astype(BF16)


def turn(node, grid, x):
    seq, width = x.shape
    rows = 256
    return pl.pallas_call(
        functools.partial(turn_kernel, grid),
        grid_spec=pltpu.PrefetchScalarGridSpec(
            num_scalar_prefetch=1,
            grid=(width // rows,),
            in_specs=[fixed(x.shape)],
            out_specs=spec((rows, seq), lambda i, n: (i, 0)),
        ),
        out_shape=struct((width, seq), BF16),
        cost_estimate=pl.CostEstimate(
            flops=2 * seq * width * width, bytes_accessed=4 * seq * width, transcendentals=0
        ),
        compiler_params=pltpu.CompilerParams(vmem_limit_bytes=16 << 20),
        name="turn",
    )(node, x)


def tail_kernel(
    parts,
    ln_lane,
    grid,
    node_ref,
    x_ref,
    xt_ref,
    gain_ref,
    small_ref,
    packed_ref,
    w_ref,
    keep_ref,
    send_ref,
    *refs,
):
    part_refs = refs[:parts]
    acc_ref = refs[parts]
    seq, width = x_ref.shape
    size = width // parts
    own = keep_ref.shape[0]
    order = functools.partial(grid.place, node_ref[0], node_ref[1])
    block = width // (2 * grid.members)
    step = pl.program_id(0)
    last = pl.num_programs(0) - 1

    @pl.when(step < last)
    def _():
        for part in range(parts):

            def weights(at):
                rows_at = pl.ds(pl.multiple_of(part * size + at.start, 256), 256)
                part_refs[part][at, :] = dot(xt_ref[rows_at, :], packed_ref[0]).astype(BF16)

            chunks(size, 256, weights)

        @pl.when(step == 0)
        def _():
            acc_ref[...] = jnp.zeros_like(acc_ref)

        def back(at):
            acc_ref[at, :] += dot_t(packed_ref[0, at, :], w_ref[...])

        chunks(seq, 256, back)

    @pl.when(step == last)
    def _():
        gain = gain_ref[...]
        node = node_ref[0]

        def column_sum(index, total):
            rows = pl.ds(pl.multiple_of(index * 256, 256), 256)
            return total + jnp.sum(
                acc_ref[rows, :] * x_ref[rows, :].astype(F32), axis=0, keepdims=True
            )

        total = lax.fori_loop(0, seq // 256, column_sum, jnp.zeros((1, width), F32)) / gain
        row = lax.broadcasted_iota(jnp.int32, (LANES, 1), 0)
        small = (small_ref[...] + jnp.where(row == ln_lane, total, 0.0)).astype(BF16)
        for part in range(parts):

            def turn(at):
                rows = permutation(order, part * size + at.start, 256, block, width, 2)
                part_refs[part][at, 0:LANES] = dot_t(rows, small).astype(BF16)

            chunks(size, 256, turn)
        keep_ref[...] = acc_ref[pl.ds(pl.multiple_of(node * own, own), own), :]
        send_ref[...] = acc_ref[pl.ds(pl.multiple_of((1 - node) * own, own), own), :].astype(BF16)


def tail(node, grid, normed, turned, gain, small, packed, w_qkv, parts, ln_lane):
    seq, width = normed.shape
    half = width // 2
    steps = 3
    part = (width // parts, half)
    return pl.pallas_call(
        functools.partial(tail_kernel, parts, ln_lane, grid),
        grid_spec=pltpu.PrefetchScalarGridSpec(
            num_scalar_prefetch=1,
            grid=(steps + 1,),
            in_specs=[
                fixed(normed.shape),
                fixed(turned.shape),
                fixed((1, width)),
                fixed((LANES, width)),
                spec((1, seq, half), lambda i, n: (jnp.minimum(i, steps - 1), 0, 0)),
                spec((width, half), lambda i, n: (0, 2 * jnp.minimum(i, steps - 1) + n[0])),
            ],
            out_specs=[fixed((seq // 2, width)), fixed((seq // 2, width))]
            + [spec(part, lambda i, n: (0, i))] * parts,
            scratch_shapes=[pltpu.VMEM((seq, width), F32)],
        ),
        out_shape=[struct((seq // 2, width), F32), struct((seq // 2, width), BF16)]
        + [struct((width // parts, steps * half + LANES), BF16)] * parts,
        cost_estimate=pl.CostEstimate(
            flops=6 * seq * width * width, bytes_accessed=16 * seq * width, transcendentals=0
        ),
        compiler_params=pltpu.CompilerParams(vmem_limit_bytes=32 << 20),
        name="tail",
    )(node, normed, turned, gain[None], small, packed, w_qkv)


class Grid:

    def __init__(self, members):
        self.third = 4 if members % 4 == 0 else 1
        self.first = round((members // self.third) ** 0.5)
        assert self.third * self.first * self.first == members
        self.members = members
        self.sizes = (self.first, self.first, self.third)

    def digits(self, node, member):
        low, high = member % self.first, (member // self.first) % self.first
        top = member // (self.first * self.first)
        return (low, high, top) if node == 0 else (high, low, top)

    def index(self, node, digits):
        low, high = (digits[0], digits[1]) if node == 0 else (digits[1], digits[0])
        return (digits[2] * self.first + high) * self.first + low

    def shift(self, stage, by):
        pairs = []
        for node in range(2):
            for member in range(self.members):
                digits = list(self.digits(node, member))
                digits[stage] = (digits[stage] + by) % self.sizes[stage]
                target = self.index(node, digits)
                pairs.append((node * self.members + member, node * self.members + target))
        return pairs

    def place(self, node, member, place):
        size, third = self.first, self.third
        low, high = member % size, (member // size) % size
        top = member // (size * size)
        one = (jnp.where(node == 0, low, high) + place // (size * third)) % size
        two = (jnp.where(node == 0, high, low) + (place // third) % size) % size
        low, high = jnp.where(node == 0, one, two), jnp.where(node == 0, two, one)
        return ((top + place % third) % third * size + high) * size + low

    def send(self, parts, stage):
        return [
            lax.ppermute(parts[by], ("node", "expert"), self.shift(stage, by))
            for by in range(1, self.sizes[stage])
        ]

    def add(self, parts, came, stage, *gates):
        if gates:
            came = [after(other, *gates) for other in came]
        pieces = self.sizes[stage + 1] if stage < 2 else 1
        rows = parts[0].shape[0] // pieces
        sums = []
        for piece in range(pieces):
            at = slice(piece * rows, (piece + 1) * rows)
            total = parts[0][at].astype(F32)
            for other in came:
                total = total + other[at].astype(F32)
            sums.append(total.astype(BF16) if stage < 2 else total)
        return sums


def shards(
    tokens,
    cotangent,
    routes,
    ln1_gain,
    w_qkv,
    w_out,
    ln2_gain,
    w_router,
    w_mix,
    w_up,
    w_down,
    expert_up,
    expert_down,
):
    node = lax.axis_index("node")
    member = lax.axis_index("expert")
    members = lax.axis_size("expert")
    width = tokens.shape[2]
    half = width // 2
    own_rows = tokens.shape[1]
    seq = 2 * own_rows
    experts = w_router.shape[1]
    capacity = 3 * seq // (2 * experts)
    slots = experts * capacity
    pairs = half // LANES
    own_start = node * own_rows
    scalar = jnp.stack([node, member]).astype(jnp.int32)
    grid = Grid(members)
    parts = grid.sizes[0]

    def swap(value):
        return lax.ppermute(value, "node", SWAP)

    def in_order(mine, other, axis):
        return jnp.where(
            node == 0,
            jnp.concatenate([mine, other], axis=axis),
            jnp.concatenate([other, mine], axis=axis),
        )

    own_tokens, own_cot = tokens[0], cotangent[0]
    other_tokens, other_cot = swap(own_tokens), swap(own_cot)

    group_routes = routes.reshape(-1)
    route_onehot = group_routes[:, None] == jnp.arange(experts)[None, :]
    ones = route_onehot.astype(BF16)
    row_at = jnp.arange(seq)
    earlier = (row_at[:, None] > row_at[None, :]).astype(BF16)
    order = jnp.sum(jnp.where(route_onehot, dot(earlier, ones), 0.0), axis=1).astype(jnp.int32)
    place = jnp.where(order < capacity, group_routes * capacity + order, slots)
    place_rows = place.reshape(2, own_rows)
    place_column = place.reshape(seq, 1)

    def exchange(value):
        value = value.reshape(experts, capacity, half)
        got = lax.all_to_all(value, "expert", split_axis=0, concat_axis=0, tiled=True)
        return got.reshape(slots, half)

    def give_back(mine, other):
        total = (mine.astype(F32) + swap(other).astype(F32)).astype(BF16)
        return total, exchange(total)

    got_cot = exchange(dispatch_rows(scalar, place_rows, own_cot, other_cot, slots))

    qkv, normed_low = front(scalar, own_tokens, other_tokens, ln1_gain, w_qkv)
    attended_own, lse = attend(qkv, pairs)
    hidden, inner_low, sent_rows = middle(
        scalar, own_tokens, other_tokens, attended_own, swap(attended_own), w_out, ln2_gain,
        place.reshape(1, seq), slots,
    )

    got_rows = exchange(sent_rows)
    head_t = jnp.concatenate(
        [w_router, w_mix, jnp.zeros((width, LANES - experts - 2), BF16)], axis=1
    ).T
    picked = (jnp.arange(LANES) == member).astype(F32)[None]
    results = branch(
        scalar, grid, [inner_low], [own_cot, other_cot, group_routes[:, None]], picked, head_t, w_up, w_down,
        experts, parts,
    )
    dense_out, dense_dx, small_dense, share = results[:4]
    pair0 = results[4:]
    came = grid.send(pair0, 0)
    got_rows = after(got_rows, small_dense)
    expert_rows = [got_rows, swap(got_rows)]
    out_keep, out_send, dx_keep, dx_send, small_expert, expert_g, expert_act, expert_dpre = branch(
        scalar, grid, expert_rows, [got_cot, swap(got_cot)], picked, head_t, expert_up[0],
        expert_down[0], experts, parts,
    )

    sent_dx, got_dx = give_back(dx_keep, dx_send)
    pair1 = grid.add(pair0, came, 0, sent_dx)
    came = grid.send(pair1, 1)
    grad_expert_down = expert_down_grad(expert_act, after(expert_g, sent_dx))
    _, got_out = give_back(out_keep, after(out_send, grad_expert_down))
    turned_low = turn(scalar, grid, after(normed_low, grad_expert_down))
    token_dx = combine_rows(place_column, after(got_dx, pair1, turned_low))
    results = middle_back(
        scalar, grid, dense_dx, swap(dense_dx), token_dx, swap(token_dx), hidden, own_cot,
        other_cot, attended_own, ln2_gain, w_out, parts,
    )
    hidden_grad, attended_grad, ln2_row = results[:3]
    out0 = results[3:]
    out_came = grid.send(out0, 0)
    pair2 = grid.add(pair1, came, 1, ln2_row)
    came = grid.send(pair2, 2)
    packed = attend_back(qkv, attended_own, attended_grad, lse)

    small = small_dense + small_expert
    small = small + jnp.where(jnp.arange(LANES)[:, None] == experts + 3, ln2_row[0:1], 0.0)
    results = tail(
        scalar, grid, normed_low, turned_low, ln1_gain, small, packed, w_qkv, parts, experts + 2
    )
    grad_keep, grad_send, last0 = results[0], results[1], results[2:]
    last_came = grid.send(last0, 0)
    out1 = grid.add(out0, out_came, 0, grad_keep)
    out_came = grid.send(out1, 1)
    grad_expert_up = expert_up_grad(scalar, *expert_rows, after(expert_dpre, grad_keep))
    last1 = grid.add(last0, last_came, 0, grad_expert_up)
    last_came = grid.send(last1, 1)

    total_out = combine_out(scalar, place_column, after(got_out, last1), dense_out, share)
    out_mine, out_other = total_out[:own_rows], swap(total_out[own_rows:])
    out2 = grid.add(out1, out_came, 1, last1)
    out_came = grid.send(out2, 2)


    last2 = grid.add(last1, last_came, 1, total_out, out2)
    last_came = grid.send(last2, 2)

    unit = width // members
    both = grid.add(pair2, came, 2, last2)[0]
    grad_w_up, grad_w_down = both[:unit], both[unit:]
    hidden_own = lax.dynamic_slice_in_dim(hidden, own_start, own_rows, 0)
    out_other = after(out_other, last2)
    mixed_out = (hidden_own + out_mine.astype(F32) + out_other.astype(F32)).astype(BF16)
    grad_w_out = grid.add(out2, out_came, 2, last2)[0]
    normed_grad = grad_keep + after(swap(grad_send), last2).astype(F32)
    _, base_one, inverse_one = layer_norm(own_tokens.astype(F32), ln1_gain)
    input_grad = hidden_grad + norm_backward(
        normed_grad, base_one, inverse_one, ln1_gain
    )
    block = width // (2 * members)
    last = grid.add(last2, last_came, 2, input_grad, grad_w_out, mixed_out, both)[0].reshape(2, block, -1)
    kept = lax.dynamic_index_in_dim(last, node, 0, False)
    other = swap(lax.dynamic_index_in_dim(last, 1 - node, 0, False).astype(BF16)).astype(F32)

    def columns(rows):
        return rows[:, : 3 * half].reshape(block, 3, half)

    grad_w_qkv = in_order(columns(kept), columns(other), 2).reshape(block, 3 * width)
    small = kept[:, 3 * half :] + other[:, 3 * half :]
    return (
        mixed_out.reshape(tokens.shape),
        input_grad.reshape(tokens.shape),
        small[:, experts + 2],
        grad_w_qkv,
        grad_w_out,
        small[:, experts + 3],
        small[:, :experts],
        small[:, experts : experts + 2],
        grad_w_up,
        grad_w_down,
        grad_expert_up[None],
        grad_expert_down[None],
    )


def solution(mesh):
    return jax.shard_map(
        shards,
        mesh=mesh,
        in_specs=(
            P("expert", "node", None),
            P("expert", "node", None),
            P("expert", None, None),
            P(),
            P(),
            P(),
            P(),
            P(),
            P(),
            P(None, "node"),
            P(None, "node"),
            P("expert", None, "node"),
            P("expert", "node", None),
        ),
        out_specs=(
            P("expert", "node", None),
            P("expert", "node", None),
            P(("node", "expert")),
            P(("node", "expert"), None),
            P(("node", "expert"), None),
            P(("node", "expert")),
            P(("node", "expert"), None),
            P(("node", "expert"), None),
            P("expert", "node"),
            P("expert", "node"),
            P("expert", None, "node"),
            P("expert", "node", None),
        ),
        check_vma=False,
    )
```

```python
import functools

import jax
import jax.numpy as jnp
from jax import lax
from jax.experimental import pallas as pl
from jax.experimental.pallas import tpu as pltpu
from jax.sharding import PartitionSpec as P


HEAD_DIM = 64
LIMIT = 60 << 20
EPS = 1e-05
LANES = 128
LOG2E = 1.4426950408889634
GELU_A = 0.7978845608028654
GELU_B = 0.044715
SWAP = [(0, 1), (1, 0)]
F32 = jnp.float32
BF16 = jnp.bfloat16


def dot(left, right):
    return jnp.dot(left, right, preferred_element_type=F32)


def dot_t(left, right):
    return lax.dot_general(left, right, (((1,), (1,)), ((), ())), preferred_element_type=F32)


def dot_n(left, right):
    return lax.dot_general(left, right, (((0,), (0,)), ((), ())), preferred_element_type=F32)


def layer_norm(values, gain):
    average = jnp.mean(values, axis=-1, keepdims=True)
    centered = values - average
    inverse = lax.rsqrt(jnp.mean(centered * centered, axis=-1, keepdims=True) + EPS)
    normed = centered * inverse
    return (normed * gain, normed, inverse)


def norm_backward(upstream, normed, inverse, gain):
    scaled = upstream * gain
    inner_term = (
        scaled
        - jnp.mean(scaled, axis=-1, keepdims=True)
        - normed * jnp.mean(scaled * normed, axis=-1, keepdims=True)
    )
    return inner_term * inverse


def spec(shape, index):
    return pl.BlockSpec(shape, index)


def fixed(shape):
    return pl.BlockSpec(shape, lambda *_: (0,) * len(shape), pipeline_mode=pl.Buffered(1))


def struct(shape, kind):
    return jax.ShapeDtypeStruct(shape, kind)


def far(shape, kind):
    return pltpu.HBM(shape, kind)


def chunks(count, size, step):
    def run(index, carry):
        step(pl.ds(pl.multiple_of(index * size, size), size))
        return carry

    lax.fori_loop(0, count // size, run, 0)


def after(value, *others):
    return lax.optimization_barrier((value, others))[0]


def row_pick(node, index, own, other):
    return jnp.where(index == node, own, other)


def permutation(order, start, count, block, columns, copies=1):
    lane = lax.broadcasted_iota(jnp.int32, (block, columns), 1)
    row = lax.broadcasted_iota(jnp.int32, (block, columns), 0)
    pieces = []
    for index in range(count // block):
        place = start // block + index
        first = order(place // copies) * block + (place % copies) * (columns // copies)
        pieces.append((row + first == lane).astype(F32))
    return jnp.concatenate(pieces, axis=0).astype(BF16)


def half_rows(shape, steps):
    return [
        spec(shape, lambda i, n, at=at: (jnp.clip(i - abs(at - n[0]) * steps, 0, steps - 1), 0))
        for at in range(2)
    ]


def front_kernel(node_ref, own_ref, other_ref, gain_ref, w_ref, qkv_ref, normed_ref):
    rows = own_ref.shape[0]
    node = node_ref[0]

    @pl.when(pl.program_id(0) == 0)
    def _():
        for place, part in ((node, own_ref), (1 - node, other_ref)):
            def norm(at):
                normed, _, _ = layer_norm(part[at, :].astype(F32), gain_ref[...])
                start = pl.multiple_of(place * rows + at.start, 128)
                normed_ref[pl.ds(start, 128), :] = normed.astype(BF16)

            chunks(rows, 128, norm)

    def project(at):
        qkv_ref[at, :] = dot(normed_ref[at, :], w_ref[...]).astype(BF16)

    chunks(2 * rows, 512, project)


def front(node, own, other, gain, w_qkv):
    rows, width = own.shape
    half = width // 2
    return pl.pallas_call(
        front_kernel,
        grid_spec=pltpu.PrefetchScalarGridSpec(
            num_scalar_prefetch=1,
            grid=(3,),
            in_specs=[
                fixed(own.shape),
                fixed(own.shape),
                fixed((1, width)),
                spec((width, half), lambda i, n: (0, 2 * i + n[0])),
            ],
            out_specs=[
                spec((2 * rows, half), lambda i, n: (0, i)),
                fixed((2 * rows, width)),
            ],
        ),
        out_shape=[struct((2 * rows, 3 * half), BF16), struct((2 * rows, width), BF16)],
        cost_estimate=pl.CostEstimate(
            flops=6 * rows * width * width, bytes_accessed=14 * rows * width, transcendentals=0
        ),
        compiler_params=pltpu.CompilerParams(vmem_limit_bytes=28 << 20),
        name="front",
    )(node, own, other, gain[None], w_qkv)


QB = 256


def head_specs(seq, pairs):
    return [spec((seq, LANES), lambda j, at=at: (0, at * pairs + j)) for at in range(3)]


def attend_kernel(q_ref, k_ref, v_ref, out_ref, lse_ref, ot_ref):
    seq = q_ref.shape[0]
    factor = HEAD_DIM ** (-0.5) * LOG2E
    lane = lax.broadcasted_iota(jnp.int32, (1, LANES), 1)
    v_t = v_ref[...].T
    below = lax.broadcasted_iota(jnp.int32, (QB, QB), 0) <= lax.broadcasted_iota(
        jnp.int32, (QB, QB), 1
    )
    for head in range(2):
        keep = (lane // HEAD_DIM) == head
        keys = jnp.where(keep, k_ref[...], 0)
        v_rows = v_t[head * HEAD_DIM : (head + 1) * HEAD_DIM]
        for block in range(seq // QB):
            lo, hi = block * QB, (block + 1) * QB
            queries = q_ref[lo:hi]
            diag = jnp.where(below, dot_t(keys[lo:hi], queries), -1e30)
            top = jnp.max(diag, axis=0, keepdims=True)
            if lo:
                past = dot_t(keys[:lo], queries)
                top = jnp.maximum(top, jnp.max(past, axis=0, keepdims=True))
            p_diag = jnp.exp2((diag - top) * factor)
            total = jnp.sum(p_diag, axis=0, keepdims=True)
            acc = dot(v_rows[:, lo:hi], p_diag.astype(BF16))
            if lo:
                p_past = jnp.exp2((past - top) * factor)
                total = total + jnp.sum(p_past, axis=0, keepdims=True)
                acc = acc + dot(v_rows[:, :lo], p_past.astype(BF16))
            ot_ref[head * HEAD_DIM : (head + 1) * HEAD_DIM, lo:hi] = acc * (1.0 / total)
            lse_ref[0, head : head + 1, lo:hi] = top * factor + jnp.log2(total)
    out_ref[...] = ot_ref[...].T.astype(BF16)


def attend(qkv, pairs):
    seq = qkv.shape[0]
    return pl.pallas_call(
        attend_kernel,
        grid=(pairs,),
        in_specs=head_specs(seq, pairs),
        out_specs=[
            spec((seq, LANES), lambda j: (0, j)),
            spec((1, 8, seq), lambda j: (j, 0, 0)),
        ],
        out_shape=[struct((seq, pairs * LANES), BF16), struct((pairs, 8, seq), F32)],
        scratch_shapes=[
            pltpu.VMEM((LANES, seq), F32),
        ],
        cost_estimate=pl.CostEstimate(
            flops=pairs * 8 * seq * seq * LANES,
            bytes_accessed=pairs * seq * LANES * 8,
            transcendentals=pairs * seq * seq,
        ),
        compiler_params=pltpu.CompilerParams(vmem_limit_bytes=14 << 20),
        name="attend",
    )(qkv, qkv, qkv)


def attend_back_kernel(
    q_ref, k_ref, v_ref, out_ref, grad_ref, lse_ref, packed_ref, dqt_ref, dka_ref, dva_ref
):
    seq = q_ref.shape[0]
    scale = HEAD_DIM ** (-0.5)
    factor = scale * LOG2E
    lane = lax.broadcasted_iota(jnp.int32, (1, LANES), 1)
    k_t = k_ref[...].T
    product = (grad_ref[...].astype(F32) * out_ref[...].astype(F32)).T
    below = lax.broadcasted_iota(jnp.int32, (QB, QB), 0) <= lax.broadcasted_iota(
        jnp.int32, (QB, QB), 1
    )
    dka_ref[...] = jnp.zeros_like(dka_ref)
    dva_ref[...] = jnp.zeros_like(dva_ref)
    for head in range(2):
        keep = (lane // HEAD_DIM) == head
        rows = slice(head * HEAD_DIM, (head + 1) * HEAD_DIM)
        keys = jnp.where(keep, k_ref[...], 0)
        values = jnp.where(keep, v_ref[...], 0)
        delta = jnp.sum(product[rows], axis=0, keepdims=True)
        for block in range(seq // QB):
            lo, hi = block * QB, (block + 1) * QB
            queries = jnp.where(keep, q_ref[lo:hi], 0)
            grads = jnp.where(keep, grad_ref[lo:hi], 0)
            lse = lse_ref[0, head : head + 1, lo:hi]
            drop = delta[:, lo:hi]
            acc = None
            for start, stop in ((lo, hi), (0, lo)):
                if start == stop:
                    continue
                probs = jnp.exp2(dot_t(keys[start:stop], queries) * factor - lse)
                if start == lo:
                    probs = jnp.where(below, probs, 0.0)
                prob_grad = dot_t(values[start:stop], grads)
                score_grad = (probs * (prob_grad - drop)).astype(BF16)
                dva_ref[start:stop] += dot(probs.astype(BF16), grads)
                dka_ref[start:stop] += dot(score_grad, queries)
                part = dot(k_t[rows, start:stop], score_grad)
                acc = part if acc is None else acc + part
            dqt_ref[rows, lo:hi] = acc
    packed_ref[0] = (dqt_ref[...].T * scale).astype(BF16)
    packed_ref[1] = (dka_ref[...] * scale).astype(BF16)
    packed_ref[2] = dva_ref[...].astype(BF16)


def attend_back(qkv, attended, grad, lse):
    seq = qkv.shape[0]
    pairs = lse.shape[0]
    one = spec((seq, LANES), lambda j: (0, j))
    return pl.pallas_call(
        attend_back_kernel,
        grid=(pairs,),
        in_specs=head_specs(seq, pairs) + [one, one, spec((1, 8, seq), lambda j: (j, 0, 0))],
        out_specs=spec((3, seq, LANES), lambda j: (0, 0, j)),
        out_shape=struct((3, *attended.shape), BF16),
        scratch_shapes=[
            pltpu.VMEM((LANES, seq), F32),
            pltpu.VMEM((seq, LANES), F32),
            pltpu.VMEM((seq, LANES), F32),
        ],
        cost_estimate=pl.CostEstimate(
            flops=pairs * 20 * seq * seq * LANES,
            bytes_accessed=pairs * seq * LANES * 16,
            transcendentals=pairs * seq * seq,
        ),
        compiler_params=pltpu.CompilerParams(vmem_limit_bytes=20 << 20),
        name="attend_back",
    )(qkv, qkv, qkv, attended, grad, lse)


def middle_kernel(
    row_steps,
    node_ref,
    tok_ref,
    tok_other_ref,
    own_ref,
    other_ref,
    w_ref,
    gain_ref,
    place_ref,
    hidden_ref,
    normed_ref,
    sent_ref,
    half_ref,
):
    rows, half = own_ref.shape
    node = node_ref[0]
    step = pl.program_id(0)
    mine = pl.ds(pl.multiple_of(node * half, half), half)
    theirs = pl.ds(pl.multiple_of((1 - node) * half, half), half)

    @pl.when(step < row_steps)
    def _():
        tok = row_pick(node, step // (row_steps // 2), tok_ref[...], tok_other_ref[...])
        hidden = tok.astype(F32) + (
            dot(own_ref[...], w_ref[mine, :]) + dot(other_ref[...], w_ref[theirs, :])
        )
        normed, _, _ = layer_norm(hidden, gain_ref[...])
        hidden_ref[...] = hidden
        normed_ref[...] = normed.astype(BF16)
        half_ref[pl.ds(pl.multiple_of(step * rows, rows), rows), :] = normed_ref[:, mine]

    @pl.when(step >= row_steps)
    def _():
        size = sent_ref.shape[0]
        first = (step - row_steps) * size
        slot = first + lax.broadcasted_iota(jnp.int32, (size, 1), 0)
        onehot = (place_ref[...] == slot).astype(F32).astype(BF16)
        sent_ref[...] = dot(onehot, half_ref[...]).astype(BF16)


def middle(node, tokens, tokens_other, own, other, w_out, gain, place, slots):
    width = tokens.shape[1]
    seq = 2 * tokens.shape[0]
    rows = 256
    size = 512
    steps = seq // rows
    mine, theirs = half_rows((rows, width), steps // 2)
    row = lambda columns: spec((rows, columns), lambda i, n: (jnp.minimum(i, steps - 1), 0))
    return pl.pallas_call(
        functools.partial(middle_kernel, steps),
        grid_spec=pltpu.PrefetchScalarGridSpec(
            num_scalar_prefetch=1,
            grid=(steps + slots // size,),
            in_specs=[
                mine,
                theirs,
                row(width // 2),
                row(width // 2),
                fixed(w_out.shape),
                fixed((1, width)),
                fixed(place.shape),
            ],
            out_specs=[
                row(width),
                row(width),
                spec((size, width // 2), lambda i, n: (jnp.maximum(i - steps, 0), 0)),
            ],
            scratch_shapes=[pltpu.VMEM((seq, width // 2), BF16)],
        ),
        out_shape=[
            far((seq, width), F32),
            far((seq, width), BF16),
            far((slots, width // 2), BF16),
        ],
        cost_estimate=pl.CostEstimate(
            flops=2 * seq * width * width + seq * slots * width,
            bytes_accessed=12 * seq * width,
            transcendentals=0,
        ),
        compiler_params=pltpu.CompilerParams(vmem_limit_bytes=24 << 20),
        name="middle",
    )(node, tokens, tokens_other, own, other, w_out, gain[None], place)


def middle_back_kernel(
    parts,
    grid,
    node_ref,
    dense_ref,
    dense_other_ref,
    token_ref,
    token_other_ref,
    hidden_ref,
    cot_ref,
    cot_other_ref,
    attended_ref,
    gain_ref,
    w_ref,
    grad_ref,
    attended_grad_ref,
    ln_ref,
    *refs,
):
    weight_refs = refs[:parts]
    acc_ref, turn_ref = refs[parts:]
    half = token_ref.shape[1]
    node = node_ref[0]
    step = pl.program_id(0)

    @pl.when(step == 0)
    def _():
        ln_ref[...] = jnp.zeros_like(ln_ref)
        acc_ref[...] = jnp.zeros_like(acc_ref)
        order = functools.partial(grid.place, node_ref[0], node_ref[1])
        turn_ref[...] = permutation(order, 0, half, half // grid.members, half)

    tok, tok_other = token_ref[...], token_other_ref[...]
    left, right = row_pick(node, 0, tok, tok_other), row_pick(node, 0, tok_other, tok)
    inner = (
        dense_ref[...].astype(F32)
        + dense_other_ref[...].astype(F32)
        + jnp.concatenate([left, right], axis=1).astype(F32)
    )
    gain = gain_ref[...]
    _, base, inverse = layer_norm(hidden_ref[...], gain)
    ln_ref[0:1, :] += 0.5 * jnp.sum(inner * base, axis=0, keepdims=True)
    index = step // (pl.num_programs(0) // 2)
    cot = row_pick(node, index, cot_ref[...], cot_other_ref[...])
    hidden_grad = cot.astype(F32) + norm_backward(inner, base, inverse, gain)

    @pl.when(index == node)
    def _():
        grad_ref[...] = hidden_grad

    low = hidden_grad.astype(BF16)
    attended_grad_ref[...] = dot_t(low, w_ref[...]).astype(BF16)
    turned = dot_t(turn_ref[...], attended_ref[...]).astype(BF16)
    acc_ref[...] += dot(turned, low)

    @pl.when(step == pl.num_programs(0) - 1)
    def _():
        size = half // parts
        for part in range(parts):
            weight_refs[part][...] = acc_ref[part * size : (part + 1) * size].astype(BF16)


def middle_back(
    node, grid, dense, dense_other, token, token_other, hidden, cot, cot_other, attended, gain, w_out, parts
):
    seq, width = hidden.shape
    half = width // 2
    rows = 256
    steps = seq // rows
    mine, theirs = half_rows((rows, width), steps // 2)
    row = lambda columns: spec((rows, columns), lambda i, n: (i, 0))
    result = (half // parts, width)
    return pl.pallas_call(
        functools.partial(middle_back_kernel, parts, grid),
        grid_spec=pltpu.PrefetchScalarGridSpec(
            num_scalar_prefetch=1,
            grid=(seq // rows,),
            in_specs=[
                row(width),
                row(width),
                row(half),
                row(half),
                row(width),
                mine,
                theirs,
                row(half),
                fixed((1, width)),
                spec((half, width), lambda i, n: (n[0], 0)),
            ],
            out_specs=[mine, row(half), fixed((8, width))] + [fixed(result)] * parts,
            scratch_shapes=[
                pltpu.VMEM((half, width), F32),
                pltpu.VMEM((half, half), BF16),
            ],
        ),
        out_shape=[
            struct((seq // 2, width), F32),
            struct((seq, half), BF16),
            struct((8, width), F32),
        ]
        + [struct(result, BF16)] * parts,
        cost_estimate=pl.CostEstimate(
            flops=2 * seq * width * width, bytes_accessed=18 * seq * width, transcendentals=0
        ),
        compiler_params=pltpu.CompilerParams(vmem_limit_bytes=LIMIT),
        name="middle_back",
    )(
        node, dense, dense_other, token, token_other, hidden, cot, cot_other, attended,
        gain[None], w_out,
    )


def dispatch_kernel(node_ref, place_ref, own_ref, other_ref, sent_ref):
    size = sent_ref.shape[0]
    node = node_ref[0]
    slot = pl.program_id(0) * size + lax.broadcasted_iota(jnp.int32, (size, 1), 0)
    total = None
    for at, ref in ((node, own_ref), (1 - node, other_ref)):
        place = place_ref[pl.ds(at, 1), :]
        part = dot((place == slot).astype(F32).astype(BF16), ref[...])
        total = part if total is None else total + part
    sent_ref[...] = total.astype(BF16)


def dispatch_rows(node, place, own, other, slots):
    rows = place.shape[1]
    half = own.shape[1] // 2
    size = 256
    column = spec((rows, half), lambda i, n: (0, n[0]))
    return pl.pallas_call(
        dispatch_kernel,
        grid_spec=pltpu.PrefetchScalarGridSpec(
            num_scalar_prefetch=1,
            grid=(slots // size,),
            in_specs=[fixed(place.shape), column, column],
            out_specs=spec((size, half), lambda i, n: (i, 0)),
        ),
        out_shape=struct((slots, half), BF16),
        cost_estimate=pl.CostEstimate(
            flops=4 * slots * rows * half, bytes_accessed=4 * slots * half, transcendentals=0
        ),
        compiler_params=pltpu.CompilerParams(vmem_limit_bytes=14 << 20),
        name="dispatch",
    )(node, place, own, other)


def combine_kernel(place_ref, got_ref, out_ref):
    size = place_ref.shape[0]
    slot = lax.broadcasted_iota(jnp.int32, (size, got_ref.shape[0]), 1)
    onehot = (place_ref[...] == slot).astype(F32).astype(BF16)
    out_ref[...] = dot(onehot, got_ref[...]).astype(BF16)


def combine_rows(place, got):
    rows = place.shape[0]
    size = 256
    return pl.pallas_call(
        combine_kernel,
        grid=(rows // size,),
        in_specs=[spec((size, 1), lambda i: (i, 0)), fixed(got.shape)],
        out_specs=spec((size, got.shape[1]), lambda i: (i, 0)),
        out_shape=struct((rows, got.shape[1]), BF16),
        cost_estimate=pl.CostEstimate(
            flops=2 * rows * got.shape[0] * got.shape[1],
            bytes_accessed=4 * rows * got.shape[1],
            transcendentals=0,
        ),
        compiler_params=pltpu.CompilerParams(vmem_limit_bytes=12 << 20),
        name="combine",
    )(place, got)


def combine_out_kernel(node_ref, place_ref, got_ref, dense_ref, share_ref, out_ref, sum_ref):
    size = place_ref.shape[0]
    half = got_ref.shape[1]
    node = node_ref[0]
    slot = lax.broadcasted_iota(jnp.int32, (size, got_ref.shape[0]), 1)
    onehot = (place_ref[...] == slot).astype(F32).astype(BF16)
    sum_ref[...] = dense_ref[...].astype(F32)
    sum_ref[:, pl.ds(pl.multiple_of(node * half, half), half)] += share_ref[:, 0:1] * dot(
        onehot, got_ref[...]
    )
    out_ref[...] = sum_ref[...].astype(BF16)


def combine_out(node, place, got, dense, share):
    rows, width = dense.shape
    size = 256
    steps = rows // size

    def chunk(i, n):
        mine = i // (steps // 2) == 0
        return (jnp.where(mine, n[0], 1 - n[0]) * (steps // 2) + i % (steps // 2), 0)

    return pl.pallas_call(
        combine_out_kernel,
        grid_spec=pltpu.PrefetchScalarGridSpec(
            num_scalar_prefetch=1,
            grid=(steps,),
            in_specs=[
                spec((size, 1), chunk),
                fixed(got.shape),
                spec((size, width), chunk),
                spec((size, LANES), chunk),
            ],
            out_specs=spec((size, width), lambda i, n: (i, 0)),
            scratch_shapes=[pltpu.VMEM((size, width), F32)],
        ),
        out_shape=struct((rows, width), BF16),
        cost_estimate=pl.CostEstimate(
            flops=2 * rows * got.shape[0] * got.shape[1],
            bytes_accessed=4 * rows * width,
            transcendentals=0,
        ),
        compiler_params=pltpu.CompilerParams(vmem_limit_bytes=LIMIT),
        name="combine_out",
    )(node, place, got, dense, share)


def branch_kernel(dense, experts, parts, layout, node_ref, *refs):
    if dense:
        x_refs, c_refs, route_ref, refs = refs[:1], refs[1:3], refs[3], refs[4:]
    else:
        x_refs, c_refs, refs = refs[:2], refs[2:4], refs[4:]
    side_ref, wct_ref, up_ref, dn_ref = refs[:4]
    refs = refs[4:]
    if dense:
        out_refs, dx_refs, gsm_ref, probs_ref = refs[:1], refs[1:2], refs[2], refs[3]
        grad_refs = refs[4 : 4 + parts]
        xt_ref, g_ref, a_ref, acc_ref, dxa_ref, act_ref, dpre_ref, gt_ref = refs[4 + parts :]
    else:
        out_refs, dx_refs, gsm_ref = refs[:2], refs[2:4], refs[4]
        g_ref, act_ref, dpre_ref, a_ref, acc_ref, dxa_ref = refs[5:]
    halves = len(x_refs)
    rows, half = x_refs[0].shape
    width = halves * half
    step = pl.program_id(0)
    small = 256
    big = 512
    unit = width // layout.members
    node = node_ref[0]
    if dense:
        order = functools.partial(layout.place, node, node_ref[1])
        split = [slice(0, width)]
    else:
        split = [
            pl.ds(pl.multiple_of(node * half, half), half),
            pl.ds(pl.multiple_of((1 - node) * half, half), half),
        ]

    @pl.when(step == 0)
    def _():
        lane = lax.broadcasted_iota(jnp.int32, (1, LANES), 1)
        is_router = lane < experts
        is_mix = (lane >= experts) & (lane < experts + 2)
        first = (lane == experts).astype(F32)
        second = (lane == experts + 1).astype(F32)
        picked = side_ref[...]

        def prepare(at):
            logits = sum(dot_t(x_refs[n][at, :], wct_ref[:, split[n]]) for n in range(halves))

            def soft(mask):
                masked = jnp.where(mask, logits, -1e30)
                shifted = jnp.exp(masked - jnp.max(masked, axis=1, keepdims=True))
                return shifted / jnp.sum(shifted, axis=1, keepdims=True)

            mix = soft(is_mix)
            if dense:
                factor = jnp.sum(mix * first, axis=1, keepdims=True)
                chosen = lane == route_ref[at, :]
                gate = jnp.sum(jnp.where(chosen, soft(is_router), 0.0), axis=1, keepdims=True)
                share = gate * jnp.sum(mix * second, axis=1, keepdims=True)
                probs_ref[at, :] = jnp.where(lane == 0, share, factor)
                a_ref[at, :] = jnp.where(is_mix, first - mix, 0.0)
            else:
                router = soft(is_router)
                gate = jnp.sum(router * picked, axis=1, keepdims=True)
                factor = gate * jnp.sum(mix * second, axis=1, keepdims=True)
                a_ref[at, :] = jnp.where(
                    is_router, picked - router, jnp.where(is_mix, second - mix, 0.0)
                )
            if dense:
                own = c_refs[0].shape[0]
                place = at.start // own
                inside = pl.ds(pl.multiple_of(at.start - place * own, small), small)
                cot = row_pick(node, place, c_refs[0][inside, :], c_refs[1][inside, :])
                scaled = (factor * cot.astype(F32)).astype(BF16)
                g_ref[at, :] = scaled
            else:
                for n in range(halves):
                    g_ref[at, split[n]] = (factor * c_refs[n][at, :].astype(F32)).astype(BF16)
            acc_ref[at, :] = jnp.zeros((small, width), F32)
            dxa_ref[at, :] = jnp.zeros((small, width), F32)

        chunks(rows, small, prepare)
        if dense:

            def transpose(at):
                turn = permutation(order, at.start, small, unit, width)
                for index in range(rows // big):
                    some = slice(index * big, (index + 1) * big)
                    xt_ref[at, some] = dot_t(turn, x_refs[0][some, :]).astype(BF16)
                    gt_ref[at, some] = dot_t(turn, g_ref[some, :]).astype(BF16)

            chunks(width, small, transpose)

    def forward(at):
        pre = sum(dot(x_refs[n][at, :], up_ref[split[n], :]) for n in range(halves))
        square = pre * pre
        bend = jnp.tanh(pre * (GELU_A + GELU_A * GELU_B * square))
        side = 0.5 * (1.0 + bend)
        act = (pre * side).astype(BF16)
        slope = side + 0.5 * pre * (1.0 - bend * bend) * (GELU_A + 3.0 * GELU_A * GELU_B * square)
        act_ref[at, :] = act
        if dense:
            act_grad = dot(g_ref[at, :], dn_ref[...])
            acc_ref[at, :] += dot_t(act, dn_ref[...])
        else:
            act_grad = dot_t(g_ref[at, :], dn_ref[...])
            acc_ref[at, :] += dot(act, dn_ref[...])
        pre_grad = (slope * act_grad).astype(BF16)
        dpre_ref[at, :] = pre_grad
        dxa_ref[at, :] += dot_t(pre_grad, up_ref[...])

    chunks(rows, big, forward)
    if dense:
        size = width // parts
        for part in range(parts):

            def weights(at):
                rows_at = pl.ds(pl.multiple_of(part * size + at.start, small), small)
                pair = (
                    dot(xt_ref[rows_at, :], dpre_ref[...]).astype(BF16),
                    dot(gt_ref[rows_at, :], act_ref[...]).astype(BF16),
                )
                for index in range(2 * small // unit):
                    to = pl.multiple_of(2 * at.start + index * unit, unit)
                    place = index // 2 * unit
                    grad_refs[part][pl.ds(to, unit), :] = pair[index % 2][place : place + unit]

            chunks(size, small, weights)

    @pl.when(step == pl.num_programs(0) - 1)
    def _():
        gsm_ref[...] = jnp.zeros_like(gsm_ref)

        def finish(at):
            out = acc_ref[at, :]
            strength = jnp.sum(g_ref[at, :].astype(F32) * out, axis=1, keepdims=True)
            logit_grad = strength * a_ref[at, :]
            low = logit_grad.astype(BF16)
            turned = logit_grad.T.astype(BF16)
            for n in range(halves):
                gsm_ref[:, split[n]] += dot(turned, x_refs[n][at, :])
                part = acc_ref[at, split[n]]
                if dense:
                    part = part * probs_ref[at, 1:2]
                out_refs[n][at, :] = part.astype(BF16)
                dx_refs[n][at, :] = (dxa_ref[at, split[n]] + dot(low, wct_ref[:, split[n]])).astype(
                    BF16
                )

        chunks(rows, small, finish)


def branch(node, layout, xs, cs, side, head_t, up, down, experts, parts):
    dense = len(xs) == 1
    rows, half = xs[0].shape
    width = len(xs) * half
    hidden = up.shape[1]
    block = 512
    column = lambda size: spec((size, block), lambda f, n: (0, f))
    up_spec = column(width)
    down_spec = up_spec if dense else spec((block, width), lambda f, n: (f, 0))
    outs = [(fixed((rows, half)), struct((rows, half), BF16))] * (2 * len(xs))
    outs = outs + [(fixed((LANES, width)), struct((LANES, width), F32))]
    sums = [
        pltpu.VMEM((rows, LANES), F32),
        pltpu.VMEM((rows, width), F32),
        pltpu.VMEM((rows, width), F32),
    ]
    if dense:
        outs = outs + [(fixed((rows, LANES)), struct((rows, LANES), F32))]
        size = 2 * width // parts
        outs = outs + [(column(size), struct((size, hidden), BF16))] * parts
        scratch = [
            pltpu.VMEM((width, rows), BF16),
            pltpu.VMEM((rows, width), BF16),
            *sums,
            pltpu.VMEM((rows, block), BF16),
            pltpu.VMEM((rows, block), BF16),
            pltpu.VMEM((width, rows), BF16),
        ]
    else:
        outs = outs + [(fixed((rows, width)), struct((rows, width), BF16))]
        outs = outs + [(column(rows), struct((rows, hidden), BF16))] * 2
        scratch = sums
    return pl.pallas_call(
        functools.partial(branch_kernel, dense, experts, parts, layout),
        grid_spec=pltpu.PrefetchScalarGridSpec(
            num_scalar_prefetch=1,
            grid=(hidden // block,),
            in_specs=[fixed(one.shape) for one in [*xs, *cs]]
            + [
                fixed(side.shape),
                fixed((LANES, width)),
                up_spec,
                down_spec,
            ],
            out_specs=[one for one, _ in outs],
            scratch_shapes=scratch,
        ),
        out_shape=[shape for _, shape in outs],
        cost_estimate=pl.CostEstimate(
            flops=(12 if dense else 8) * rows * width * hidden,
            bytes_accessed=12 * width * hidden + 8 * rows * width,
            transcendentals=rows * hidden,
        ),
        compiler_params=pltpu.CompilerParams(vmem_limit_bytes=LIMIT),
        name="dense_branch" if dense else "expert_branch",
    )(node, *xs, *cs, side, head_t, up, down)


def expert_up_kernel(node_ref, own_ref, other_ref, dpre_ref, grad_ref, xt_ref):
    rows, half = own_ref.shape
    node = node_ref[0]

    @pl.when(pl.program_id(0) == 0)
    def _():
        for at, ref in ((node, own_ref), (1 - node, other_ref)):
            place = pl.ds(pl.multiple_of(at * half, half), half)

            def turn(rows_at):
                xt_ref[place, rows_at] = ref[rows_at, :].T

            chunks(rows, 256, turn)

    def weights(at):
        grad_ref[at, :] = dot(xt_ref[at, :], dpre_ref[...])

    chunks(2 * half, 256, weights)


def expert_down_kernel(act_ref, g_ref, grad_ref):
    grad_ref[...] = dot_n(act_ref[...], g_ref[...])


def expert_up_grad(node, own, other, dpre):
    rows, half = own.shape
    hidden = dpre.shape[1]
    block = 512
    return pl.pallas_call(
        expert_up_kernel,
        grid_spec=pltpu.PrefetchScalarGridSpec(
            num_scalar_prefetch=1,
            grid=(hidden // block,),
            in_specs=[
                fixed(own.shape),
                fixed(own.shape),
                spec((rows, block), lambda f, n: (0, f)),
            ],
            out_specs=spec((2 * half, block), lambda f, n: (0, f)),
            scratch_shapes=[pltpu.VMEM((2 * half, rows), BF16)],
        ),
        out_shape=struct((2 * half, hidden), F32),
        cost_estimate=pl.CostEstimate(
            flops=4 * rows * half * hidden,
            bytes_accessed=8 * half * hidden + 2 * rows * hidden,
            transcendentals=0,
        ),
        compiler_params=pltpu.CompilerParams(vmem_limit_bytes=LIMIT),
        name="expert_up_grad",
    )(node, own, other, dpre)


def expert_down_grad(act, g):
    rows, hidden = act.shape
    width = g.shape[1]
    block = 256
    return pl.pallas_call(
        expert_down_kernel,
        grid=(hidden // block,),
        in_specs=[spec((rows, block), lambda f: (0, f)), fixed(g.shape)],
        out_specs=spec((block, width), lambda f: (f, 0)),
        out_shape=struct((hidden, width), F32),
        cost_estimate=pl.CostEstimate(
            flops=2 * rows * width * hidden,
            bytes_accessed=4 * width * hidden + 2 * rows * hidden,
            transcendentals=0,
        ),
        compiler_params=pltpu.CompilerParams(vmem_limit_bytes=28 << 20),
        name="expert_down_grad",
    )(act, g)


def turn_kernel(grid, node_ref, x_ref, out_ref):
    rows, width = out_ref.shape[0], x_ref.shape[1]
    order = functools.partial(grid.place, node_ref[0], node_ref[1])
    start = pl.program_id(0) * rows
    rows_of = permutation(order, start, rows, width // (2 * grid.members), width, 2)
    out_ref[...] = dot_t(rows_of, x_ref[...]).astype(BF16)


def turn(node, grid, x):
    seq, width = x.shape
    rows = 256
    return pl.pallas_call(
        functools.partial(turn_kernel, grid),
        grid_spec=pltpu.PrefetchScalarGridSpec(
            num_scalar_prefetch=1,
            grid=(width // rows,),
            in_specs=[fixed(x.shape)],
            out_specs=spec((rows, seq), lambda i, n: (i, 0)),
        ),
        out_shape=struct((width, seq), BF16),
        cost_estimate=pl.CostEstimate(
            flops=2 * seq * width * width, bytes_accessed=4 * seq * width, transcendentals=0
        ),
        compiler_params=pltpu.CompilerParams(vmem_limit_bytes=16 << 20),
        name="turn",
    )(node, x)


def tail_kernel(
    parts,
    ln_lane,
    grid,
    node_ref,
    x_ref,
    xt_ref,
    gain_ref,
    small_ref,
    packed_ref,
    w_ref,
    keep_ref,
    send_ref,
    *refs,
):
    part_refs = refs[:parts]
    acc_ref = refs[parts]
    seq, width = x_ref.shape
    size = width // parts
    own = keep_ref.shape[0]
    order = functools.partial(grid.place, node_ref[0], node_ref[1])
    block = width // (2 * grid.members)
    step = pl.program_id(0)
    last = pl.num_programs(0) - 1

    @pl.when(step < last)
    def _():
        for part in range(parts):

            def weights(at):
                rows_at = pl.ds(pl.multiple_of(part * size + at.start, 256), 256)
                part_refs[part][at, :] = dot(xt_ref[rows_at, :], packed_ref[0]).astype(BF16)

            chunks(size, 256, weights)

        @pl.when(step == 0)
        def _():
            acc_ref[...] = jnp.zeros_like(acc_ref)

        def back(at):
            acc_ref[at, :] += dot_t(packed_ref[0, at, :], w_ref[...])

        chunks(seq, 256, back)

    @pl.when(step == last)
    def _():
        gain = gain_ref[...]
        node = node_ref[0]

        def column_sum(index, total):
            rows = pl.ds(pl.multiple_of(index * 256, 256), 256)
            return total + jnp.sum(
                acc_ref[rows, :] * x_ref[rows, :].astype(F32), axis=0, keepdims=True
            )

        total = lax.fori_loop(0, seq // 256, column_sum, jnp.zeros((1, width), F32)) / gain
        row = lax.broadcasted_iota(jnp.int32, (LANES, 1), 0)
        small = (small_ref[...] + jnp.where(row == ln_lane, total, 0.0)).astype(BF16)
        for part in range(parts):

            def turn(at):
                rows = permutation(order, part * size + at.start, 256, block, width, 2)
                part_refs[part][at, 0:LANES] = dot_t(rows, small).astype(BF16)

            chunks(size, 256, turn)
        keep_ref[...] = acc_ref[pl.ds(pl.multiple_of(node * own, own), own), :]
        send_ref[...] = acc_ref[pl.ds(pl.multiple_of((1 - node) * own, own), own), :].astype(BF16)


def tail(node, grid, normed, turned, gain, small, packed, w_qkv, parts, ln_lane):
    seq, width = normed.shape
    half = width // 2
    steps = 3
    part = (width // parts, half)
    return pl.pallas_call(
        functools.partial(tail_kernel, parts, ln_lane, grid),
        grid_spec=pltpu.PrefetchScalarGridSpec(
            num_scalar_prefetch=1,
            grid=(steps + 1,),
            in_specs=[
                fixed(normed.shape),
                fixed(turned.shape),
                fixed((1, width)),
                fixed((LANES, width)),
                spec((1, seq, half), lambda i, n: (jnp.minimum(i, steps - 1), 0, 0)),
                spec((width, half), lambda i, n: (0, 2 * jnp.minimum(i, steps - 1) + n[0])),
            ],
            out_specs=[fixed((seq // 2, width)), fixed((seq // 2, width))]
            + [spec(part, lambda i, n: (0, i))] * parts,
            scratch_shapes=[pltpu.VMEM((seq, width), F32)],
        ),
        out_shape=[struct((seq // 2, width), F32), struct((seq // 2, width), BF16)]
        + [far((width // parts, steps * half + LANES), BF16)] * parts,
        cost_estimate=pl.CostEstimate(
            flops=6 * seq * width * width, bytes_accessed=16 * seq * width, transcendentals=0
        ),
        compiler_params=pltpu.CompilerParams(vmem_limit_bytes=32 << 20),
        name="tail",
    )(node, normed, turned, gain[None], small, packed, w_qkv)


class Grid:

    def __init__(self, members):
        self.third = 4 if members % 4 == 0 else 1
        self.first = round((members // self.third) ** 0.5)
        assert self.third * self.first * self.first == members
        self.members = members
        self.sizes = (self.first, self.first, self.third)

    def digits(self, node, member):
        low, high = member % self.first, (member // self.first) % self.first
        top = member // (self.first * self.first)
        return (low, high, top) if node == 0 else (high, low, top)

    def index(self, node, digits):
        low, high = (digits[0], digits[1]) if node == 0 else (digits[1], digits[0])
        return (digits[2] * self.first + high) * self.first + low

    def shift(self, stage, by):
        pairs = []
        for node in range(2):
            for member in range(self.members):
                digits = list(self.digits(node, member))
                digits[stage] = (digits[stage] + by) % self.sizes[stage]
                target = self.index(node, digits)
                pairs.append((node * self.members + member, node * self.members + target))
        return pairs

    def place(self, node, member, place):
        size, third = self.first, self.third
        low, high = member % size, (member // size) % size
        top = member // (size * size)
        one = (jnp.where(node == 0, low, high) + place // (size * third)) % size
        two = (jnp.where(node == 0, high, low) + (place // third) % size) % size
        low, high = jnp.where(node == 0, one, two), jnp.where(node == 0, two, one)
        return ((top + place % third) % third * size + high) * size + low

    def send(self, parts, stage):
        return [
            lax.ppermute(parts[by], ("node", "expert"), self.shift(stage, by))
            for by in range(1, self.sizes[stage])
        ]

    def add(self, parts, came, stage, *gates):
        if gates:
            came = [after(other, *gates) for other in came]
        pieces = self.sizes[stage + 1] if stage < 2 else 1
        rows = parts[0].shape[0] // pieces
        sums = []
        for piece in range(pieces):
            at = slice(piece * rows, (piece + 1) * rows)
            total = parts[0][at].astype(F32)
            for other in came:
                total = total + other[at].astype(F32)
            sums.append(total.astype(BF16) if stage < 2 else total)
        return sums


def shards(
    tokens,
    cotangent,
    routes,
    ln1_gain,
    w_qkv,
    w_out,
    ln2_gain,
    w_router,
    w_mix,
    w_up,
    w_down,
    expert_up,
    expert_down,
):
    node = lax.axis_index("node")
    member = lax.axis_index("expert")
    members = lax.axis_size("expert")
    width = tokens.shape[2]
    half = width // 2
    own_rows = tokens.shape[1]
    seq = 2 * own_rows
    experts = w_router.shape[1]
    capacity = 3 * seq // (2 * experts)
    slots = experts * capacity
    pairs = half // LANES
    own_start = node * own_rows
    scalar = jnp.stack([node, member]).astype(jnp.int32)
    grid = Grid(members)
    parts = grid.sizes[0]

    def swap(value):
        return lax.ppermute(value, "node", SWAP)

    def in_order(mine, other, axis):
        return jnp.where(
            node == 0,
            jnp.concatenate([mine, other], axis=axis),
            jnp.concatenate([other, mine], axis=axis),
        )

    own_tokens, own_cot = tokens[0], cotangent[0]
    other_tokens, other_cot = swap(own_tokens), swap(own_cot)

    group_routes = routes.reshape(-1)
    route_onehot = group_routes[:, None] == jnp.arange(experts)[None, :]
    ones = route_onehot.astype(BF16)
    row_at = jnp.arange(seq)
    earlier = (row_at[:, None] > row_at[None, :]).astype(BF16)
    order = jnp.sum(jnp.where(route_onehot, dot(earlier, ones), 0.0), axis=1).astype(jnp.int32)
    place = jnp.where(order < capacity, group_routes * capacity + order, slots)
    place_rows = place.reshape(2, own_rows)
    place_column = place.reshape(seq, 1)

    def exchange(value):
        value = value.reshape(experts, capacity, half)
        got = lax.all_to_all(value, "expert", split_axis=0, concat_axis=0, tiled=True)
        return got.reshape(slots, half)

    def give_back(mine, other):
        total = (mine.astype(F32) + swap(other).astype(F32)).astype(BF16)
        return total, exchange(total)

    got_cot = exchange(dispatch_rows(scalar, place_rows, own_cot, other_cot, slots))

    route_column = group_routes[:, None]
    head_t = jnp.concatenate(
        [w_router, w_mix, jnp.zeros((width, LANES - experts - 2), BF16)], axis=1
    ).T
    first_gain = after(ln1_gain, route_column, head_t)
    qkv, normed_low = front(scalar, own_tokens, other_tokens, first_gain, w_qkv)
    attended_own, lse = attend(qkv, pairs)
    hidden, inner_low, sent_rows = middle(
        scalar, own_tokens, other_tokens, attended_own, swap(attended_own), w_out, ln2_gain,
        place.reshape(1, seq), slots,
    )

    got_rows = exchange(sent_rows)
    picked = (jnp.arange(LANES) == member).astype(F32)[None]
    results = branch(
        scalar, grid, [inner_low], [own_cot, other_cot, route_column], picked, head_t, w_up, w_down,
        experts, parts,
    )
    dense_out, dense_dx, small_dense, share = results[:4]
    pair0 = results[4:]
    came = grid.send(pair0, 0)
    got_rows = after(got_rows, small_dense)
    expert_rows = [got_rows, swap(got_rows)]
    out_keep, out_send, dx_keep, dx_send, small_expert, expert_g, expert_act, expert_dpre = branch(
        scalar, grid, expert_rows, [got_cot, swap(got_cot)], picked, head_t, expert_up[0],
        expert_down[0], experts, parts,
    )

    sent_dx, got_dx = give_back(dx_keep, dx_send)
    pair1 = grid.add(pair0, came, 0, sent_dx)
    came = grid.send(pair1, 1)
    grad_expert_down = expert_down_grad(expert_act, after(expert_g, sent_dx))
    _, got_out = give_back(out_keep, after(out_send, grad_expert_down))
    turned_low = turn(scalar, grid, after(normed_low, grad_expert_down))
    token_dx = combine_rows(place_column, after(got_dx, pair1, turned_low))
    results = middle_back(
        scalar, grid, dense_dx, swap(dense_dx), token_dx, swap(token_dx), hidden, own_cot,
        other_cot, attended_own, ln2_gain, w_out, parts,
    )
    hidden_grad, attended_grad, ln2_row = results[:3]
    out0 = results[3:]
    out_came = grid.send(out0, 0)
    pair2 = grid.add(pair1, came, 1, ln2_row)
    came = grid.send(pair2, 2)
    packed = attend_back(qkv, attended_own, attended_grad, lse)

    small = small_dense + small_expert
    small = small + jnp.where(jnp.arange(LANES)[:, None] == experts + 3, ln2_row[0:1], 0.0)
    results = tail(
        scalar, grid, normed_low, turned_low, ln1_gain, small, packed, w_qkv, parts, experts + 2
    )
    grad_keep, grad_send, last0 = results[0], results[1], results[2:]
    last_came = grid.send(last0, 0)
    out1 = grid.add(out0, out_came, 0, grad_keep)
    out_came = grid.send(out1, 1)
    grad_expert_up = expert_up_grad(scalar, *expert_rows, after(expert_dpre, grad_keep))
    out2 = grid.add(out1, out_came, 1, grad_expert_up)
    out_came = grid.send(out2, 2)
    last1 = grid.add(last0, last_came, 0, grad_expert_up, *out2)
    last_came = grid.send(last1, 1)

    total_out = combine_out(scalar, place_column, after(got_out, last1), dense_out, share)
    out_mine, out_other = total_out[:own_rows], swap(total_out[own_rows:])


    last2 = grid.add(last1, last_came, 1, total_out)
    last_came = grid.send(last2, 2)

    unit = width // members
    both = grid.add(pair2, came, 2, last2)[0]
    grad_w_up, grad_w_down = both[:unit], both[unit:]
    hidden_own = lax.dynamic_slice_in_dim(hidden, own_start, own_rows, 0)
    out_other = after(out_other, last2)
    mixed_out = (hidden_own + out_mine.astype(F32) + out_other.astype(F32)).astype(BF16)
    grad_w_out = grid.add(out2, out_came, 2, last2)[0]
    normed_grad = grad_keep + after(swap(grad_send), last2).astype(F32)
    _, base_one, inverse_one = layer_norm(own_tokens.astype(F32), ln1_gain)
    input_grad = hidden_grad + norm_backward(
        normed_grad, base_one, inverse_one, ln1_gain
    )
    block = width // (2 * members)
    last = grid.add(last2, last_came, 2, input_grad, grad_w_out, mixed_out, both)[0].reshape(2, block, -1)
    kept = lax.dynamic_index_in_dim(last, node, 0, False)
    other = swap(lax.dynamic_index_in_dim(last, 1 - node, 0, False).astype(BF16)).astype(F32)

    def columns(rows):
        return rows[:, : 3 * half].reshape(block, 3, half)

    grad_w_qkv = in_order(columns(kept), columns(other), 2).reshape(block, 3 * width)
    small = kept[:, 3 * half :] + other[:, 3 * half :]
    return (
        mixed_out.reshape(tokens.shape),
        input_grad.reshape(tokens.shape),
        small[:, experts + 2],
        grad_w_qkv,
        grad_w_out,
        small[:, experts + 3],
        small[:, :experts],
        small[:, experts : experts + 2],
        grad_w_up,
        grad_w_down,
        grad_expert_up[None],
        grad_expert_down[None],
    )


def solution(mesh):
    return jax.shard_map(
        shards,
        mesh=mesh,
        in_specs=(
            P("expert", "node", None),
            P("expert", "node", None),
            P("expert", None, None),
            P(),
            P(),
            P(),
            P(),
            P(),
            P(),
            P(None, "node"),
            P(None, "node"),
            P("expert", None, "node"),
            P("expert", "node", None),
        ),
        out_specs=(
            P("expert", "node", None),
            P("expert", "node", None),
            P(("node", "expert")),
            P(("node", "expert"), None),
            P(("node", "expert"), None),
            P(("node", "expert")),
            P(("node", "expert"), None),
            P(("node", "expert"), None),
            P("expert", "node"),
            P("expert", "node"),
            P("expert", None, "node"),
            P("expert", "node", None),
        ),
        check_vma=False,
    )
```
